128 devices in a mesh: gx: 8 (over z, x_lo), gy: 16 (over x_hi, y, core).
Axes of the slice: x: 4 (x_hi: 2, x_lo: 2; x = x_hi * 2 + x_lo), y: 4, z: 4, core: 2. Of those that a mesh axis runs over, the one named last changes fastest.
Arguments:
- fields: float32 [6, 256, 512, 128], P(None, 'gx', 'gy'), may hold values from -6 to 6
- eps_background: float32 [256, 512, 128], P('gx', 'gy'), may hold values from 1 to 4
- target: float32 [256, 256], replicated, may hold values from 1 to 10
- widths: float32 [16384], P(('gx', 'gy')), may hold values from 0.2 to 1
- intersection: float32 [16384, 16], P(('gx', 'gy')), may hold values from 0.1 to 1
- pillar_tile: int32 [16384, 1], P(('gx', 'gy')), may hold values from 0 to 127; in each aligned block of 128 rows (0 to 127, 128 to 255, ...) at most 2 rows name the same one
- anchors: int32 [16384, 2], P(('gx', 'gy')), may hold values from 0 to 28
Outputs:
- final_fields: float32 [6, 256, 512, 128], P(None, 'gx', 'gy')
- focal_power: float32 [256, 256], P(('gx', 'gy'))
- grad_widths: float32 [16384], P(('gx', 'gy'))
The draws below stay inside these ranges and needn't reach their ends.
Inputs may be any that keep to these rules, and one draw needn't show every extreme that they name: `pillar_tile`: in the pillars of one device (aligned blocks of 128), no tile is named by more than 2 pillars, a bound that some block reaches. Tile t is the one at gx index t div (512 div 32) and gy index t mod (512 div 32).
All inputs are finite; a program needn't handle non-finite values.
Results may differ from the reference program's by a relative error of at most 0.00016.
Values sent between devices are 32-bit elements; how exact they have to be, the bound alone decides.
A program may use at most 128 MiB of HBM per device.

```python
import math
import jax
import jax.numpy as jnp
import numpy as np
from jax import lax

TILE = 32
NZ = 128
P_DEV = 128
NT = 4
ZP = 4
U = 256
V = 256
NX = 256
NY = 512
ZM = 64
PILLARS = 16384
CAP = 2
DEVICES = 128


def with_ends(drawn, key, low, largest):
    extent = drawn.shape
    spot = [jax.random.randint(jax.random.fold_in(key, axis), (), 0, extent[axis]) for axis in range(len(extent))]
    drawn = drawn.at[tuple(spot)].set(low)
    longest = extent.index(max(extent))
    spot[longest] = (spot[longest] + 1) % extent[longest]
    return drawn.at[tuple(spot)].set(largest)


def block_levels(key, shape, pieces, least, high):
    level = 1.0
    for axis_at, shards_of in pieces:
        steps = jax.random.uniform(jax.random.fold_in(jax.random.fold_in(key, 6), axis_at), (shards_of,), jnp.float32, least / len(pieces), high / len(pieces))
        level = level * jnp.repeat(jnp.exp(steps), shape[axis_at] // shards_of).reshape((-1,) + (1,) * (len(shape) - 1 - axis_at))
    return level


def routed_block(stream_key, own, number, rows, count, top, most, lean):
    order = jax.random.permutation(stream_key, count)
    packed, usual = portions_of(count, rows * top, most, lean, True), portions_of(count, rows * top, most, lean, False)
    places = jnp.arange(count)

    def named(sizes, offset_by):
        used = int((sizes > 0).sum())
        fixed = max(1, used // 4)
        shifted = fixed + (places - fixed + offset_by * (used - fixed)) % max(1, count - fixed)
        return jnp.zeros((count,), jnp.int32).at[order[jnp.where(places < fixed, places, shifted)]].set(jnp.asarray(sizes, jnp.int32))

    sizes = jnp.where(number % 4 == 0, named(packed, number // 4), named(usual, number - number // 4 - 1))
    mixed = jax.random.permutation(jax.random.fold_in(own, 3), count)
    giver, sink = mixed[0:count // 2 * 2:2], mixed[1:count // 2 * 2:2]
    slack = jnp.minimum(sizes[giver] - 1, most - sizes[sink]) // 2
    slack = jnp.where((giver == order[0]) | (sink == order[0]) | (sizes[sink] == 0), 0, jnp.maximum(slack, 0))
    shifted = jax.random.randint(jax.random.fold_in(own, 4), (count // 2,), 0, 1 << 20) % (slack + 1)
    sizes = sizes.at[giver].add(-shifted).at[sink].add(shifted)
    labels = jnp.searchsorted(jnp.cumsum(sizes), jnp.arange(rows * top), side="right").astype(jnp.int32)
    listing = labels.reshape(top, rows).T
    listing = listing[jax.random.permutation(jax.random.fold_in(own, 1), rows)]
    offset_by = jax.random.randint(jax.random.fold_in(own, 2), (rows, 1), 0, top)
    return jnp.take_along_axis(listing, (jnp.arange(top)[None, :] + offset_by) % top, axis=1)


def portions_of(number_of, total, bound, lean, full):
    portions = [(1 << 20) // math.isqrt(standing ** lean) + 1 for standing in range(1, number_of + 1)]
    largest = bound if full else min(bound, max(-(-total // number_of), total * portions[0] // sum(portions)))
    least = 1 if total - largest >= number_of - 1 else 0
    given, spare = [largest] + [least] * (number_of - 1), total - largest - least * (number_of - 1)
    while spare > 0:
        movable = [i for i in range(1, number_of) if given[i] < largest] or [i for i in range(1, number_of) if given[i] < bound]
        pool, left = sum([portions[i] for i in movable]), spare
        for i in movable:
            extra = min(bound - given[i], max(1, left * portions[i] // pool), spare)
            given[i] = given[i] + extra
            spare = spare - extra
    return np.array(given)


def bell_draw(own_key, dims, spread, reach, cuts=(), held_as=jnp.bfloat16):
    values = jax.random.normal(own_key, dims, jnp.float32) * spread
    if len(cuts) > 0:
        values = block_levels(own_key, dims, cuts, -0.22, 0.18) * values
    return jnp.clip(values, min=-reach, max=reach).astype(held_as)


def setup_inputs(seed: int = 0) -> dict:
    key_of = jax.random.split(jax.random.key(seed), 8)
    fields = bell_draw(key_of[0], (6, NX, NY, NZ), 1.0, 6.0, ((1, 8), (2, 16)), jnp.float32)
    eps_background = jnp.clip(1.0 + 3.0 * jax.random.uniform(key_of[1], (NX, NY, NZ), jnp.float32) ** block_levels(key_of[1], (NX, NY, NZ), ((0, 8), (1, 16)), -0.2, 0.2), 1.0, 4.0)
    target = jnp.clip(jnp.exp(jax.random.uniform(key_of[2], (U, V), jnp.float32, math.log(1.0), math.log(10.0))), 1.0, 10.0)
    widths = jnp.clip(0.2 + 0.8 * jax.random.uniform(key_of[3], (PILLARS,), jnp.float32) ** block_levels(key_of[3], (PILLARS,), ((0, 128),), -0.2, 0.2), 0.2, 1.0)
    intersection = jnp.clip(0.1 + 0.9 * jax.random.uniform(key_of[4], (PILLARS, 16), jnp.float32) ** block_levels(key_of[4], (PILLARS, 16), ((0, 128),), -0.2, 0.2), 0.1, 1.0)
    pillar_tile_keys = jax.random.split(jax.random.fold_in(key_of[5], 1), PILLARS // P_DEV)
    pillar_tile_turns = jax.random.permutation(jax.random.fold_in(key_of[5], 3), PILLARS // P_DEV)
    pillar_tile = jax.vmap(lambda own, number: routed_block(jax.random.fold_in(key_of[5], 2), own, number, P_DEV, DEVICES, 1, CAP, 2))(pillar_tile_keys, pillar_tile_turns).reshape((PILLARS, 1))
    anchors = with_ends(jax.random.randint(key_of[6], (PILLARS, 2), 0, TILE - 3), jax.random.fold_in(key_of[6], 1), 0, (TILE - 3) - 1).astype(jnp.int32)
    return dict(fields=fields, eps_background=eps_background, target=target, widths=widths, intersection=intersection, pillar_tile=pillar_tile, anchors=anchors)


COURANT = 0.5
ANGULAR_STEP = 0.9
DELTA_EPS = 4.0


def plus_diff(field, axis):
    length = field.shape[axis]
    ahead = jnp.concatenate([lax.slice_in_dim(field, 1, length, axis=axis), jnp.zeros_like(lax.slice_in_dim(field, 0, 1, axis=axis))], axis=axis)
    return ahead - field


def minus_diff(field, axis):
    length = field.shape[axis]
    behind = jnp.concatenate([jnp.zeros_like(lax.slice_in_dim(field, 0, 1, axis=axis)), lax.slice_in_dim(field, 0, length - 1, axis=axis)], axis=axis)
    return field - behind


def leap_step(fields_now, inv_eps, sources):
    elec_x, elec_y, elec_z, magn_x, magn_y, magn_z = fields_now
    curl_x = plus_diff(elec_z, 1) - plus_diff(elec_y, 2)
    curl_y = plus_diff(elec_x, 2) - plus_diff(elec_z, 0)
    curl_z = plus_diff(elec_y, 0) - plus_diff(elec_x, 1)
    magn_x = magn_x - COURANT * curl_x
    magn_y = magn_y - COURANT * curl_y
    magn_z = magn_z - COURANT * curl_z
    curl_x = minus_diff(magn_z, 1) - minus_diff(magn_y, 2)
    curl_y = minus_diff(magn_x, 2) - minus_diff(magn_z, 0)
    curl_z = minus_diff(magn_y, 0) - minus_diff(magn_x, 1)
    elec_x = elec_x + COURANT * (curl_x - sources[0]) * inv_eps
    elec_y = elec_y + COURANT * (curl_y - sources[1]) * inv_eps
    elec_z = elec_z + COURANT * (curl_z - sources[2]) * inv_eps
    return (elec_x, elec_y, elec_z, magn_x, magn_y, magn_z)


def kernel_table(count_out, count_in, offset, length):
    focal_pos = (jnp.arange(count_out, dtype=jnp.float32) + 0.5) / count_out - 0.5
    cell_pos = (offset.astype(jnp.float32) + jnp.arange(length, dtype=jnp.float32) + 0.5) / count_in - 0.5
    phase = (math.pi * count_out) * (focal_pos[:, None] - cell_pos[None, :]) ** 2
    return jnp.cos(phase), jnp.sin(phase)


def contract(pattern, first_op, second_op):
    return jnp.einsum(pattern, first_op, second_op, precision=lax.Precision.HIGHEST)


def project_forward(mon_re, mon_im, table_x, table_y, norm_scale):
    x_re, x_im = table_x
    y_re, y_im = table_y
    part_re = contract("ux,cxy->cuy", x_re, mon_re) - contract("ux,cxy->cuy", x_im, mon_im)
    part_im = contract("ux,cxy->cuy", x_re, mon_im) + contract("ux,cxy->cuy", x_im, mon_re)
    far_re = contract("cuy,vy->cuv", part_re, y_re) - contract("cuy,vy->cuv", part_im, y_im)
    far_im = contract("cuy,vy->cuv", part_re, y_im) + contract("cuy,vy->cuv", part_im, y_re)
    return norm_scale * jnp.stack([far_re, far_im])


def project_back(weighted, table_x, table_y, norm_scale):
    x_re, x_im = table_x
    y_re, y_im = table_y
    w_re = weighted[0]
    w_im = weighted[1]
    half_re = contract("cuv,vy->cuy", w_re, y_re) - contract("cuv,vy->cuy", w_im, y_im)
    half_im = contract("cuv,vy->cuy", w_re, y_im) + contract("cuv,vy->cuy", w_im, y_re)
    back_re = contract("ux,cuy->cxy", x_re, half_re) - contract("ux,cuy->cxy", x_im, half_im)
    back_im = contract("ux,cuy->cxy", x_re, half_im) + contract("ux,cuy->cxy", x_im, half_re)
    return 2.0 * norm_scale * back_re, 2.0 * norm_scale * back_im


def reference(fields, eps_background, target, widths, intersection, pillar_tile, anchors):
    offsets = jnp.arange(16, dtype=jnp.int32)
    tiles_y = NY // TILE
    tile_ids = pillar_tile[:, 0]
    start_x = (tile_ids // tiles_y) * TILE + anchors[:, 0]
    start_y = (tile_ids % tiles_y) * TILE + anchors[:, 1]
    cells_x = start_x[:, None] + (offsets // 4)[None, :]
    cells_y = start_y[:, None] + (offsets % 4)[None, :]
    filling = jnp.zeros((NX, NY), jnp.float32).at[cells_x, cells_y].add(intersection * widths[:, None])
    z_index = jnp.arange(NZ, dtype=jnp.int32)
    layers = ((z_index >= ZM - ZP) & (z_index < ZM)).astype(jnp.float32)
    permittivity = eps_background + DELTA_EPS * filling[:, :, None] * layers[None, None, :]
    inv_eps = 1.0 / permittivity
    blank = jnp.zeros_like(eps_background)
    fields_now = tuple(fields[component] for component in range(6))
    mon_re = jnp.zeros((2, NX, NY), jnp.float32)
    mon_im = jnp.zeros((2, NX, NY), jnp.float32)
    changes = []
    for moment in range(1, NT + 1):
        before = fields_now[:3]
        fields_now = leap_step(fields_now, inv_eps, (blank, blank, blank))
        monitor = jnp.stack([fields_now[0][:, :, ZM], fields_now[1][:, :, ZM]])
        mon_re = mon_re + math.cos(ANGULAR_STEP * moment) * monitor
        mon_im = mon_im - math.sin(ANGULAR_STEP * moment) * monitor
        changes.append(tuple((fields_now[component] - before[component])[:, :, ZM - ZP:ZM] for component in range(3)))
    norm_scale = (NX * NY) ** -0.5
    table_x = kernel_table(U, NX, jnp.zeros((), jnp.int32), NX)
    table_y = kernel_table(V, NY, jnp.zeros((), jnp.int32), NY)
    far_field = project_forward(mon_re, mon_im, table_x, table_y, norm_scale)
    focal_power = jnp.sum(far_field * far_field, axis=(0, 1))
    weighted = jnp.stack([target * far_field[0], -(target * far_field[1])])
    back_re, back_im = project_back(weighted, table_x, table_y, norm_scale)
    adjoint = tuple(blank for component in range(6))
    inv_layer = inv_eps[:, :, ZM - ZP:ZM]
    grad_eps = jnp.zeros((NX, NY, ZP), jnp.float32)
    for moment in range(1, NT + 1):
        source_step = NT + 1 - moment
        adj_drive = math.cos(ANGULAR_STEP * source_step) * back_re + math.sin(ANGULAR_STEP * source_step) * back_im
        source_x = blank.at[:, :, ZM].set(adj_drive[0])
        source_y = blank.at[:, :, ZM].set(adj_drive[1])
        adjoint = leap_step(adjoint, inv_eps, (source_x, source_y, blank))
        change = changes[source_step - 1]
        product = adjoint[0][:, :, ZM - ZP:ZM] * change[0] + adjoint[1][:, :, ZM - ZP:ZM] * change[1] + adjoint[2][:, :, ZM - ZP:ZM] * change[2]
        grad_eps = grad_eps - product * inv_layer
    column_grad = jnp.sum(grad_eps, axis=2)
    grad_widths = DELTA_EPS * jnp.sum(intersection * column_grad[cells_x, cells_y], axis=1)
    return jnp.stack(fields_now), focal_power, grad_widths
```

```python
import math

import jax
import jax.numpy as jnp
from jax import lax
from jax.sharding import PartitionSpec as P

TILE = 32
P_DEV = 128
NT = 4
ZP = 4
U = 256
V = 256
ZM = 64


COURANT = 0.5
ANGULAR_STEP = 0.9
DELTA_EPS = 4.0


def passed_along(shard, axis, by):
    count = lax.axis_size(axis)
    pairs = [(i, i + by) for i in range(count) if 0 <= i + by < count]
    return lax.ppermute(shard, axis, pairs)


def plus_diff(field, rim_layer, axis):
    extended = jnp.concatenate([field, rim_layer], axis=axis)
    return lax.slice_in_dim(extended, 1, extended.shape[axis], axis=axis) - field


def minus_diff(field, rim_layer, axis):
    extended = jnp.concatenate([rim_layer, field], axis=axis)
    return field - lax.slice_in_dim(extended, 0, field.shape[axis], axis=axis)


def leap_step(fields_now, inv_eps, sources):
    elec_x, elec_y, elec_z, magn_x, magn_y, magn_z = fields_now
    z_blank = jnp.zeros_like(elec_x[:, :, :1])
    rim_east = passed_along(jnp.stack([elec_y[:1], elec_z[:1]]), "gx", -1)
    rim_north = passed_along(jnp.stack([elec_x[:, :1], elec_z[:, :1]]), "gy", -1)
    curl_x = plus_diff(elec_z, rim_north[1], 1) - plus_diff(elec_y, z_blank, 2)
    curl_y = plus_diff(elec_x, z_blank, 2) - plus_diff(elec_z, rim_east[1], 0)
    curl_z = plus_diff(elec_y, rim_east[0], 0) - plus_diff(elec_x, rim_north[0], 1)
    magn_x = magn_x - COURANT * curl_x
    magn_y = magn_y - COURANT * curl_y
    magn_z = magn_z - COURANT * curl_z
    rim_west = passed_along(jnp.stack([magn_y[-1:], magn_z[-1:]]), "gx", 1)
    rim_south = passed_along(jnp.stack([magn_x[:, -1:], magn_z[:, -1:]]), "gy", 1)
    curl_x = minus_diff(magn_z, rim_south[1], 1) - minus_diff(magn_y, z_blank, 2)
    curl_y = minus_diff(magn_x, z_blank, 2) - minus_diff(magn_z, rim_west[1], 0)
    curl_z = minus_diff(magn_y, rim_west[0], 0) - minus_diff(magn_x, rim_south[0], 1)
    elec_x = elec_x + COURANT * (curl_x - sources[0]) * inv_eps
    elec_y = elec_y + COURANT * (curl_y - sources[1]) * inv_eps
    elec_z = elec_z + COURANT * curl_z * inv_eps
    return (elec_x, elec_y, elec_z, magn_x, magn_y, magn_z)


def kernel_table(count_out, count_in, offset, length):
    focal_pos = (jnp.arange(count_out, dtype=jnp.float32) + 0.5) / count_out - 0.5
    cell_pos = (
        offset.astype(jnp.float32) + jnp.arange(length, dtype=jnp.float32) + 0.5
    ) / count_in - 0.5
    phase = math.pi * count_out * (focal_pos[:, None] - cell_pos[None, :]) ** 2
    return (jnp.cos(phase), jnp.sin(phase))


def contract(pattern, first_op, second_op):
    return jnp.einsum(pattern, first_op, second_op, precision=lax.Precision.HIGHEST)


def route_pillars(rows, slot_ids, devices, capacity):
    slots = devices * capacity
    placing = (slot_ids[:, None] == jnp.arange(slots, dtype=jnp.int32)[None, :]).astype(
        jnp.float32
    )
    packed = contract("ps,pk->sk", placing, rows)
    got = lax.all_to_all(
        packed.reshape(devices, capacity, rows.shape[1]),
        ("gx", "gy"),
        split_axis=0,
        concat_axis=0,
        tiled=True,
    )
    return placing, got.reshape(slots, rows.shape[1])


def shards(fields, eps_background, target, widths, intersection, pillar_tile, anchors):
    span_x = lax.axis_size("gx")
    span_y = lax.axis_size("gy")
    devices = span_x * span_y
    place_x = lax.axis_index("gx")
    place_y = lax.axis_index("gy")
    linear = place_x * span_y + place_y
    offsets = jnp.arange(16, dtype=jnp.int32)
    capacity = 2 * max(1, P_DEV // devices)
    target_tile = pillar_tile[:, 0]
    onehot = (target_tile[:, None] == jnp.arange(devices, dtype=jnp.int32)[None, :]).astype(
        jnp.int32
    )
    earlier = jnp.cumsum(onehot, axis=0) - onehot
    order_in = jnp.sum(earlier * onehot, axis=1)
    slot_ids = target_tile * capacity + order_in
    rows = jnp.concatenate(
        [intersection * widths[:, None], anchors.astype(jnp.float32)], axis=1
    )
    placing, got = route_pillars(rows, slot_ids, devices, capacity)
    local_vals = got[:, :16]
    local_at = got[:, 16:18].astype(jnp.int32)
    cells_x = (local_at[:, 0:1] + (offsets // 4)[None, :]).reshape(-1)
    cells_y = (local_at[:, 1:2] + (offsets % 4)[None, :]).reshape(-1)
    lanes = jnp.arange(TILE, dtype=jnp.int32)
    pick_x = (cells_x[:, None] == lanes[None, :]).astype(jnp.float32)
    pick_y = (cells_y[:, None] == lanes[None, :]).astype(jnp.float32)
    filling = contract("sx,sy->xy", pick_x, pick_y * local_vals.reshape(-1)[:, None])
    z_index = jnp.arange(fields.shape[3], dtype=jnp.int32)
    layers = ((z_index >= ZM - ZP) & (z_index < ZM)).astype(jnp.float32)
    permittivity = eps_background + DELTA_EPS * filling[:, :, None] * layers[None, None, :]
    inv_eps = 1.0 / permittivity
    blank = jnp.zeros_like(eps_background)
    fields_now = tuple((fields[component] for component in range(6)))
    mon_re = jnp.zeros((2, TILE, TILE), jnp.float32)
    mon_im = jnp.zeros((2, TILE, TILE), jnp.float32)
    changes = []
    for moment in range(1, NT + 1):
        before = fields_now[:3]
        fields_now = leap_step(fields_now, inv_eps, (blank, blank, blank))
        monitor = jnp.stack([fields_now[0][:, :, ZM], fields_now[1][:, :, ZM]])
        mon_re = mon_re + math.cos(ANGULAR_STEP * moment) * monitor
        mon_im = mon_im - math.sin(ANGULAR_STEP * moment) * monitor
        changes.append(
            tuple(
                (
                    (fields_now[component] - before[component])[:, :, ZM - ZP : ZM]
                    for component in range(3)
                )
            )
        )
    norm_scale = (TILE * span_x * TILE * span_y) ** (-0.5)
    x_re, x_im = kernel_table(U, TILE * span_x, place_x * TILE, TILE)
    y_re, y_im = kernel_table(V, TILE * span_y, place_y * TILE, TILE)
    part = jnp.stack(
        [
            contract("ux,cxy->ucy", x_re, mon_re) - contract("ux,cxy->ucy", x_im, mon_im),
            contract("ux,cxy->ucy", x_re, mon_im) + contract("ux,cxy->ucy", x_im, mon_re),
        ]
    )
    part = lax.psum_scatter(part, "gx", scatter_dimension=1, tiled=True)
    part_re, part_im = part[0], part[1]
    far = jnp.stack(
        [
            contract("ucy,vy->cuv", part_re, y_re) - contract("ucy,vy->cuv", part_im, y_im),
            contract("ucy,vy->cuv", part_re, y_im) + contract("ucy,vy->cuv", part_im, y_re),
        ],
        axis=2,
    )
    far = norm_scale * lax.psum_scatter(far, "gy", scatter_dimension=1, tiled=True)
    row_count = U // devices
    focal_power = jnp.sum(far * far, axis=(0, 2))
    mine_target = lax.dynamic_slice_in_dim(target, linear * row_count, row_count, 0)
    weighted = jnp.stack(
        [mine_target * far[:, :, 0], -(mine_target * far[:, :, 1])], axis=2
    )
    weighted = lax.all_gather(weighted, "gy", axis=1, tiled=True)
    w_re, w_im = weighted[:, :, 0], weighted[:, :, 1]
    half = jnp.stack(
        [
            contract("cuv,vy->cuy", w_re, y_re) - contract("cuv,vy->cuy", w_im, y_im),
            contract("cuv,vy->cuy", w_re, y_im) + contract("cuv,vy->cuy", w_im, y_re),
        ]
    )
    half = lax.all_gather(half, "gx", axis=2, tiled=True)
    half_re, half_im = half[0], half[1]
    back_re = 2.0 * norm_scale * (
        contract("ux,cuy->cxy", x_re, half_re) - contract("ux,cuy->cxy", x_im, half_im)
    )
    back_im = 2.0 * norm_scale * (
        contract("ux,cuy->cxy", x_re, half_im) + contract("ux,cuy->cxy", x_im, half_re)
    )
    adjoint = tuple((blank for component in range(6)))
    inv_layer = inv_eps[:, :, ZM - ZP : ZM]
    grad_eps = jnp.zeros((TILE, TILE, ZP), jnp.float32)
    for moment in range(1, NT + 1):
        source_step = NT + 1 - moment
        adj_drive = (
            math.cos(ANGULAR_STEP * source_step) * back_re
            + math.sin(ANGULAR_STEP * source_step) * back_im
        )
        source_x = blank.at[:, :, ZM].set(adj_drive[0])
        source_y = blank.at[:, :, ZM].set(adj_drive[1])
        adjoint = leap_step(adjoint, inv_eps, (source_x, source_y, blank))
        change = changes[source_step - 1]
        product = (
            adjoint[0][:, :, ZM - ZP : ZM] * change[0]
            + adjoint[1][:, :, ZM - ZP : ZM] * change[1]
            + adjoint[2][:, :, ZM - ZP : ZM] * change[2]
        )
        grad_eps = grad_eps - product * inv_layer
    column_grad = jnp.sum(grad_eps, axis=2)
    spread = contract("sx,xy->sy", pick_x, column_grad)
    picked = jnp.sum(spread * pick_y, axis=1).reshape(devices * capacity, 16)
    returned = lax.all_to_all(
        picked.reshape(devices, capacity, 16), ("gx", "gy"), split_axis=0, concat_axis=0, tiled=True
    )
    own_vals = contract("ps,sk->pk", placing, returned.reshape(devices * capacity, 16))
    grad_widths = DELTA_EPS * jnp.sum(intersection * own_vals, axis=1)
    return (jnp.stack(fields_now), focal_power, grad_widths)


def solution(mesh):
    placed = (
        P(None, "gx", "gy", None),
        P("gx", "gy", None),
        P(),
        P(("gx", "gy")),
        P(("gx", "gy"), None),
        P(("gx", "gy"), None),
        P(("gx", "gy"), None),
    )
    return jax.shard_map(
        shards,
        mesh=mesh,
        in_specs=placed,
        out_specs=(P(None, "gx", "gy", None), P(("gx", "gy"), None), P(("gx", "gy"))),
        check_vma=False,
    )
```

```python
import math

import jax
import jax.numpy as jnp
from jax import lax
from jax.sharding import PartitionSpec as P
from jax.experimental import pallas as pl
from jax.experimental.pallas import tpu as pltpu

TILE = 32
P_DEV = 128
NT = 4
ZP = 4
U = 256
V = 256
ZM = 64


COURANT = 0.5
ANGULAR_STEP = 0.9
DELTA_EPS = 4.0


def passed_along(shard, axis, by):
    count = lax.axis_size(axis)
    pairs = [(i, i + by) for i in range(count) if 0 <= i + by < count]
    return lax.ppermute(shard, axis, pairs)


def plus_diff(field, rim_layer, axis):
    extended = jnp.concatenate([field, rim_layer], axis=axis)
    return lax.slice_in_dim(extended, 1, extended.shape[axis], axis=axis) - field


def minus_diff(field, rim_layer, axis):
    extended = jnp.concatenate([rim_layer, field], axis=axis)
    return field - lax.slice_in_dim(extended, 0, field.shape[axis], axis=axis)


def leap_step(fields_now, inv_eps, sources):
    elec_x, elec_y, elec_z, magn_x, magn_y, magn_z = fields_now
    z_blank = jnp.zeros_like(elec_x[:, :, :1])
    rim_east = passed_along(jnp.stack([elec_y[:1], elec_z[:1]]), "gx", -1)
    rim_north = passed_along(jnp.stack([elec_x[:, :1], elec_z[:, :1]]), "gy", -1)
    curl_x = plus_diff(elec_z, rim_north[1], 1) - plus_diff(elec_y, z_blank, 2)
    curl_y = plus_diff(elec_x, z_blank, 2) - plus_diff(elec_z, rim_east[1], 0)
    curl_z = plus_diff(elec_y, rim_east[0], 0) - plus_diff(elec_x, rim_north[0], 1)
    magn_x = magn_x - COURANT * curl_x
    magn_y = magn_y - COURANT * curl_y
    magn_z = magn_z - COURANT * curl_z
    rim_west = passed_along(jnp.stack([magn_y[-1:], magn_z[-1:]]), "gx", 1)
    rim_south = passed_along(jnp.stack([magn_x[:, -1:], magn_z[:, -1:]]), "gy", 1)
    curl_x = minus_diff(magn_z, rim_south[1], 1) - minus_diff(magn_y, z_blank, 2)
    curl_y = minus_diff(magn_x, z_blank, 2) - minus_diff(magn_z, rim_west[1], 0)
    curl_z = minus_diff(magn_y, rim_west[0], 0) - minus_diff(magn_x, rim_south[0], 1)
    elec_x = elec_x + COURANT * (curl_x - sources[0]) * inv_eps
    elec_y = elec_y + COURANT * (curl_y - sources[1]) * inv_eps
    elec_z = elec_z + COURANT * curl_z * inv_eps
    return (elec_x, elec_y, elec_z, magn_x, magn_y, magn_z)


def group_of(axes):
    sizes = [lax.axis_size(a) for a in axes]
    count = math.prod(sizes)
    return count, sizes


def group_place(axes, sizes):
    place = 0
    for axis, size in zip(axes, sizes):
        place = place * size + lax.axis_index(axis)
    return place


def group_device(axes, sizes, peer):
    coords = {}
    rest = peer
    for axis, size in reversed(list(zip(axes, sizes))):
        coords[axis] = rest % size
        rest = rest // size
    return tuple(coords[a] if a in coords else lax.axis_index(a) for a in ("gx", "gy"))


def exchange(pieces, axes, gather, tag):
    count, sizes = group_of(axes)
    piece_shape = pieces.shape if gather else pieces.shape[1:]

    def kernel(x_ref, o_ref, send_sem, recv_sem):
        me = group_place(axes, sizes)
        barrier = pltpu.get_barrier_semaphore()
        for step in range(1, count):
            peer = lax.rem(me + step, count)
            pl.semaphore_signal(
                barrier, 1, device_id=group_device(axes, sizes, peer),
                device_id_type=pl.DeviceIdType.MESH,
            )
        pl.semaphore_wait(barrier, count - 1)
        copies = []
        for step in range(1, count):
            peer = lax.rem(me + step, count)
            copy = pltpu.make_async_remote_copy(
                src_ref=x_ref if gather else x_ref.at[peer],
                dst_ref=o_ref.at[me],
                send_sem=send_sem.at[step],
                recv_sem=recv_sem.at[step],
                device_id=group_device(axes, sizes, peer),
                device_id_type=pl.DeviceIdType.MESH,
            )
            copy.start()
            copies.append(copy)
        own = x_ref[...] if gather else x_ref[me]
        o_ref[me] = own
        for copy in copies:
            copy.wait_send()
        for step in range(1, count):
            source = lax.rem(me + count - step, count)
            pltpu.make_async_remote_copy(
                src_ref=x_ref if gather else x_ref.at[source],
                dst_ref=o_ref.at[source],
                send_sem=send_sem.at[step],
                recv_sem=recv_sem.at[step],
                device_id=group_device(axes, sizes, source),
                device_id_type=pl.DeviceIdType.MESH,
            ).wait_recv()

    return pl.pallas_call(
        kernel,
        out_shape=jax.ShapeDtypeStruct((count,) + tuple(piece_shape), pieces.dtype),
        in_specs=[pl.BlockSpec(memory_space=pltpu.VMEM)],
        out_specs=pl.BlockSpec(memory_space=pltpu.VMEM),
        scratch_shapes=[pltpu.SemaphoreType.DMA((count,)), pltpu.SemaphoreType.DMA((count,))],
        compiler_params=pltpu.CompilerParams(collective_id=tag, has_side_effects=True),
    )(pieces)


def kernel_table(count_out, count_in, offset, length):
    focal_pos = (jnp.arange(count_out, dtype=jnp.float32) + 0.5) / count_out - 0.5
    cell_pos = (
        offset.astype(jnp.float32) + jnp.arange(length, dtype=jnp.float32) + 0.5
    ) / count_in - 0.5
    phase = math.pi * count_out * (focal_pos[:, None] - cell_pos[None, :]) ** 2
    return (jnp.cos(phase), jnp.sin(phase))


def contract(pattern, first_op, second_op):
    return jnp.einsum(pattern, first_op, second_op, precision=lax.Precision.HIGHEST)


def route_pillars(rows, slot_ids, devices, capacity):
    slots = devices * capacity
    placing = (slot_ids[:, None] == jnp.arange(slots, dtype=jnp.int32)[None, :]).astype(
        jnp.float32
    )
    packed = contract("ps,pk->sk", placing, rows)
    got = exchange(packed.reshape(devices, capacity, rows.shape[1]), ("gx", "gy"), False, 0)
    return placing, got.reshape(slots, rows.shape[1])


def shards(fields, eps_background, target, widths, intersection, pillar_tile, anchors):
    span_x = lax.axis_size("gx")
    span_y = lax.axis_size("gy")
    devices = span_x * span_y
    place_x = lax.axis_index("gx")
    place_y = lax.axis_index("gy")
    linear = place_x * span_y + place_y
    offsets = jnp.arange(16, dtype=jnp.int32)
    capacity = 2 * max(1, P_DEV // devices)
    target_tile = pillar_tile[:, 0]
    onehot = (target_tile[:, None] == jnp.arange(devices, dtype=jnp.int32)[None, :]).astype(
        jnp.int32
    )
    earlier = jnp.cumsum(onehot, axis=0) - onehot
    order_in = jnp.sum(earlier * onehot, axis=1)
    slot_ids = target_tile * capacity + order_in
    rows = jnp.concatenate(
        [intersection * widths[:, None], anchors.astype(jnp.float32)], axis=1
    )
    placing, got = route_pillars(rows, slot_ids, devices, capacity)
    local_vals = got[:, :16]
    local_at = got[:, 16:18].astype(jnp.int32)
    cells_x = (local_at[:, 0:1] + (offsets // 4)[None, :]).reshape(-1)
    cells_y = (local_at[:, 1:2] + (offsets % 4)[None, :]).reshape(-1)
    lanes = jnp.arange(TILE, dtype=jnp.int32)
    pick_x = (cells_x[:, None] == lanes[None, :]).astype(jnp.float32)
    pick_y = (cells_y[:, None] == lanes[None, :]).astype(jnp.float32)
    filling = contract("sx,sy->xy", pick_x, pick_y * local_vals.reshape(-1)[:, None])
    z_index = jnp.arange(fields.shape[3], dtype=jnp.int32)
    layers = ((z_index >= ZM - ZP) & (z_index < ZM)).astype(jnp.float32)
    permittivity = eps_background + DELTA_EPS * filling[:, :, None] * layers[None, None, :]
    inv_eps = 1.0 / permittivity
    blank = jnp.zeros_like(eps_background)
    fields_now = tuple((fields[component] for component in range(6)))
    mon_re = jnp.zeros((2, TILE, TILE), jnp.float32)
    mon_im = jnp.zeros((2, TILE, TILE), jnp.float32)
    changes = []
    for moment in range(1, NT + 1):
        before = fields_now[:3]
        fields_now = leap_step(fields_now, inv_eps, (blank, blank, blank))
        monitor = jnp.stack([fields_now[0][:, :, ZM], fields_now[1][:, :, ZM]])
        mon_re = mon_re + math.cos(ANGULAR_STEP * moment) * monitor
        mon_im = mon_im - math.sin(ANGULAR_STEP * moment) * monitor
        changes.append(
            tuple(
                (
                    (fields_now[component] - before[component])[:, :, ZM - ZP : ZM]
                    for component in range(3)
                )
            )
        )
    norm_scale = (TILE * span_x * TILE * span_y) ** (-0.5)
    x_re, x_im = kernel_table(U, TILE * span_x, place_x * TILE, TILE)
    y_re, y_im = kernel_table(V, TILE * span_y, place_y * TILE, TILE)
    part = jnp.stack(
        [
            contract("ux,cxy->ucy", x_re, mon_re) - contract("ux,cxy->ucy", x_im, mon_im),
            contract("ux,cxy->ucy", x_re, mon_im) + contract("ux,cxy->ucy", x_im, mon_re),
        ]
    )
    chunk_u = U // span_x
    part = part.reshape(2, span_x, chunk_u, 2, TILE).transpose(1, 2, 0, 3, 4)
    part = exchange(part.reshape(span_x, chunk_u, 4 * TILE), ("gx",), False, 1)
    part = jnp.sum(part, axis=0).reshape(chunk_u, 2, 2, TILE)
    part_re, part_im = part[:, 0], part[:, 1]
    far = jnp.stack(
        [
            contract("ucy,vy->cuv", part_re, y_re) - contract("ucy,vy->cuv", part_im, y_im),
            contract("ucy,vy->cuv", part_re, y_im) + contract("ucy,vy->cuv", part_im, y_re),
        ],
        axis=2,
    )
    row_count = U // devices
    far = far.reshape(2, span_y, row_count, 2, V).transpose(1, 0, 2, 3, 4)
    far = exchange(far.reshape(span_y, 2 * row_count * 2, V), ("gy",), False, 2)
    far = norm_scale * jnp.sum(far, axis=0).reshape(2, row_count, 2, V)
    focal_power = jnp.sum(far * far, axis=(0, 2))
    mine_target = lax.dynamic_slice_in_dim(target, linear * row_count, row_count, 0)
    weighted = jnp.stack(
        [mine_target * far[:, :, 0], -(mine_target * far[:, :, 1])], axis=2
    )
    weighted = exchange(weighted.reshape(2 * row_count * 2, V), ("gy",), True, 3)
    weighted = weighted.reshape(span_y, 2, row_count, 2, V).transpose(1, 0, 2, 3, 4)
    weighted = weighted.reshape(2, span_y * row_count, 2, V)
    w_re, w_im = weighted[:, :, 0], weighted[:, :, 1]
    half = jnp.stack(
        [
            contract("cuv,vy->cuy", w_re, y_re) - contract("cuv,vy->cuy", w_im, y_im),
            contract("cuv,vy->cuy", w_re, y_im) + contract("cuv,vy->cuy", w_im, y_re),
        ]
    )
    half = half.transpose(2, 0, 1, 3).reshape(chunk_u, 4 * TILE)
    half = exchange(half, ("gx",), True, 4)
    half = half.reshape(span_x * chunk_u, 2, 2, TILE).transpose(1, 2, 0, 3)
    half_re, half_im = half[0], half[1]
    back_re = 2.0 * norm_scale * (
        contract("ux,cuy->cxy", x_re, half_re) - contract("ux,cuy->cxy", x_im, half_im)
    )
    back_im = 2.0 * norm_scale * (
        contract("ux,cuy->cxy", x_re, half_im) + contract("ux,cuy->cxy", x_im, half_re)
    )
    adjoint = tuple((blank for component in range(6)))
    inv_layer = inv_eps[:, :, ZM - ZP : ZM]
    grad_eps = jnp.zeros((TILE, TILE, ZP), jnp.float32)
    for moment in range(1, NT + 1):
        source_step = NT + 1 - moment
        adj_drive = (
            math.cos(ANGULAR_STEP * source_step) * back_re
            + math.sin(ANGULAR_STEP * source_step) * back_im
        )
        source_x = blank.at[:, :, ZM].set(adj_drive[0])
        source_y = blank.at[:, :, ZM].set(adj_drive[1])
        adjoint = leap_step(adjoint, inv_eps, (source_x, source_y, blank))
        change = changes[source_step - 1]
        product = (
            adjoint[0][:, :, ZM - ZP : ZM] * change[0]
            + adjoint[1][:, :, ZM - ZP : ZM] * change[1]
            + adjoint[2][:, :, ZM - ZP : ZM] * change[2]
        )
        grad_eps = grad_eps - product * inv_layer
    column_grad = jnp.sum(grad_eps, axis=2)
    spread = contract("sx,xy->sy", pick_x, column_grad)
    picked = jnp.sum(spread * pick_y, axis=1).reshape(devices * capacity, 16)
    returned = exchange(picked.reshape(devices, capacity, 16), ("gx", "gy"), False, 5)
    own_vals = contract("ps,sk->pk", placing, returned.reshape(devices * capacity, 16))
    grad_widths = DELTA_EPS * jnp.sum(intersection * own_vals, axis=1)
    return (jnp.stack(fields_now), focal_power, grad_widths)


def solution(mesh):
    placed = (
        P(None, "gx", "gy", None),
        P("gx", "gy", None),
        P(),
        P(("gx", "gy")),
        P(("gx", "gy"), None),
        P(("gx", "gy"), None),
        P(("gx", "gy"), None),
    )
    return jax.shard_map(
        shards,
        mesh=mesh,
        in_specs=placed,
        out_specs=(P(None, "gx", "gy", None), P(("gx", "gy"), None), P(("gx", "gy"))),
        check_vma=False,
    )
```

```python
import math

import jax
import jax.numpy as jnp
from jax import lax
from jax.sharding import PartitionSpec as P
from jax.experimental import pallas as pl
from jax.experimental.pallas import tpu as pltpu

TILE = 32
P_DEV = 128
NT = 4
ZP = 4
U = 256
V = 256
ZM = 64


COURANT = 0.5
ANGULAR_STEP = 0.9
DELTA_EPS = 4.0


def passed_along(shard, axis, by):
    count = lax.axis_size(axis)
    pairs = [(i, i + by) for i in range(count) if 0 <= i + by < count]
    return lax.ppermute(shard, axis, pairs)


def plus_diff(field, rim_layer, axis):
    extended = jnp.concatenate([field, rim_layer], axis=axis)
    return lax.slice_in_dim(extended, 1, extended.shape[axis], axis=axis) - field


def minus_diff(field, rim_layer, axis):
    extended = jnp.concatenate([rim_layer, field], axis=axis)
    return field - lax.slice_in_dim(extended, 0, field.shape[axis], axis=axis)


def rim_swap(rim_x, rim_y, by, tag):
    span_x = lax.axis_size("gx")
    span_y = lax.axis_size("gy")

    def kernel(rx_ref, ry_ref, ox_ref, oy_ref, send_sem, recv_sem):
        px = lax.axis_index("gx")
        py = lax.axis_index("gy")
        barrier = pltpu.get_barrier_semaphore()
        for peer in (
            (lax.rem(px + 1, span_x), py),
            (lax.rem(px + span_x - 1, span_x), py),
            (px, lax.rem(py + 1, span_y)),
            (px, lax.rem(py + span_y - 1, span_y)),
        ):
            pl.semaphore_signal(barrier, 1, device_id=peer, device_id_type=pl.DeviceIdType.MESH)
        pl.semaphore_wait(barrier, 4)
        to_x = px + by
        to_y = py + by
        from_x = px - by
        from_y = py - by
        copy_x = pltpu.make_async_remote_copy(
            src_ref=rx_ref, dst_ref=ox_ref, send_sem=send_sem.at[0], recv_sem=recv_sem.at[0],
            device_id=(lax.rem(to_x + span_x, span_x), py), device_id_type=pl.DeviceIdType.MESH,
        )
        copy_y = pltpu.make_async_remote_copy(
            src_ref=ry_ref, dst_ref=oy_ref, send_sem=send_sem.at[1], recv_sem=recv_sem.at[1],
            device_id=(px, lax.rem(to_y + span_y, span_y)), device_id_type=pl.DeviceIdType.MESH,
        )
        sends_x = (to_x >= 0) & (to_x < span_x)
        sends_y = (to_y >= 0) & (to_y < span_y)
        gets_x = (from_x >= 0) & (from_x < span_x)
        gets_y = (from_y >= 0) & (from_y < span_y)

        @pl.when(sends_x)
        def _():
            copy_x.start()

        @pl.when(sends_y)
        def _():
            copy_y.start()

        @pl.when(jnp.logical_not(gets_x))
        def _():
            ox_ref[...] = jnp.zeros(ox_ref.shape, ox_ref.dtype)

        @pl.when(jnp.logical_not(gets_y))
        def _():
            oy_ref[...] = jnp.zeros(oy_ref.shape, oy_ref.dtype)

        @pl.when(sends_x)
        def _():
            copy_x.wait_send()

        @pl.when(sends_y)
        def _():
            copy_y.wait_send()

        @pl.when(gets_x)
        def _():
            copy_x.wait_recv()

        @pl.when(gets_y)
        def _():
            copy_y.wait_recv()

    return pl.pallas_call(
        kernel,
        out_shape=(
            jax.ShapeDtypeStruct(rim_x.shape, rim_x.dtype),
            jax.ShapeDtypeStruct(rim_y.shape, rim_y.dtype),
        ),
        in_specs=[pl.BlockSpec(memory_space=pltpu.VMEM)] * 2,
        out_specs=(pl.BlockSpec(memory_space=pltpu.VMEM),) * 2,
        scratch_shapes=[pltpu.SemaphoreType.DMA((2,)), pltpu.SemaphoreType.DMA((2,))],
        compiler_params=pltpu.CompilerParams(collective_id=tag, has_side_effects=True),
    )(rim_x, rim_y)


def leap_step(fields_now, inv_eps, sources, tag):
    elec_x, elec_y, elec_z, magn_x, magn_y, magn_z = fields_now
    z_blank = jnp.zeros_like(elec_x[:, :, :1])
    rim_east, rim_north = rim_swap(
        jnp.stack([elec_y[0], elec_z[0]]), jnp.stack([elec_x[:, 0], elec_z[:, 0]]), -1, tag
    )
    rim_east = rim_east[:, None]
    rim_north = rim_north[:, :, None]
    curl_x = plus_diff(elec_z, rim_north[1], 1) - plus_diff(elec_y, z_blank, 2)
    curl_y = plus_diff(elec_x, z_blank, 2) - plus_diff(elec_z, rim_east[1], 0)
    curl_z = plus_diff(elec_y, rim_east[0], 0) - plus_diff(elec_x, rim_north[0], 1)
    magn_x = magn_x - COURANT * curl_x
    magn_y = magn_y - COURANT * curl_y
    magn_z = magn_z - COURANT * curl_z
    rim_west, rim_south = rim_swap(
        jnp.stack([magn_y[-1], magn_z[-1]]), jnp.stack([magn_x[:, -1], magn_z[:, -1]]), 1, tag + 1
    )
    rim_west = rim_west[:, None]
    rim_south = rim_south[:, :, None]
    curl_x = minus_diff(magn_z, rim_south[1], 1) - minus_diff(magn_y, z_blank, 2)
    curl_y = minus_diff(magn_x, z_blank, 2) - minus_diff(magn_z, rim_west[1], 0)
    curl_z = minus_diff(magn_y, rim_west[0], 0) - minus_diff(magn_x, rim_south[0], 1)
    elec_x = elec_x + COURANT * (curl_x - sources[0]) * inv_eps
    elec_y = elec_y + COURANT * (curl_y - sources[1]) * inv_eps
    elec_z = elec_z + COURANT * curl_z * inv_eps
    return (elec_x, elec_y, elec_z, magn_x, magn_y, magn_z)


def group_of(axes):
    sizes = [lax.axis_size(a) for a in axes]
    count = math.prod(sizes)
    return count, sizes


def group_place(axes, sizes):
    place = 0
    for axis, size in zip(axes, sizes):
        place = place * size + lax.axis_index(axis)
    return place


def group_device(axes, sizes, peer):
    coords = {}
    rest = peer
    for axis, size in reversed(list(zip(axes, sizes))):
        coords[axis] = rest % size
        rest = rest // size
    return tuple(coords[a] if a in coords else lax.axis_index(a) for a in ("gx", "gy"))


def exchange(pieces, axes, gather, tag):
    count, sizes = group_of(axes)
    piece_shape = pieces.shape if gather else pieces.shape[1:]

    def kernel(x_ref, o_ref, send_sem, recv_sem):
        me = group_place(axes, sizes)
        barrier = pltpu.get_barrier_semaphore()
        for step in range(1, count):
            peer = lax.rem(me + step, count)
            pl.semaphore_signal(
                barrier, 1, device_id=group_device(axes, sizes, peer),
                device_id_type=pl.DeviceIdType.MESH,
            )
        pl.semaphore_wait(barrier, count - 1)
        copies = []
        for step in range(1, count):
            peer = lax.rem(me + step, count)
            copy = pltpu.make_async_remote_copy(
                src_ref=x_ref if gather else x_ref.at[peer],
                dst_ref=o_ref.at[me],
                send_sem=send_sem.at[step],
                recv_sem=recv_sem.at[step],
                device_id=group_device(axes, sizes, peer),
                device_id_type=pl.DeviceIdType.MESH,
            )
            copy.start()
            copies.append(copy)
        own = x_ref[...] if gather else x_ref[me]
        o_ref[me] = own
        for copy in copies:
            copy.wait_send()
        for step in range(1, count):
            source = lax.rem(me + count - step, count)
            pltpu.make_async_remote_copy(
                src_ref=x_ref if gather else x_ref.at[source],
                dst_ref=o_ref.at[source],
                send_sem=send_sem.at[step],
                recv_sem=recv_sem.at[step],
                device_id=group_device(axes, sizes, source),
                device_id_type=pl.DeviceIdType.MESH,
            ).wait_recv()

    return pl.pallas_call(
        kernel,
        out_shape=jax.ShapeDtypeStruct((count,) + tuple(piece_shape), pieces.dtype),
        in_specs=[pl.BlockSpec(memory_space=pltpu.VMEM)],
        out_specs=pl.BlockSpec(memory_space=pltpu.VMEM),
        scratch_shapes=[pltpu.SemaphoreType.DMA((count,)), pltpu.SemaphoreType.DMA((count,))],
        compiler_params=pltpu.CompilerParams(collective_id=tag, has_side_effects=True),
    )(pieces)


def kernel_table(count_out, count_in, offset, length):
    focal_pos = (jnp.arange(count_out, dtype=jnp.float32) + 0.5) / count_out - 0.5
    cell_pos = (
        offset.astype(jnp.float32) + jnp.arange(length, dtype=jnp.float32) + 0.5
    ) / count_in - 0.5
    phase = math.pi * count_out * (focal_pos[:, None] - cell_pos[None, :]) ** 2
    return (jnp.cos(phase), jnp.sin(phase))


def contract(pattern, first_op, second_op):
    return jnp.einsum(pattern, first_op, second_op, precision=lax.Precision.HIGHEST)


def route_pillars(rows, slot_ids, devices, capacity):
    slots = devices * capacity
    placing = (slot_ids[:, None] == jnp.arange(slots, dtype=jnp.int32)[None, :]).astype(
        jnp.float32
    )
    packed = contract("ps,pk->sk", placing, rows)
    got = exchange(packed.reshape(devices, capacity, rows.shape[1]), ("gx", "gy"), False, 0)
    return placing, got.reshape(slots, rows.shape[1])


def shards(fields, eps_background, target, widths, intersection, pillar_tile, anchors):
    span_x = lax.axis_size("gx")
    span_y = lax.axis_size("gy")
    devices = span_x * span_y
    place_x = lax.axis_index("gx")
    place_y = lax.axis_index("gy")
    linear = place_x * span_y + place_y
    offsets = jnp.arange(16, dtype=jnp.int32)
    capacity = 2 * max(1, P_DEV // devices)
    target_tile = pillar_tile[:, 0]
    onehot = (target_tile[:, None] == jnp.arange(devices, dtype=jnp.int32)[None, :]).astype(
        jnp.int32
    )
    earlier = jnp.cumsum(onehot, axis=0) - onehot
    order_in = jnp.sum(earlier * onehot, axis=1)
    slot_ids = target_tile * capacity + order_in
    rows = jnp.concatenate(
        [intersection * widths[:, None], anchors.astype(jnp.float32)], axis=1
    )
    placing, got = route_pillars(rows, slot_ids, devices, capacity)
    local_vals = got[:, :16]
    local_at = got[:, 16:18].astype(jnp.int32)
    cells_x = (local_at[:, 0:1] + (offsets // 4)[None, :]).reshape(-1)
    cells_y = (local_at[:, 1:2] + (offsets % 4)[None, :]).reshape(-1)
    lanes = jnp.arange(TILE, dtype=jnp.int32)
    pick_x = (cells_x[:, None] == lanes[None, :]).astype(jnp.float32)
    pick_y = (cells_y[:, None] == lanes[None, :]).astype(jnp.float32)
    filling = contract("sx,sy->xy", pick_x, pick_y * local_vals.reshape(-1)[:, None])
    z_index = jnp.arange(fields.shape[3], dtype=jnp.int32)
    layers = ((z_index >= ZM - ZP) & (z_index < ZM)).astype(jnp.float32)
    permittivity = eps_background + DELTA_EPS * filling[:, :, None] * layers[None, None, :]
    inv_eps = 1.0 / permittivity
    blank = jnp.zeros_like(eps_background)
    fields_now = tuple((fields[component] for component in range(6)))
    mon_re = jnp.zeros((2, TILE, TILE), jnp.float32)
    mon_im = jnp.zeros((2, TILE, TILE), jnp.float32)
    changes = []
    for moment in range(1, NT + 1):
        before = fields_now[:3]
        fields_now = leap_step(fields_now, inv_eps, (blank, blank, blank), 10 + 2 * moment)
        monitor = jnp.stack([fields_now[0][:, :, ZM], fields_now[1][:, :, ZM]])
        mon_re = mon_re + math.cos(ANGULAR_STEP * moment) * monitor
        mon_im = mon_im - math.sin(ANGULAR_STEP * moment) * monitor
        changes.append(
            tuple(
                (
                    (fields_now[component] - before[component])[:, :, ZM - ZP : ZM]
                    for component in range(3)
                )
            )
        )
    norm_scale = (TILE * span_x * TILE * span_y) ** (-0.5)
    x_re, x_im = kernel_table(U, TILE * span_x, place_x * TILE, TILE)
    y_re, y_im = kernel_table(V, TILE * span_y, place_y * TILE, TILE)
    part = jnp.stack(
        [
            contract("ux,cxy->ucy", x_re, mon_re) - contract("ux,cxy->ucy", x_im, mon_im),
            contract("ux,cxy->ucy", x_re, mon_im) + contract("ux,cxy->ucy", x_im, mon_re),
        ]
    )
    chunk_u = U // span_x
    part = part.reshape(2, span_x, chunk_u, 2, TILE).transpose(1, 2, 0, 3, 4)
    part = exchange(part.reshape(span_x, chunk_u, 4 * TILE), ("gx",), False, 1)
    part = jnp.sum(part, axis=0).reshape(chunk_u, 2, 2, TILE)
    part_re, part_im = part[:, 0], part[:, 1]
    far = jnp.stack(
        [
            contract("ucy,vy->cuv", part_re, y_re) - contract("ucy,vy->cuv", part_im, y_im),
            contract("ucy,vy->cuv", part_re, y_im) + contract("ucy,vy->cuv", part_im, y_re),
        ],
        axis=2,
    )
    row_count = U // devices
    far = far.reshape(2, span_y, row_count, 2, V).transpose(1, 0, 2, 3, 4)
    far = exchange(far.reshape(span_y, 2 * row_count * 2, V), ("gy",), False, 2)
    far = norm_scale * jnp.sum(far, axis=0).reshape(2, row_count, 2, V)
    focal_power = jnp.sum(far * far, axis=(0, 2))
    mine_target = lax.dynamic_slice_in_dim(target, linear * row_count, row_count, 0)
    weighted = jnp.stack(
        [mine_target * far[:, :, 0], -(mine_target * far[:, :, 1])], axis=2
    )
    weighted = exchange(weighted.reshape(2 * row_count * 2, V), ("gy",), True, 3)
    weighted = weighted.reshape(span_y, 2, row_count, 2, V).transpose(1, 0, 2, 3, 4)
    weighted = weighted.reshape(2, span_y * row_count, 2, V)
    w_re, w_im = weighted[:, :, 0], weighted[:, :, 1]
    half = jnp.stack(
        [
            contract("cuv,vy->cuy", w_re, y_re) - contract("cuv,vy->cuy", w_im, y_im),
            contract("cuv,vy->cuy", w_re, y_im) + contract("cuv,vy->cuy", w_im, y_re),
        ]
    )
    half = half.transpose(2, 0, 1, 3).reshape(chunk_u, 4 * TILE)
    half = exchange(half, ("gx",), True, 4)
    half = half.reshape(span_x * chunk_u, 2, 2, TILE).transpose(1, 2, 0, 3)
    half_re, half_im = half[0], half[1]
    back_re = 2.0 * norm_scale * (
        contract("ux,cuy->cxy", x_re, half_re) - contract("ux,cuy->cxy", x_im, half_im)
    )
    back_im = 2.0 * norm_scale * (
        contract("ux,cuy->cxy", x_re, half_im) + contract("ux,cuy->cxy", x_im, half_re)
    )
    adjoint = tuple((blank for component in range(6)))
    inv_layer = inv_eps[:, :, ZM - ZP : ZM]
    grad_eps = jnp.zeros((TILE, TILE, ZP), jnp.float32)
    for moment in range(1, NT + 1):
        source_step = NT + 1 - moment
        adj_drive = (
            math.cos(ANGULAR_STEP * source_step) * back_re
            + math.sin(ANGULAR_STEP * source_step) * back_im
        )
        source_x = blank.at[:, :, ZM].set(adj_drive[0])
        source_y = blank.at[:, :, ZM].set(adj_drive[1])
        adjoint = leap_step(adjoint, inv_eps, (source_x, source_y, blank), 20 + 2 * moment)
        change = changes[source_step - 1]
        product = (
            adjoint[0][:, :, ZM - ZP : ZM] * change[0]
            + adjoint[1][:, :, ZM - ZP : ZM] * change[1]
            + adjoint[2][:, :, ZM - ZP : ZM] * change[2]
        )
        grad_eps = grad_eps - product * inv_layer
    column_grad = jnp.sum(grad_eps, axis=2)
    spread = contract("sx,xy->sy", pick_x, column_grad)
    picked = jnp.sum(spread * pick_y, axis=1).reshape(devices * capacity, 16)
    returned = exchange(picked.reshape(devices, capacity, 16), ("gx", "gy"), False, 5)
    own_vals = contract("ps,sk->pk", placing, returned.reshape(devices * capacity, 16))
    grad_widths = DELTA_EPS * jnp.sum(intersection * own_vals, axis=1)
    return (jnp.stack(fields_now), focal_power, grad_widths)


def solution(mesh):
    placed = (
        P(None, "gx", "gy", None),
        P("gx", "gy", None),
        P(),
        P(("gx", "gy")),
        P(("gx", "gy"), None),
        P(("gx", "gy"), None),
        P(("gx", "gy"), None),
    )
    return jax.shard_map(
        shards,
        mesh=mesh,
        in_specs=placed,
        out_specs=(P(None, "gx", "gy", None), P(("gx", "gy"), None), P(("gx", "gy"))),
        check_vma=False,
    )
```

```python
import math

import jax
import jax.numpy as jnp
from jax import lax
from jax.sharding import PartitionSpec as P
from jax.experimental import pallas as pl
from jax.experimental.pallas import tpu as pltpu

TILE = 32
P_DEV = 128
NT = 4
ZP = 4
U = 256
V = 256
ZM = 64


COURANT = 0.5
ANGULAR_STEP = 0.9
DELTA_EPS = 4.0


def passed_along(shard, axis, by):
    count = lax.axis_size(axis)
    pairs = [(i, i + by) for i in range(count) if 0 <= i + by < count]
    return lax.ppermute(shard, axis, pairs)


def plus_diff(field, rim_layer, axis):
    extended = jnp.concatenate([field, rim_layer], axis=axis)
    return lax.slice_in_dim(extended, 1, extended.shape[axis], axis=axis) - field


def minus_diff(field, rim_layer, axis):
    extended = jnp.concatenate([rim_layer, field], axis=axis)
    return field - lax.slice_in_dim(extended, 0, field.shape[axis], axis=axis)


def leap_step(fields_now, inv_eps, sources):
    elec_x, elec_y, elec_z, magn_x, magn_y, magn_z = fields_now
    z_blank = jnp.zeros_like(elec_x[:, :, :1])
    rim_east = passed_along(jnp.stack([elec_y[:1], elec_z[:1]]), "gx", -1)
    rim_north = passed_along(jnp.stack([elec_x[:, :1], elec_z[:, :1]]), "gy", -1)
    curl_x = plus_diff(elec_z, rim_north[1], 1) - plus_diff(elec_y, z_blank, 2)
    curl_y = plus_diff(elec_x, z_blank, 2) - plus_diff(elec_z, rim_east[1], 0)
    curl_z = plus_diff(elec_y, rim_east[0], 0) - plus_diff(elec_x, rim_north[0], 1)
    magn_x = magn_x - COURANT * curl_x
    magn_y = magn_y - COURANT * curl_y
    magn_z = magn_z - COURANT * curl_z
    rim_west = passed_along(jnp.stack([magn_y[-1:], magn_z[-1:]]), "gx", 1)
    rim_south = passed_along(jnp.stack([magn_x[:, -1:], magn_z[:, -1:]]), "gy", 1)
    curl_x = minus_diff(magn_z, rim_south[1], 1) - minus_diff(magn_y, z_blank, 2)
    curl_y = minus_diff(magn_x, z_blank, 2) - minus_diff(magn_z, rim_west[1], 0)
    curl_z = minus_diff(magn_y, rim_west[0], 0) - minus_diff(magn_x, rim_south[0], 1)
    elec_x = elec_x + COURANT * (curl_x - sources[0]) * inv_eps
    elec_y = elec_y + COURANT * (curl_y - sources[1]) * inv_eps
    elec_z = elec_z + COURANT * curl_z * inv_eps
    return (elec_x, elec_y, elec_z, magn_x, magn_y, magn_z)


def run_leaps(e_start, h_start, inv_eps, drive, tag):
    span_x = lax.axis_size("gx")
    span_y = lax.axis_size("gy")
    size_x, size_y, size_z = inv_eps.shape
    zero_start = e_start is None
    with_drive = drive is not None
    mesh_id = pl.DeviceIdType.MESH

    def kernel(*refs):
        refs = list(refs)
        if zero_start:
            e_in = h_in = None
        else:
            e_in, h_in = refs.pop(0), refs.pop(0)
        eps_ref = refs.pop(0)
        drv = refs.pop(0) if with_drive else None
        e_out, h_out, east, north, west, south, xs_e, ys_e, xs_h, ys_h, ssem, rsem = refs
        px = lax.axis_index("gx")
        py = lax.axis_index("gy")
        barrier = pltpu.get_barrier_semaphore()
        for peer in (
            (lax.rem(px + 1, span_x), py),
            (lax.rem(px + span_x - 1, span_x), py),
            (px, lax.rem(py + 1, span_y)),
            (px, lax.rem(py + span_y - 1, span_y)),
        ):
            pl.semaphore_signal(barrier, 1, device_id=peer, device_id_type=mesh_id)
        pl.semaphore_wait(barrier, 4)
        has_east = px < span_x - 1
        has_west = px > 0
        has_north = py < span_y - 1
        has_south = py > 0
        zero_slab = jnp.zeros((size_y, size_z), jnp.float32)
        iy = lax.broadcasted_iota(jnp.int32, (size_y, size_z), 0)
        iz = lax.broadcasted_iota(jnp.int32, (size_y, size_z), 1)

        def up_y(slab, row):
            return jnp.where(iy == size_y - 1, row, pltpu.roll(slab, size_y - 1, 0))

        def down_y(slab, row):
            return jnp.where(iy == 0, row, pltpu.roll(slab, 1, 0))

        def up_z(slab):
            return jnp.where(iz == size_z - 1, 0.0, pltpu.roll(slab, size_z - 1, 1))

        def down_z(slab):
            return jnp.where(iz == 0, 0.0, pltpu.roll(slab, 1, 1))

        def load_e(step, comp, x):
            if step == 0:
                return zero_slab if zero_start else e_in[comp, x]
            return e_out[step - 1, comp, x]

        def load_h(step, comp, x):
            if step == 0:
                return zero_slab if zero_start else h_in[comp, x]
            return h_out[comp, x]

        def swap(src_x, dst_x, src_y, dst_y, sem, to_x, to_y, sends_x, sends_y, gets_x, gets_y):
            copy_x = pltpu.make_async_remote_copy(
                src_ref=src_x, dst_ref=dst_x, send_sem=ssem.at[sem], recv_sem=rsem.at[sem],
                device_id=(to_x, py), device_id_type=mesh_id,
            )
            copy_y = pltpu.make_async_remote_copy(
                src_ref=src_y, dst_ref=dst_y, send_sem=ssem.at[sem + 1], recv_sem=rsem.at[sem + 1],
                device_id=(px, to_y), device_id_type=mesh_id,
            )
            pl.when(sends_x)(copy_x.start)
            pl.when(sends_y)(copy_y.start)

            @pl.when(jnp.logical_not(gets_x))
            def _():
                dst_x[...] = jnp.zeros(dst_x.shape, jnp.float32)

            @pl.when(jnp.logical_not(gets_y))
            def _():
                dst_y[...] = jnp.zeros(dst_y.shape, jnp.float32)

            pl.when(gets_x)(copy_x.wait_recv)
            pl.when(gets_y)(copy_y.wait_recv)
            pl.when(sends_x)(copy_x.wait_send)
            pl.when(sends_y)(copy_y.wait_send)

        if not zero_start:
            xs_e[0, 0] = e_in[1, 0]
            xs_e[0, 1] = e_in[2, 0]

            def stage_first(x, carry):
                ys_e[0, 0, pl.ds(x, 1), :] = e_in[0, x][0:1, :]
                ys_e[0, 1, pl.ds(x, 1), :] = e_in[2, x][0:1, :]
                return carry

            lax.fori_loop(0, size_x, stage_first, 0)

        for step in range(NT):
            if step == 0 and zero_start:
                east[0] = jnp.zeros(east.shape[1:], jnp.float32)
                north[0] = jnp.zeros(north.shape[1:], jnp.float32)
            else:
                swap(
                    xs_e.at[step], east.at[step], ys_e.at[step], north.at[step], 4 * step,
                    lax.rem(px + span_x - 1, span_x), lax.rem(py + span_y - 1, span_y),
                    has_west, has_south, has_east, has_north,
                )

            def magnetic(x, ey_next, ez_next, step=step):
                ex = load_e(step, 0, x)
                ey = load_e(step, 1, x)
                ez = load_e(step, 2, x)
                nx_row = north[step, 0, pl.ds(x, 1), :]
                nz_row = north[step, 1, pl.ds(x, 1), :]
                curl_x = (up_y(ez, nz_row) - ez) - (up_z(ey) - ey)
                curl_y = (up_z(ex) - ex) - (ez_next - ez)
                curl_z = (ey_next - ey) - (up_y(ex, nx_row) - ex)
                hx = load_h(step, 0, x) - COURANT * curl_x
                hy = load_h(step, 1, x) - COURANT * curl_y
                hz = load_h(step, 2, x) - COURANT * curl_z
                h_out[0, x] = hx
                h_out[1, x] = hy
                h_out[2, x] = hz
                ys_h[step, 0, pl.ds(x, 1), :] = hx[size_y - 1 : size_y, :]
                ys_h[step, 1, pl.ds(x, 1), :] = hz[size_y - 1 : size_y, :]
                return hy, hz

            def magnetic_body(x, carry, step=step):
                magnetic(x, load_e(step, 1, x + 1), load_e(step, 2, x + 1))
                return carry

            lax.fori_loop(0, size_x - 1, magnetic_body, 0)
            hy_last, hz_last = magnetic(size_x - 1, east[step, 0], east[step, 1])
            xs_h[step, 0] = hy_last
            xs_h[step, 1] = hz_last
            swap(
                xs_h.at[step], west.at[step], ys_h.at[step], south.at[step], 4 * step + 2,
                lax.rem(px + 1, span_x), lax.rem(py + 1, span_y),
                has_east, has_north, has_west, has_south,
            )

            def electric(x, hy_prev, hz_prev, step=step):
                hx = h_out[0, x]
                hy = h_out[1, x]
                hz = h_out[2, x]
                sx_row = south[step, 0, pl.ds(x, 1), :]
                sz_row = south[step, 1, pl.ds(x, 1), :]
                curl_x = (hz - down_y(hz, sz_row)) - (hy - down_z(hy))
                curl_y = (hx - down_z(hx)) - (hz - hz_prev)
                curl_z = (hy - hy_prev) - (hx - down_y(hx, sx_row))
                if with_drive:
                    curl_x = curl_x - drv[step, 0, x]
                    curl_y = curl_y - drv[step, 1, x]
                scale = eps_ref[x]
                ex = load_e(step, 0, x) + COURANT * curl_x * scale
                ey = load_e(step, 1, x) + COURANT * curl_y * scale
                ez = load_e(step, 2, x) + COURANT * curl_z * scale
                e_out[step, 0, x] = ex
                e_out[step, 1, x] = ey
                e_out[step, 2, x] = ez
                if step + 1 < NT:
                    ys_e[step + 1, 0, pl.ds(x, 1), :] = ex[0:1, :]
                    ys_e[step + 1, 1, pl.ds(x, 1), :] = ez[0:1, :]
                return ey, ez

            ey_first, ez_first = electric(0, west[step, 0], west[step, 1])
            if step + 1 < NT:
                xs_e[step + 1, 0] = ey_first
                xs_e[step + 1, 1] = ez_first

            def electric_body(x, carry, step=step):
                electric(x, h_out[1, x - 1], h_out[2, x - 1])
                return carry

            lax.fori_loop(1, size_x, electric_body, 0)

    rim_x = pltpu.VMEM((NT, 2, size_y, size_z), jnp.float32)
    rim_y = pltpu.VMEM((NT, 2, size_x, size_z), jnp.float32)
    operands = ([] if zero_start else [e_start, h_start]) + [inv_eps] + ([drive] if with_drive else [])
    return pl.pallas_call(
        kernel,
        out_shape=(
            jax.ShapeDtypeStruct((NT, 3, size_x, size_y, size_z), jnp.float32),
            jax.ShapeDtypeStruct((3, size_x, size_y, size_z), jnp.float32),
        ),
        in_specs=[pl.BlockSpec(memory_space=pltpu.VMEM)] * len(operands),
        out_specs=(pl.BlockSpec(memory_space=pltpu.VMEM),) * 2,
        scratch_shapes=[
            rim_x, rim_y, rim_x, rim_y, rim_x, rim_y, rim_x, rim_y,
            pltpu.SemaphoreType.DMA((4 * NT,)),
            pltpu.SemaphoreType.DMA((4 * NT,)),
        ],
        compiler_params=pltpu.CompilerParams(
            collective_id=tag, has_side_effects=True, vmem_limit_bytes=48 * 1024 * 1024
        ),
    )(*operands)


def group_of(axes):
    sizes = [lax.axis_size(a) for a in axes]
    count = math.prod(sizes)
    return count, sizes


def group_place(axes, sizes):
    place = 0
    for axis, size in zip(axes, sizes):
        place = place * size + lax.axis_index(axis)
    return place


def group_device(axes, sizes, peer):
    coords = {}
    rest = peer
    for axis, size in reversed(list(zip(axes, sizes))):
        coords[axis] = rest % size
        rest = rest // size
    return tuple(coords[a] if a in coords else lax.axis_index(a) for a in ("gx", "gy"))


def exchange(pieces, axes, gather, tag):
    count, sizes = group_of(axes)
    piece_shape = pieces.shape if gather else pieces.shape[1:]

    def kernel(x_ref, o_ref, send_sem, recv_sem):
        me = group_place(axes, sizes)
        barrier = pltpu.get_barrier_semaphore()
        for step in range(1, count):
            peer = lax.rem(me + step, count)
            pl.semaphore_signal(
                barrier, 1, device_id=group_device(axes, sizes, peer),
                device_id_type=pl.DeviceIdType.MESH,
            )
        pl.semaphore_wait(barrier, count - 1)
        copies = []
        for step in range(1, count):
            peer = lax.rem(me + step, count)
            copy = pltpu.make_async_remote_copy(
                src_ref=x_ref if gather else x_ref.at[peer],
                dst_ref=o_ref.at[me],
                send_sem=send_sem.at[step],
                recv_sem=recv_sem.at[step],
                device_id=group_device(axes, sizes, peer),
                device_id_type=pl.DeviceIdType.MESH,
            )
            copy.start()
            copies.append(copy)
        own = x_ref[...] if gather else x_ref[me]
        o_ref[me] = own
        for copy in copies:
            copy.wait_send()
        for step in range(1, count):
            source = lax.rem(me + count - step, count)
            pltpu.make_async_remote_copy(
                src_ref=x_ref if gather else x_ref.at[source],
                dst_ref=o_ref.at[source],
                send_sem=send_sem.at[step],
                recv_sem=recv_sem.at[step],
                device_id=group_device(axes, sizes, source),
                device_id_type=pl.DeviceIdType.MESH,
            ).wait_recv()

    return pl.pallas_call(
        kernel,
        out_shape=jax.ShapeDtypeStruct((count,) + tuple(piece_shape), pieces.dtype),
        in_specs=[pl.BlockSpec(memory_space=pltpu.VMEM)],
        out_specs=pl.BlockSpec(memory_space=pltpu.VMEM),
        scratch_shapes=[pltpu.SemaphoreType.DMA((count,)), pltpu.SemaphoreType.DMA((count,))],
        compiler_params=pltpu.CompilerParams(collective_id=tag, has_side_effects=True),
    )(pieces)


def kernel_table(count_out, count_in, offset, length):
    focal_pos = (jnp.arange(count_out, dtype=jnp.float32) + 0.5) / count_out - 0.5
    cell_pos = (
        offset.astype(jnp.float32) + jnp.arange(length, dtype=jnp.float32) + 0.5
    ) / count_in - 0.5
    phase = math.pi * count_out * (focal_pos[:, None] - cell_pos[None, :]) ** 2
    return (jnp.cos(phase), jnp.sin(phase))


def contract(pattern, first_op, second_op):
    return jnp.einsum(pattern, first_op, second_op, precision=lax.Precision.HIGHEST)


def route_pillars(rows, slot_ids, devices, capacity):
    slots = devices * capacity
    placing = (slot_ids[:, None] == jnp.arange(slots, dtype=jnp.int32)[None, :]).astype(
        jnp.float32
    )
    packed = contract("ps,pk->sk", placing, rows)
    got = exchange(packed.reshape(devices, capacity, rows.shape[1]), ("gx", "gy"), False, 0)
    return placing, got.reshape(slots, rows.shape[1])


def shards(fields, eps_background, target, widths, intersection, pillar_tile, anchors):
    span_x = lax.axis_size("gx")
    span_y = lax.axis_size("gy")
    devices = span_x * span_y
    place_x = lax.axis_index("gx")
    place_y = lax.axis_index("gy")
    linear = place_x * span_y + place_y
    offsets = jnp.arange(16, dtype=jnp.int32)
    capacity = 2 * max(1, P_DEV // devices)
    target_tile = pillar_tile[:, 0]
    onehot = (target_tile[:, None] == jnp.arange(devices, dtype=jnp.int32)[None, :]).astype(
        jnp.int32
    )
    earlier = jnp.cumsum(onehot, axis=0) - onehot
    order_in = jnp.sum(earlier * onehot, axis=1)
    slot_ids = target_tile * capacity + order_in
    rows = jnp.concatenate(
        [intersection * widths[:, None], anchors.astype(jnp.float32)], axis=1
    )
    placing, got = route_pillars(rows, slot_ids, devices, capacity)
    local_vals = got[:, :16]
    local_at = got[:, 16:18].astype(jnp.int32)
    cells_x = (local_at[:, 0:1] + (offsets // 4)[None, :]).reshape(-1)
    cells_y = (local_at[:, 1:2] + (offsets % 4)[None, :]).reshape(-1)
    lanes = jnp.arange(TILE, dtype=jnp.int32)
    pick_x = (cells_x[:, None] == lanes[None, :]).astype(jnp.float32)
    pick_y = (cells_y[:, None] == lanes[None, :]).astype(jnp.float32)
    filling = contract("sx,sy->xy", pick_x, pick_y * local_vals.reshape(-1)[:, None])
    z_index = jnp.arange(fields.shape[3], dtype=jnp.int32)
    layers = ((z_index >= ZM - ZP) & (z_index < ZM)).astype(jnp.float32)
    permittivity = eps_background + DELTA_EPS * filling[:, :, None] * layers[None, None, :]
    inv_eps = 1.0 / permittivity
    fields_now = tuple((fields[component] for component in range(6)))
    e_steps, h_last = run_leaps(fields[:3], fields[3:], inv_eps, None, 10)
    mon_re = jnp.zeros((2, TILE, TILE), jnp.float32)
    mon_im = jnp.zeros((2, TILE, TILE), jnp.float32)
    changes = []
    before = fields[:3]
    for moment in range(1, NT + 1):
        after = e_steps[moment - 1]
        monitor = after[0:2, :, :, ZM]
        mon_re = mon_re + math.cos(ANGULAR_STEP * moment) * monitor
        mon_im = mon_im - math.sin(ANGULAR_STEP * moment) * monitor
        changes.append((after - before)[:, :, :, ZM - ZP : ZM])
        before = after
    norm_scale = (TILE * span_x * TILE * span_y) ** (-0.5)
    x_re, x_im = kernel_table(U, TILE * span_x, place_x * TILE, TILE)
    y_re, y_im = kernel_table(V, TILE * span_y, place_y * TILE, TILE)
    part = jnp.stack(
        [
            contract("ux,cxy->ucy", x_re, mon_re) - contract("ux,cxy->ucy", x_im, mon_im),
            contract("ux,cxy->ucy", x_re, mon_im) + contract("ux,cxy->ucy", x_im, mon_re),
        ]
    )
    chunk_u = U // span_x
    part = part.reshape(2, span_x, chunk_u, 2, TILE).transpose(1, 2, 0, 3, 4)
    part = exchange(part.reshape(span_x, chunk_u, 4 * TILE), ("gx",), False, 1)
    part = jnp.sum(part, axis=0).reshape(chunk_u, 2, 2, TILE)
    part_re, part_im = part[:, 0], part[:, 1]
    far = jnp.stack(
        [
            contract("ucy,vy->cuv", part_re, y_re) - contract("ucy,vy->cuv", part_im, y_im),
            contract("ucy,vy->cuv", part_re, y_im) + contract("ucy,vy->cuv", part_im, y_re),
        ],
        axis=2,
    )
    row_count = U // devices
    far = far.reshape(2, span_y, row_count, 2, V).transpose(1, 0, 2, 3, 4)
    far = exchange(far.reshape(span_y, 2 * row_count * 2, V), ("gy",), False, 2)
    far = norm_scale * jnp.sum(far, axis=0).reshape(2, row_count, 2, V)
    focal_power = jnp.sum(far * far, axis=(0, 2))
    mine_target = lax.dynamic_slice_in_dim(target, linear * row_count, row_count, 0)
    weighted = jnp.stack(
        [mine_target * far[:, :, 0], -(mine_target * far[:, :, 1])], axis=2
    )
    weighted = exchange(weighted.reshape(2 * row_count * 2, V), ("gy",), True, 3)
    weighted = weighted.reshape(span_y, 2, row_count, 2, V).transpose(1, 0, 2, 3, 4)
    weighted = weighted.reshape(2, span_y * row_count, 2, V)
    w_re, w_im = weighted[:, :, 0], weighted[:, :, 1]
    half = jnp.stack(
        [
            contract("cuv,vy->cuy", w_re, y_re) - contract("cuv,vy->cuy", w_im, y_im),
            contract("cuv,vy->cuy", w_re, y_im) + contract("cuv,vy->cuy", w_im, y_re),
        ]
    )
    half = half.transpose(2, 0, 1, 3).reshape(chunk_u, 4 * TILE)
    half = exchange(half, ("gx",), True, 4)
    half = half.reshape(span_x * chunk_u, 2, 2, TILE).transpose(1, 2, 0, 3)
    half_re, half_im = half[0], half[1]
    back_re = 2.0 * norm_scale * (
        contract("ux,cuy->cxy", x_re, half_re) - contract("ux,cuy->cxy", x_im, half_im)
    )
    back_im = 2.0 * norm_scale * (
        contract("ux,cuy->cxy", x_re, half_im) + contract("ux,cuy->cxy", x_im, half_re)
    )
    inv_layer = inv_eps[:, :, ZM - ZP : ZM]
    drives = []
    for moment in range(1, NT + 1):
        source_step = NT + 1 - moment
        adj_drive = (
            math.cos(ANGULAR_STEP * source_step) * back_re
            + math.sin(ANGULAR_STEP * source_step) * back_im
        )
        drives.append(adj_drive)
    drive = jnp.stack(drives)
    z_index = jnp.arange(fields.shape[3], dtype=jnp.int32)
    drive = jnp.where(z_index == ZM, drive[..., None], 0.0)
    a_steps, _ = run_leaps(None, None, inv_eps, drive, 11)
    grad_eps = jnp.zeros((TILE, TILE, ZP), jnp.float32)
    for moment in range(1, NT + 1):
        source_step = NT + 1 - moment
        change = changes[source_step - 1]
        adjoint = a_steps[moment - 1][:, :, :, ZM - ZP : ZM]
        product = adjoint[0] * change[0] + adjoint[1] * change[1] + adjoint[2] * change[2]
        grad_eps = grad_eps - product * inv_layer
    column_grad = jnp.sum(grad_eps, axis=2)
    spread = contract("sx,xy->sy", pick_x, column_grad)
    picked = jnp.sum(spread * pick_y, axis=1).reshape(devices * capacity, 16)
    returned = exchange(picked.reshape(devices, capacity, 16), ("gx", "gy"), False, 5)
    own_vals = contract("ps,sk->pk", placing, returned.reshape(devices * capacity, 16))
    grad_widths = DELTA_EPS * jnp.sum(intersection * own_vals, axis=1)
    return (jnp.concatenate([e_steps[NT - 1], h_last]), focal_power, grad_widths)


def solution(mesh):
    placed = (
        P(None, "gx", "gy", None),
        P("gx", "gy", None),
        P(),
        P(("gx", "gy")),
        P(("gx", "gy"), None),
        P(("gx", "gy"), None),
        P(("gx", "gy"), None),
    )
    return jax.shard_map(
        shards,
        mesh=mesh,
        in_specs=placed,
        out_specs=(P(None, "gx", "gy", None), P(("gx", "gy"), None), P(("gx", "gy"))),
        check_vma=False,
    )
```

```python
import math

import jax
import jax.numpy as jnp
from jax import lax
from jax.sharding import PartitionSpec as P
from jax.experimental import pallas as pl
from jax.experimental.pallas import tpu as pltpu

TILE = 32
P_DEV = 128
NT = 4
ZP = 4
U = 256
V = 256
ZM = 64


COURANT = 0.5
ANGULAR_STEP = 0.9
DELTA_EPS = 4.0


def passed_along(shard, axis, by):
    count = lax.axis_size(axis)
    pairs = [(i, i + by) for i in range(count) if 0 <= i + by < count]
    return lax.ppermute(shard, axis, pairs)


def plus_diff(field, rim_layer, axis):
    extended = jnp.concatenate([field, rim_layer], axis=axis)
    return lax.slice_in_dim(extended, 1, extended.shape[axis], axis=axis) - field


def minus_diff(field, rim_layer, axis):
    extended = jnp.concatenate([rim_layer, field], axis=axis)
    return field - lax.slice_in_dim(extended, 0, field.shape[axis], axis=axis)


def leap_step(fields_now, inv_eps, sources):
    elec_x, elec_y, elec_z, magn_x, magn_y, magn_z = fields_now
    z_blank = jnp.zeros_like(elec_x[:, :, :1])
    rim_east = passed_along(jnp.stack([elec_y[:1], elec_z[:1]]), "gx", -1)
    rim_north = passed_along(jnp.stack([elec_x[:, :1], elec_z[:, :1]]), "gy", -1)
    curl_x = plus_diff(elec_z, rim_north[1], 1) - plus_diff(elec_y, z_blank, 2)
    curl_y = plus_diff(elec_x, z_blank, 2) - plus_diff(elec_z, rim_east[1], 0)
    curl_z = plus_diff(elec_y, rim_east[0], 0) - plus_diff(elec_x, rim_north[0], 1)
    magn_x = magn_x - COURANT * curl_x
    magn_y = magn_y - COURANT * curl_y
    magn_z = magn_z - COURANT * curl_z
    rim_west = passed_along(jnp.stack([magn_y[-1:], magn_z[-1:]]), "gx", 1)
    rim_south = passed_along(jnp.stack([magn_x[:, -1:], magn_z[:, -1:]]), "gy", 1)
    curl_x = minus_diff(magn_z, rim_south[1], 1) - minus_diff(magn_y, z_blank, 2)
    curl_y = minus_diff(magn_x, z_blank, 2) - minus_diff(magn_z, rim_west[1], 0)
    curl_z = minus_diff(magn_y, rim_west[0], 0) - minus_diff(magn_x, rim_south[0], 1)
    elec_x = elec_x + COURANT * (curl_x - sources[0]) * inv_eps
    elec_y = elec_y + COURANT * (curl_y - sources[1]) * inv_eps
    elec_z = elec_z + COURANT * curl_z * inv_eps
    return (elec_x, elec_y, elec_z, magn_x, magn_y, magn_z)


def run_leaps(e_start, h_start, inv_eps, drive, tag):
    span_x = lax.axis_size("gx")
    span_y = lax.axis_size("gy")
    size_x, size_y, size_z = inv_eps.shape
    zero_start = e_start is None
    with_drive = drive is not None
    mesh_id = pl.DeviceIdType.MESH

    def kernel(*refs):
        refs = list(refs)
        if zero_start:
            e_in = h_in = None
        else:
            e_in, h_in = refs.pop(0), refs.pop(0)
        eps_ref = refs.pop(0)
        drv = refs.pop(0) if with_drive else None
        e_out, h_out, east, north, west, south, xs_e, ys_e, xs_h, ys_h, ssem, rsem = refs
        px = lax.axis_index("gx")
        py = lax.axis_index("gy")
        barrier = pltpu.get_barrier_semaphore()
        for peer in (
            (lax.rem(px + 1, span_x), py),
            (lax.rem(px + span_x - 1, span_x), py),
            (px, lax.rem(py + 1, span_y)),
            (px, lax.rem(py + span_y - 1, span_y)),
        ):
            pl.semaphore_signal(barrier, 1, device_id=peer, device_id_type=mesh_id)
        pl.semaphore_wait(barrier, 4)
        has_east = px < span_x - 1
        has_west = px > 0
        has_north = py < span_y - 1
        has_south = py > 0
        zero_slab = jnp.zeros((size_y, size_z), jnp.float32)
        iy = lax.broadcasted_iota(jnp.int32, (size_y, size_z), 0)
        iz = lax.broadcasted_iota(jnp.int32, (size_y, size_z), 1)

        def up_y(slab, row):
            return jnp.where(iy == size_y - 1, row, pltpu.roll(slab, size_y - 1, 0))

        def down_y(slab, row):
            return jnp.where(iy == 0, row, pltpu.roll(slab, 1, 0))

        def up_z(slab):
            return jnp.where(iz == size_z - 1, 0.0, pltpu.roll(slab, size_z - 1, 1))

        def down_z(slab):
            return jnp.where(iz == 0, 0.0, pltpu.roll(slab, 1, 1))

        def load_e(step, comp, x):
            if step == 0:
                return zero_slab if zero_start else e_in[comp, x]
            return e_out[step - 1, comp, x]

        def load_h(step, comp, x):
            if step == 0:
                return zero_slab if zero_start else h_in[comp, x]
            return h_out[comp, x]

        def swap(src_x, dst_x, src_y, dst_y, sem, to_x, to_y, sends_x, sends_y, gets_x, gets_y):
            copy_x = pltpu.make_async_remote_copy(
                src_ref=src_x, dst_ref=dst_x, send_sem=ssem.at[sem], recv_sem=rsem.at[sem],
                device_id=(to_x, py), device_id_type=mesh_id,
            )
            copy_y = pltpu.make_async_remote_copy(
                src_ref=src_y, dst_ref=dst_y, send_sem=ssem.at[sem + 1], recv_sem=rsem.at[sem + 1],
                device_id=(px, to_y), device_id_type=mesh_id,
            )
            pl.when(sends_x)(copy_x.start)
            pl.when(sends_y)(copy_y.start)

            @pl.when(jnp.logical_not(gets_x))
            def _():
                dst_x[...] = jnp.zeros(dst_x.shape, jnp.float32)

            @pl.when(jnp.logical_not(gets_y))
            def _():
                dst_y[...] = jnp.zeros(dst_y.shape, jnp.float32)

            pl.when(gets_x)(copy_x.wait_recv)
            pl.when(gets_y)(copy_y.wait_recv)
            pl.when(sends_x)(copy_x.wait_send)
            pl.when(sends_y)(copy_y.wait_send)

        if not zero_start:
            xs_e[0, 0] = e_in[1, 0]
            xs_e[0, 1] = e_in[2, 0]

            def stage_first(x, carry):
                ys_e[0, 0, pl.ds(x, 1), :] = e_in[0, x][0:1, :]
                ys_e[0, 1, pl.ds(x, 1), :] = e_in[2, x][0:1, :]
                return carry

            lax.fori_loop(0, size_x, stage_first, 0)

        for step in range(NT):
            if step == 0 and zero_start:
                east[0] = jnp.zeros(east.shape[1:], jnp.float32)
                north[0] = jnp.zeros(north.shape[1:], jnp.float32)
            else:
                swap(
                    xs_e.at[step], east.at[step], ys_e.at[step], north.at[step], 4 * step,
                    lax.rem(px + span_x - 1, span_x), lax.rem(py + span_y - 1, span_y),
                    has_west, has_south, has_east, has_north,
                )

            def magnetic(x, ey_next, ez_next, step=step):
                ex = load_e(step, 0, x)
                ey = load_e(step, 1, x)
                ez = load_e(step, 2, x)
                nx_row = north[step, 0, pl.ds(x, 1), :]
                nz_row = north[step, 1, pl.ds(x, 1), :]
                curl_x = (up_y(ez, nz_row) - ez) - (up_z(ey) - ey)
                curl_y = (up_z(ex) - ex) - (ez_next - ez)
                curl_z = (ey_next - ey) - (up_y(ex, nx_row) - ex)
                hx = load_h(step, 0, x) - COURANT * curl_x
                hy = load_h(step, 1, x) - COURANT * curl_y
                hz = load_h(step, 2, x) - COURANT * curl_z
                h_out[0, x] = hx
                h_out[1, x] = hy
                h_out[2, x] = hz
                ys_h[step, 0, pl.ds(x, 1), :] = hx[size_y - 1 : size_y, :]
                ys_h[step, 1, pl.ds(x, 1), :] = hz[size_y - 1 : size_y, :]
                return hy, hz

            def magnetic_body(x, carry, step=step):
                magnetic(x, load_e(step, 1, x + 1), load_e(step, 2, x + 1))
                return carry

            lax.fori_loop(0, size_x - 1, magnetic_body, 0, unroll=True)
            hy_last, hz_last = magnetic(size_x - 1, east[step, 0], east[step, 1])
            xs_h[step, 0] = hy_last
            xs_h[step, 1] = hz_last
            swap(
                xs_h.at[step], west.at[step], ys_h.at[step], south.at[step], 4 * step + 2,
                lax.rem(px + 1, span_x), lax.rem(py + 1, span_y),
                has_east, has_north, has_west, has_south,
            )

            def electric(x, hy_prev, hz_prev, step=step):
                hx = h_out[0, x]
                hy = h_out[1, x]
                hz = h_out[2, x]
                sx_row = south[step, 0, pl.ds(x, 1), :]
                sz_row = south[step, 1, pl.ds(x, 1), :]
                curl_x = (hz - down_y(hz, sz_row)) - (hy - down_z(hy))
                curl_y = (hx - down_z(hx)) - (hz - hz_prev)
                curl_z = (hy - hy_prev) - (hx - down_y(hx, sx_row))
                if with_drive:
                    curl_x = curl_x - drv[step, 0, x]
                    curl_y = curl_y - drv[step, 1, x]
                scale = eps_ref[x]
                ex = load_e(step, 0, x) + COURANT * curl_x * scale
                ey = load_e(step, 1, x) + COURANT * curl_y * scale
                ez = load_e(step, 2, x) + COURANT * curl_z * scale
                e_out[step, 0, x] = ex
                e_out[step, 1, x] = ey
                e_out[step, 2, x] = ez
                if step + 1 < NT:
                    ys_e[step + 1, 0, pl.ds(x, 1), :] = ex[0:1, :]
                    ys_e[step + 1, 1, pl.ds(x, 1), :] = ez[0:1, :]
                return ey, ez

            ey_first, ez_first = electric(0, west[step, 0], west[step, 1])
            if step + 1 < NT:
                xs_e[step + 1, 0] = ey_first
                xs_e[step + 1, 1] = ez_first

            def electric_body(x, carry, step=step):
                electric(x, h_out[1, x - 1], h_out[2, x - 1])
                return carry

            lax.fori_loop(1, size_x, electric_body, 0, unroll=True)

    rim_x = pltpu.VMEM((NT, 2, size_y, size_z), jnp.float32)
    rim_y = pltpu.VMEM((NT, 2, size_x, size_z), jnp.float32)
    operands = ([] if zero_start else [e_start, h_start]) + [inv_eps] + ([drive] if with_drive else [])
    return pl.pallas_call(
        kernel,
        out_shape=(
            jax.ShapeDtypeStruct((NT, 3, size_x, size_y, size_z), jnp.float32),
            jax.ShapeDtypeStruct((3, size_x, size_y, size_z), jnp.float32),
        ),
        in_specs=[pl.BlockSpec(memory_space=pltpu.VMEM)] * len(operands),
        out_specs=(pl.BlockSpec(memory_space=pltpu.VMEM),) * 2,
        scratch_shapes=[
            rim_x, rim_y, rim_x, rim_y, rim_x, rim_y, rim_x, rim_y,
            pltpu.SemaphoreType.DMA((4 * NT,)),
            pltpu.SemaphoreType.DMA((4 * NT,)),
        ],
        compiler_params=pltpu.CompilerParams(
            collective_id=tag, has_side_effects=True, vmem_limit_bytes=48 * 1024 * 1024
        ),
    )(*operands)


def group_of(axes):
    sizes = [lax.axis_size(a) for a in axes]
    count = math.prod(sizes)
    return count, sizes


def group_place(axes, sizes):
    place = 0
    for axis, size in zip(axes, sizes):
        place = place * size + lax.axis_index(axis)
    return place


def group_device(axes, sizes, peer):
    coords = {}
    rest = peer
    for axis, size in reversed(list(zip(axes, sizes))):
        coords[axis] = rest % size
        rest = rest // size
    return tuple(coords[a] if a in coords else lax.axis_index(a) for a in ("gx", "gy"))


def exchange(pieces, axes, gather, tag):
    count, sizes = group_of(axes)
    piece_shape = pieces.shape if gather else pieces.shape[1:]

    def kernel(x_ref, o_ref, send_sem, recv_sem):
        me = group_place(axes, sizes)
        barrier = pltpu.get_barrier_semaphore()
        for step in range(1, count):
            peer = lax.rem(me + step, count)
            pl.semaphore_signal(
                barrier, 1, device_id=group_device(axes, sizes, peer),
                device_id_type=pl.DeviceIdType.MESH,
            )
        pl.semaphore_wait(barrier, count - 1)
        copies = []
        for step in range(1, count):
            peer = lax.rem(me + step, count)
            copy = pltpu.make_async_remote_copy(
                src_ref=x_ref if gather else x_ref.at[peer],
                dst_ref=o_ref.at[me],
                send_sem=send_sem.at[step],
                recv_sem=recv_sem.at[step],
                device_id=group_device(axes, sizes, peer),
                device_id_type=pl.DeviceIdType.MESH,
            )
            copy.start()
            copies.append(copy)
        own = x_ref[...] if gather else x_ref[me]
        o_ref[me] = own
        for copy in copies:
            copy.wait_send()
        for step in range(1, count):
            source = lax.rem(me + count - step, count)
            pltpu.make_async_remote_copy(
                src_ref=x_ref if gather else x_ref.at[source],
                dst_ref=o_ref.at[source],
                send_sem=send_sem.at[step],
                recv_sem=recv_sem.at[step],
                device_id=group_device(axes, sizes, source),
                device_id_type=pl.DeviceIdType.MESH,
            ).wait_recv()

    return pl.pallas_call(
        kernel,
        out_shape=jax.ShapeDtypeStruct((count,) + tuple(piece_shape), pieces.dtype),
        in_specs=[pl.BlockSpec(memory_space=pltpu.VMEM)],
        out_specs=pl.BlockSpec(memory_space=pltpu.VMEM),
        scratch_shapes=[pltpu.SemaphoreType.DMA((count,)), pltpu.SemaphoreType.DMA((count,))],
        compiler_params=pltpu.CompilerParams(collective_id=tag, has_side_effects=True),
    )(pieces)


def kernel_table(count_out, count_in, offset, length):
    focal_pos = (jnp.arange(count_out, dtype=jnp.float32) + 0.5) / count_out - 0.5
    cell_pos = (
        offset.astype(jnp.float32) + jnp.arange(length, dtype=jnp.float32) + 0.5
    ) / count_in - 0.5
    phase = math.pi * count_out * (focal_pos[:, None] - cell_pos[None, :]) ** 2
    return (jnp.cos(phase), jnp.sin(phase))


def contract(pattern, first_op, second_op):
    return jnp.einsum(pattern, first_op, second_op, precision=lax.Precision.HIGHEST)


def route_pillars(rows, slot_ids, devices, capacity):
    slots = devices * capacity
    placing = (slot_ids[:, None] == jnp.arange(slots, dtype=jnp.int32)[None, :]).astype(
        jnp.float32
    )
    packed = contract("ps,pk->sk", placing, rows)
    got = exchange(packed.reshape(devices, capacity, rows.shape[1]), ("gx", "gy"), False, 0)
    return placing, got.reshape(slots, rows.shape[1])


def shards(fields, eps_background, target, widths, intersection, pillar_tile, anchors):
    span_x = lax.axis_size("gx")
    span_y = lax.axis_size("gy")
    devices = span_x * span_y
    place_x = lax.axis_index("gx")
    place_y = lax.axis_index("gy")
    linear = place_x * span_y + place_y
    offsets = jnp.arange(16, dtype=jnp.int32)
    capacity = 2 * max(1, P_DEV // devices)
    target_tile = pillar_tile[:, 0]
    onehot = (target_tile[:, None] == jnp.arange(devices, dtype=jnp.int32)[None, :]).astype(
        jnp.int32
    )
    earlier = jnp.cumsum(onehot, axis=0) - onehot
    order_in = jnp.sum(earlier * onehot, axis=1)
    slot_ids = target_tile * capacity + order_in
    rows = jnp.concatenate(
        [intersection * widths[:, None], anchors.astype(jnp.float32)], axis=1
    )
    placing, got = route_pillars(rows, slot_ids, devices, capacity)
    local_vals = got[:, :16]
    local_at = got[:, 16:18].astype(jnp.int32)
    cells_x = (local_at[:, 0:1] + (offsets // 4)[None, :]).reshape(-1)
    cells_y = (local_at[:, 1:2] + (offsets % 4)[None, :]).reshape(-1)
    lanes = jnp.arange(TILE, dtype=jnp.int32)
    pick_x = (cells_x[:, None] == lanes[None, :]).astype(jnp.float32)
    pick_y = (cells_y[:, None] == lanes[None, :]).astype(jnp.float32)
    filling = contract("sx,sy->xy", pick_x, pick_y * local_vals.reshape(-1)[:, None])
    z_index = jnp.arange(fields.shape[3], dtype=jnp.int32)
    layers = ((z_index >= ZM - ZP) & (z_index < ZM)).astype(jnp.float32)
    permittivity = eps_background + DELTA_EPS * filling[:, :, None] * layers[None, None, :]
    inv_eps = 1.0 / permittivity
    fields_now = tuple((fields[component] for component in range(6)))
    e_steps, h_last = run_leaps(fields[:3], fields[3:], inv_eps, None, 10)
    mon_re = jnp.zeros((2, TILE, TILE), jnp.float32)
    mon_im = jnp.zeros((2, TILE, TILE), jnp.float32)
    changes = []
    before = fields[:3]
    for moment in range(1, NT + 1):
        after = e_steps[moment - 1]
        monitor = after[0:2, :, :, ZM]
        mon_re = mon_re + math.cos(ANGULAR_STEP * moment) * monitor
        mon_im = mon_im - math.sin(ANGULAR_STEP * moment) * monitor
        changes.append((after - before)[:, :, :, ZM - ZP : ZM])
        before = after
    norm_scale = (TILE * span_x * TILE * span_y) ** (-0.5)
    x_re, x_im = kernel_table(U, TILE * span_x, place_x * TILE, TILE)
    y_re, y_im = kernel_table(V, TILE * span_y, place_y * TILE, TILE)
    part = jnp.stack(
        [
            contract("ux,cxy->ucy", x_re, mon_re) - contract("ux,cxy->ucy", x_im, mon_im),
            contract("ux,cxy->ucy", x_re, mon_im) + contract("ux,cxy->ucy", x_im, mon_re),
        ]
    )
    chunk_u = U // span_x
    part = part.reshape(2, span_x, chunk_u, 2, TILE).transpose(1, 2, 0, 3, 4)
    part = exchange(part.reshape(span_x, chunk_u, 4 * TILE), ("gx",), False, 1)
    part = jnp.sum(part, axis=0).reshape(chunk_u, 2, 2, TILE)
    part_re, part_im = part[:, 0], part[:, 1]
    far = jnp.stack(
        [
            contract("ucy,vy->cuv", part_re, y_re) - contract("ucy,vy->cuv", part_im, y_im),
            contract("ucy,vy->cuv", part_re, y_im) + contract("ucy,vy->cuv", part_im, y_re),
        ],
        axis=2,
    )
    row_count = U // devices
    far = far.reshape(2, span_y, row_count, 2, V).transpose(1, 0, 2, 3, 4)
    far = exchange(far.reshape(span_y, 2 * row_count * 2, V), ("gy",), False, 2)
    far = norm_scale * jnp.sum(far, axis=0).reshape(2, row_count, 2, V)
    focal_power = jnp.sum(far * far, axis=(0, 2))
    mine_target = lax.dynamic_slice_in_dim(target, linear * row_count, row_count, 0)
    weighted = jnp.stack(
        [mine_target * far[:, :, 0], -(mine_target * far[:, :, 1])], axis=2
    )
    weighted = exchange(weighted.reshape(2 * row_count * 2, V), ("gy",), True, 3)
    weighted = weighted.reshape(span_y, 2, row_count, 2, V).transpose(1, 0, 2, 3, 4)
    weighted = weighted.reshape(2, span_y * row_count, 2, V)
    w_re, w_im = weighted[:, :, 0], weighted[:, :, 1]
    half = jnp.stack(
        [
            contract("cuv,vy->cuy", w_re, y_re) - contract("cuv,vy->cuy", w_im, y_im),
            contract("cuv,vy->cuy", w_re, y_im) + contract("cuv,vy->cuy", w_im, y_re),
        ]
    )
    half = half.transpose(2, 0, 1, 3).reshape(chunk_u, 4 * TILE)
    half = exchange(half, ("gx",), True, 4)
    half = half.reshape(span_x * chunk_u, 2, 2, TILE).transpose(1, 2, 0, 3)
    half_re, half_im = half[0], half[1]
    back_re = 2.0 * norm_scale * (
        contract("ux,cuy->cxy", x_re, half_re) - contract("ux,cuy->cxy", x_im, half_im)
    )
    back_im = 2.0 * norm_scale * (
        contract("ux,cuy->cxy", x_re, half_im) + contract("ux,cuy->cxy", x_im, half_re)
    )
    inv_layer = inv_eps[:, :, ZM - ZP : ZM]
    drives = []
    for moment in range(1, NT + 1):
        source_step = NT + 1 - moment
        adj_drive = (
            math.cos(ANGULAR_STEP * source_step) * back_re
            + math.sin(ANGULAR_STEP * source_step) * back_im
        )
        drives.append(adj_drive)
    drive = jnp.stack(drives)
    z_index = jnp.arange(fields.shape[3], dtype=jnp.int32)
    drive = jnp.where(z_index == ZM, drive[..., None], 0.0)
    a_steps, _ = run_leaps(None, None, inv_eps, drive, 11)
    grad_eps = jnp.zeros((TILE, TILE, ZP), jnp.float32)
    for moment in range(1, NT + 1):
        source_step = NT + 1 - moment
        change = changes[source_step - 1]
        adjoint = a_steps[moment - 1][:, :, :, ZM - ZP : ZM]
        product = adjoint[0] * change[0] + adjoint[1] * change[1] + adjoint[2] * change[2]
        grad_eps = grad_eps - product * inv_layer
    column_grad = jnp.sum(grad_eps, axis=2)
    spread = contract("sx,xy->sy", pick_x, column_grad)
    picked = jnp.sum(spread * pick_y, axis=1).reshape(devices * capacity, 16)
    returned = exchange(picked.reshape(devices, capacity, 16), ("gx", "gy"), False, 5)
    own_vals = contract("ps,sk->pk", placing, returned.reshape(devices * capacity, 16))
    grad_widths = DELTA_EPS * jnp.sum(intersection * own_vals, axis=1)
    return (jnp.concatenate([e_steps[NT - 1], h_last]), focal_power, grad_widths)


def solution(mesh):
    placed = (
        P(None, "gx", "gy", None),
        P("gx", "gy", None),
        P(),
        P(("gx", "gy")),
        P(("gx", "gy"), None),
        P(("gx", "gy"), None),
        P(("gx", "gy"), None),
    )
    return jax.shard_map(
        shards,
        mesh=mesh,
        in_specs=placed,
        out_specs=(P(None, "gx", "gy", None), P(("gx", "gy"), None), P(("gx", "gy"))),
        check_vma=False,
    )
```

```python
import math

import jax
import jax.numpy as jnp
from jax import lax
from jax.sharding import PartitionSpec as P
from jax.experimental import pallas as pl
from jax.experimental.pallas import tpu as pltpu

TILE = 32
P_DEV = 128
NT = 4
ZP = 4
U = 256
V = 256
ZM = 64


COURANT = 0.5
ANGULAR_STEP = 0.9
DELTA_EPS = 4.0


def passed_along(shard, axis, by):
    count = lax.axis_size(axis)
    pairs = [(i, i + by) for i in range(count) if 0 <= i + by < count]
    return lax.ppermute(shard, axis, pairs)


def plus_diff(field, rim_layer, axis):
    extended = jnp.concatenate([field, rim_layer], axis=axis)
    return lax.slice_in_dim(extended, 1, extended.shape[axis], axis=axis) - field


def minus_diff(field, rim_layer, axis):
    extended = jnp.concatenate([rim_layer, field], axis=axis)
    return field - lax.slice_in_dim(extended, 0, field.shape[axis], axis=axis)


def leap_step(fields_now, inv_eps, sources):
    elec_x, elec_y, elec_z, magn_x, magn_y, magn_z = fields_now
    z_blank = jnp.zeros_like(elec_x[:, :, :1])
    rim_east = passed_along(jnp.stack([elec_y[:1], elec_z[:1]]), "gx", -1)
    rim_north = passed_along(jnp.stack([elec_x[:, :1], elec_z[:, :1]]), "gy", -1)
    curl_x = plus_diff(elec_z, rim_north[1], 1) - plus_diff(elec_y, z_blank, 2)
    curl_y = plus_diff(elec_x, z_blank, 2) - plus_diff(elec_z, rim_east[1], 0)
    curl_z = plus_diff(elec_y, rim_east[0], 0) - plus_diff(elec_x, rim_north[0], 1)
    magn_x = magn_x - COURANT * curl_x
    magn_y = magn_y - COURANT * curl_y
    magn_z = magn_z - COURANT * curl_z
    rim_west = passed_along(jnp.stack([magn_y[-1:], magn_z[-1:]]), "gx", 1)
    rim_south = passed_along(jnp.stack([magn_x[:, -1:], magn_z[:, -1:]]), "gy", 1)
    curl_x = minus_diff(magn_z, rim_south[1], 1) - minus_diff(magn_y, z_blank, 2)
    curl_y = minus_diff(magn_x, z_blank, 2) - minus_diff(magn_z, rim_west[1], 0)
    curl_z = minus_diff(magn_y, rim_west[0], 0) - minus_diff(magn_x, rim_south[0], 1)
    elec_x = elec_x + COURANT * (curl_x - sources[0]) * inv_eps
    elec_y = elec_y + COURANT * (curl_y - sources[1]) * inv_eps
    elec_z = elec_z + COURANT * curl_z * inv_eps
    return (elec_x, elec_y, elec_z, magn_x, magn_y, magn_z)


def run_leaps(e_start, h_start, inv_eps, drive, tag):
    span_x = lax.axis_size("gx")
    span_y = lax.axis_size("gy")
    size_x, size_y, size_z = inv_eps.shape
    zero_start = e_start is None
    with_drive = drive is not None
    mesh_id = pl.DeviceIdType.MESH

    def kernel(*refs):
        refs = list(refs)
        if zero_start:
            e_in = h_in = None
        else:
            e_in, h_in = refs.pop(0), refs.pop(0)
        eps_ref = refs.pop(0)
        drv = refs.pop(0) if with_drive else None
        e_out, h_out, east, north, west, south, xs_e, ys_e, xs_h, ys_h, ssem, rsem = refs
        px = lax.axis_index("gx")
        py = lax.axis_index("gy")
        barrier = pltpu.get_barrier_semaphore()
        for peer in (
            (lax.rem(px + 1, span_x), py),
            (lax.rem(px + span_x - 1, span_x), py),
            (px, lax.rem(py + 1, span_y)),
            (px, lax.rem(py + span_y - 1, span_y)),
        ):
            pl.semaphore_signal(barrier, 1, device_id=peer, device_id_type=mesh_id)
        pl.semaphore_wait(barrier, 4)
        has_east = px < span_x - 1
        has_west = px > 0
        has_north = py < span_y - 1
        has_south = py > 0
        zero_slab = jnp.zeros((size_y, size_z), jnp.float32)
        iy = lax.broadcasted_iota(jnp.int32, (size_y, size_z), 0)
        iz = lax.broadcasted_iota(jnp.int32, (size_y, size_z), 1)

        def up_y(slab, row):
            return jnp.where(iy == size_y - 1, row, pltpu.roll(slab, size_y - 1, 0))

        def down_y(slab, row):
            return jnp.where(iy == 0, row, pltpu.roll(slab, 1, 0))

        def up_z(slab):
            return jnp.where(iz == size_z - 1, 0.0, pltpu.roll(slab, size_z - 1, 1))

        def down_z(slab):
            return jnp.where(iz == 0, 0.0, pltpu.roll(slab, 1, 1))

        def load_e(step, comp, x):
            if step == 0:
                return zero_slab if zero_start else e_in[comp, x]
            return e_out[step - 1, comp, x]

        def load_h(step, comp, x):
            if step == 0:
                return zero_slab if zero_start else h_in[comp, x]
            return h_out[comp, x]

        def swap(src_x, dst_x, src_y, dst_y, sem, to_x, to_y, sends_x, sends_y, gets_x, gets_y):
            copy_x = pltpu.make_async_remote_copy(
                src_ref=src_x, dst_ref=dst_x, send_sem=ssem.at[sem], recv_sem=rsem.at[sem],
                device_id=(to_x, py), device_id_type=mesh_id,
            )
            copy_y = pltpu.make_async_remote_copy(
                src_ref=src_y, dst_ref=dst_y, send_sem=ssem.at[sem + 1], recv_sem=rsem.at[sem + 1],
                device_id=(px, to_y), device_id_type=mesh_id,
            )
            pl.when(sends_x)(copy_x.start)
            pl.when(sends_y)(copy_y.start)

            @pl.when(jnp.logical_not(gets_x))
            def _():
                dst_x[...] = jnp.zeros(dst_x.shape, jnp.float32)

            @pl.when(jnp.logical_not(gets_y))
            def _():
                dst_y[...] = jnp.zeros(dst_y.shape, jnp.float32)

            pl.when(gets_x)(copy_x.wait_recv)
            pl.when(gets_y)(copy_y.wait_recv)
            pl.when(sends_x)(copy_x.wait_send)
            pl.when(sends_y)(copy_y.wait_send)

        if not zero_start:
            xs_e[0, 0] = e_in[1, 0]
            xs_e[0, 1] = e_in[2, 0]

            def stage_first(x, carry):
                ys_e[0, 0, pl.ds(x, 1), :] = e_in[0, x][0:1, :]
                ys_e[0, 1, pl.ds(x, 1), :] = e_in[2, x][0:1, :]
                return carry

            lax.fori_loop(0, size_x, stage_first, 0)

        for step in range(NT):
            if step == 0 and zero_start:
                east[0] = jnp.zeros(east.shape[1:], jnp.float32)
                north[0] = jnp.zeros(north.shape[1:], jnp.float32)
            else:
                swap(
                    xs_e.at[step], east.at[step], ys_e.at[step], north.at[step], 4 * step,
                    lax.rem(px + span_x - 1, span_x), lax.rem(py + span_y - 1, span_y),
                    has_west, has_south, has_east, has_north,
                )

            def magnetic(x, ey_next, ez_next, step=step):
                ex = load_e(step, 0, x)
                ey = load_e(step, 1, x)
                ez = load_e(step, 2, x)
                nx_row = north[step, 0, pl.ds(x, 1), :]
                nz_row = north[step, 1, pl.ds(x, 1), :]
                curl_x = (up_y(ez, nz_row) - ez) - (up_z(ey) - ey)
                curl_y = (up_z(ex) - ex) - (ez_next - ez)
                curl_z = (ey_next - ey) - (up_y(ex, nx_row) - ex)
                hx = load_h(step, 0, x) - COURANT * curl_x
                hy = load_h(step, 1, x) - COURANT * curl_y
                hz = load_h(step, 2, x) - COURANT * curl_z
                h_out[0, x] = hx
                h_out[1, x] = hy
                h_out[2, x] = hz
                ys_h[step, 0, pl.ds(x, 1), :] = hx[size_y - 1 : size_y, :]
                ys_h[step, 1, pl.ds(x, 1), :] = hz[size_y - 1 : size_y, :]
                return hy, hz

            def magnetic_body(x, carry, step=step):
                magnetic(x, load_e(step, 1, x + 1), load_e(step, 2, x + 1))
                return carry

            lax.fori_loop(0, size_x - 1, magnetic_body, 0, unroll=True)
            hy_last, hz_last = magnetic(size_x - 1, east[step, 0], east[step, 1])
            xs_h[step, 0] = hy_last
            xs_h[step, 1] = hz_last
            swap(
                xs_h.at[step], west.at[step], ys_h.at[step], south.at[step], 4 * step + 2,
                lax.rem(px + 1, span_x), lax.rem(py + 1, span_y),
                has_east, has_north, has_west, has_south,
            )

            def electric(x, hy_prev, hz_prev, step=step):
                hx = h_out[0, x]
                hy = h_out[1, x]
                hz = h_out[2, x]
                sx_row = south[step, 0, pl.ds(x, 1), :]
                sz_row = south[step, 1, pl.ds(x, 1), :]
                curl_x = (hz - down_y(hz, sz_row)) - (hy - down_z(hy))
                curl_y = (hx - down_z(hx)) - (hz - hz_prev)
                curl_z = (hy - hy_prev) - (hx - down_y(hx, sx_row))
                if with_drive:
                    curl_x = curl_x - drv[step, 0, x]
                    curl_y = curl_y - drv[step, 1, x]
                scale = eps_ref[x]
                ex = load_e(step, 0, x) + COURANT * curl_x * scale
                ey = load_e(step, 1, x) + COURANT * curl_y * scale
                ez = load_e(step, 2, x) + COURANT * curl_z * scale
                e_out[step, 0, x] = ex
                e_out[step, 1, x] = ey
                e_out[step, 2, x] = ez
                if step + 1 < NT:
                    ys_e[step + 1, 0, pl.ds(x, 1), :] = ex[0:1, :]
                    ys_e[step + 1, 1, pl.ds(x, 1), :] = ez[0:1, :]
                return ey, ez

            ey_first, ez_first = electric(0, west[step, 0], west[step, 1])
            if step + 1 < NT:
                xs_e[step + 1, 0] = ey_first
                xs_e[step + 1, 1] = ez_first

            def electric_body(x, carry, step=step):
                electric(x, h_out[1, x - 1], h_out[2, x - 1])
                return carry

            lax.fori_loop(1, size_x, electric_body, 0, unroll=True)

    rim_x = pltpu.VMEM((NT, 2, size_y, size_z), jnp.float32)
    rim_y = pltpu.VMEM((NT, 2, size_x, size_z), jnp.float32)
    operands = ([] if zero_start else [e_start, h_start]) + [inv_eps] + ([drive] if with_drive else [])
    return pl.pallas_call(
        kernel,
        out_shape=(
            jax.ShapeDtypeStruct((NT, 3, size_x, size_y, size_z), jnp.float32),
            jax.ShapeDtypeStruct((3, size_x, size_y, size_z), jnp.float32),
        ),
        in_specs=[pl.BlockSpec(memory_space=pltpu.VMEM)] * len(operands),
        out_specs=(pl.BlockSpec(memory_space=pltpu.VMEM),) * 2,
        scratch_shapes=[
            rim_x, rim_y, rim_x, rim_y, rim_x, rim_y, rim_x, rim_y,
            pltpu.SemaphoreType.DMA((4 * NT,)),
            pltpu.SemaphoreType.DMA((4 * NT,)),
        ],
        compiler_params=pltpu.CompilerParams(
            collective_id=tag, has_side_effects=True, vmem_limit_bytes=48 * 1024 * 1024
        ),
    )(*operands)


def group_of(axes):
    sizes = [lax.axis_size(a) for a in axes]
    count = math.prod(sizes)
    return count, sizes


def group_place(axes, sizes):
    place = 0
    for axis, size in zip(axes, sizes):
        place = place * size + lax.axis_index(axis)
    return place


def group_device(axes, sizes, peer):
    coords = {}
    rest = peer
    for axis, size in reversed(list(zip(axes, sizes))):
        coords[axis] = rest % size
        rest = rest // size
    return tuple(coords[a] if a in coords else lax.axis_index(a) for a in ("gx", "gy"))


def exchange(pieces, axes, gather, tag):
    count, sizes = group_of(axes)
    piece_shape = pieces.shape if gather else pieces.shape[1:]

    def kernel(x_ref, o_ref, send_sem, recv_sem):
        me = group_place(axes, sizes)
        barrier = pltpu.get_barrier_semaphore()
        for step in range(1, count):
            peer = lax.rem(me + step, count)
            pl.semaphore_signal(
                barrier, 1, device_id=group_device(axes, sizes, peer),
                device_id_type=pl.DeviceIdType.MESH,
            )
        pl.semaphore_wait(barrier, count - 1)
        copies = []
        for step in range(1, count):
            peer = lax.rem(me + step, count)
            copy = pltpu.make_async_remote_copy(
                src_ref=x_ref if gather else x_ref.at[peer],
                dst_ref=o_ref.at[me],
                send_sem=send_sem.at[step],
                recv_sem=recv_sem.at[step],
                device_id=group_device(axes, sizes, peer),
                device_id_type=pl.DeviceIdType.MESH,
            )
            copy.start()
            copies.append(copy)
        own = x_ref[...] if gather else x_ref[me]
        o_ref[me] = own
        for copy in copies:
            copy.wait_send()
        for step in range(1, count):
            source = lax.rem(me + count - step, count)
            pltpu.make_async_remote_copy(
                src_ref=x_ref if gather else x_ref.at[source],
                dst_ref=o_ref.at[source],
                send_sem=send_sem.at[step],
                recv_sem=recv_sem.at[step],
                device_id=group_device(axes, sizes, source),
                device_id_type=pl.DeviceIdType.MESH,
            ).wait_recv()

    return pl.pallas_call(
        kernel,
        out_shape=jax.ShapeDtypeStruct((count,) + tuple(piece_shape), pieces.dtype),
        in_specs=[pl.BlockSpec(memory_space=pltpu.VMEM)],
        out_specs=pl.BlockSpec(memory_space=pltpu.VMEM),
        scratch_shapes=[pltpu.SemaphoreType.DMA((count,)), pltpu.SemaphoreType.DMA((count,))],
        compiler_params=pltpu.CompilerParams(collective_id=tag, has_side_effects=True),
    )(pieces)


def route_tiles(pieces, tags):
    span_x = lax.axis_size("gx")
    span_y = lax.axis_size("gy")
    tail = pieces.shape[1:]
    staged = pieces.reshape((span_x, span_y) + tail).swapaxes(0, 1)
    staged = exchange(staged, ("gy",), False, tags[0])
    staged = exchange(staged.swapaxes(0, 1), ("gx",), False, tags[1])
    return staged.reshape((span_x * span_y,) + tail)


def kernel_table(count_out, count_in, offset, length):
    focal_pos = (jnp.arange(count_out, dtype=jnp.float32) + 0.5) / count_out - 0.5
    cell_pos = (
        offset.astype(jnp.float32) + jnp.arange(length, dtype=jnp.float32) + 0.5
    ) / count_in - 0.5
    phase = math.pi * count_out * (focal_pos[:, None] - cell_pos[None, :]) ** 2
    return (jnp.cos(phase), jnp.sin(phase))


def contract(pattern, first_op, second_op):
    return jnp.einsum(pattern, first_op, second_op, precision=lax.Precision.HIGHEST)


def route_pillars(rows, slot_ids, devices, capacity):
    slots = devices * capacity
    placing = (slot_ids[:, None] == jnp.arange(slots, dtype=jnp.int32)[None, :]).astype(
        jnp.float32
    )
    packed = contract("ps,pk->sk", placing, rows)
    got = route_tiles(packed.reshape(devices, capacity, rows.shape[1]), (0, 6))
    return placing, got.reshape(slots, rows.shape[1])


def shards(fields, eps_background, target, widths, intersection, pillar_tile, anchors):
    span_x = lax.axis_size("gx")
    span_y = lax.axis_size("gy")
    devices = span_x * span_y
    place_x = lax.axis_index("gx")
    place_y = lax.axis_index("gy")
    linear = place_x * span_y + place_y
    offsets = jnp.arange(16, dtype=jnp.int32)
    capacity = 2 * max(1, P_DEV // devices)
    target_tile = pillar_tile[:, 0]
    onehot = (target_tile[:, None] == jnp.arange(devices, dtype=jnp.int32)[None, :]).astype(
        jnp.int32
    )
    earlier = jnp.cumsum(onehot, axis=0) - onehot
    order_in = jnp.sum(earlier * onehot, axis=1)
    slot_ids = target_tile * capacity + order_in
    rows = jnp.concatenate(
        [intersection * widths[:, None], anchors.astype(jnp.float32)], axis=1
    )
    placing, got = route_pillars(rows, slot_ids, devices, capacity)
    local_vals = got[:, :16]
    local_at = got[:, 16:18].astype(jnp.int32)
    cells_x = (local_at[:, 0:1] + (offsets // 4)[None, :]).reshape(-1)
    cells_y = (local_at[:, 1:2] + (offsets % 4)[None, :]).reshape(-1)
    lanes = jnp.arange(TILE, dtype=jnp.int32)
    pick_x = (cells_x[:, None] == lanes[None, :]).astype(jnp.float32)
    pick_y = (cells_y[:, None] == lanes[None, :]).astype(jnp.float32)
    filling = contract("sx,sy->xy", pick_x, pick_y * local_vals.reshape(-1)[:, None])
    z_index = jnp.arange(fields.shape[3], dtype=jnp.int32)
    layers = ((z_index >= ZM - ZP) & (z_index < ZM)).astype(jnp.float32)
    permittivity = eps_background + DELTA_EPS * filling[:, :, None] * layers[None, None, :]
    inv_eps = 1.0 / permittivity
    fields_now = tuple((fields[component] for component in range(6)))
    e_steps, h_last = run_leaps(fields[:3], fields[3:], inv_eps, None, 10)
    mon_re = jnp.zeros((2, TILE, TILE), jnp.float32)
    mon_im = jnp.zeros((2, TILE, TILE), jnp.float32)
    changes = []
    before = fields[:3]
    for moment in range(1, NT + 1):
        after = e_steps[moment - 1]
        monitor = after[0:2, :, :, ZM]
        mon_re = mon_re + math.cos(ANGULAR_STEP * moment) * monitor
        mon_im = mon_im - math.sin(ANGULAR_STEP * moment) * monitor
        changes.append((after - before)[:, :, :, ZM - ZP : ZM])
        before = after
    norm_scale = (TILE * span_x * TILE * span_y) ** (-0.5)
    x_re, x_im = kernel_table(U, TILE * span_x, place_x * TILE, TILE)
    y_re, y_im = kernel_table(V, TILE * span_y, place_y * TILE, TILE)
    part = jnp.stack(
        [
            contract("ux,cxy->ucy", x_re, mon_re) - contract("ux,cxy->ucy", x_im, mon_im),
            contract("ux,cxy->ucy", x_re, mon_im) + contract("ux,cxy->ucy", x_im, mon_re),
        ]
    )
    chunk_u = U // span_x
    part = part.reshape(2, span_x, chunk_u, 2, TILE).transpose(1, 2, 0, 3, 4)
    part = exchange(part.reshape(span_x, chunk_u, 4 * TILE), ("gx",), False, 1)
    part = jnp.sum(part, axis=0).reshape(chunk_u, 2, 2, TILE)
    part_re, part_im = part[:, 0], part[:, 1]
    far = jnp.stack(
        [
            contract("ucy,vy->cuv", part_re, y_re) - contract("ucy,vy->cuv", part_im, y_im),
            contract("ucy,vy->cuv", part_re, y_im) + contract("ucy,vy->cuv", part_im, y_re),
        ],
        axis=2,
    )
    row_count = U // devices
    far = far.reshape(2, span_y, row_count, 2, V).transpose(1, 0, 2, 3, 4)
    far = exchange(far.reshape(span_y, 2 * row_count * 2, V), ("gy",), False, 2)
    far = norm_scale * jnp.sum(far, axis=0).reshape(2, row_count, 2, V)
    focal_power = jnp.sum(far * far, axis=(0, 2))
    mine_target = lax.dynamic_slice_in_dim(target, linear * row_count, row_count, 0)
    weighted = jnp.stack(
        [mine_target * far[:, :, 0], -(mine_target * far[:, :, 1])], axis=2
    )
    weighted = exchange(weighted.reshape(2 * row_count * 2, V), ("gy",), True, 3)
    weighted = weighted.reshape(span_y, 2, row_count, 2, V).transpose(1, 0, 2, 3, 4)
    weighted = weighted.reshape(2, span_y * row_count, 2, V)
    w_re, w_im = weighted[:, :, 0], weighted[:, :, 1]
    half = jnp.stack(
        [
            contract("cuv,vy->cuy", w_re, y_re) - contract("cuv,vy->cuy", w_im, y_im),
            contract("cuv,vy->cuy", w_re, y_im) + contract("cuv,vy->cuy", w_im, y_re),
        ]
    )
    half = half.transpose(2, 0, 1, 3).reshape(chunk_u, 4 * TILE)
    half = exchange(half, ("gx",), True, 4)
    half = half.reshape(span_x * chunk_u, 2, 2, TILE).transpose(1, 2, 0, 3)
    half_re, half_im = half[0], half[1]
    back_re = 2.0 * norm_scale * (
        contract("ux,cuy->cxy", x_re, half_re) - contract("ux,cuy->cxy", x_im, half_im)
    )
    back_im = 2.0 * norm_scale * (
        contract("ux,cuy->cxy", x_re, half_im) + contract("ux,cuy->cxy", x_im, half_re)
    )
    inv_layer = inv_eps[:, :, ZM - ZP : ZM]
    drives = []
    for moment in range(1, NT + 1):
        source_step = NT + 1 - moment
        adj_drive = (
            math.cos(ANGULAR_STEP * source_step) * back_re
            + math.sin(ANGULAR_STEP * source_step) * back_im
        )
        drives.append(adj_drive)
    drive = jnp.stack(drives)
    z_index = jnp.arange(fields.shape[3], dtype=jnp.int32)
    drive = jnp.where(z_index == ZM, drive[..., None], 0.0)
    a_steps, _ = run_leaps(None, None, inv_eps, drive, 11)
    grad_eps = jnp.zeros((TILE, TILE, ZP), jnp.float32)
    for moment in range(1, NT + 1):
        source_step = NT + 1 - moment
        change = changes[source_step - 1]
        adjoint = a_steps[moment - 1][:, :, :, ZM - ZP : ZM]
        product = adjoint[0] * change[0] + adjoint[1] * change[1] + adjoint[2] * change[2]
        grad_eps = grad_eps - product * inv_layer
    column_grad = jnp.sum(grad_eps, axis=2)
    spread = contract("sx,xy->sy", pick_x, column_grad)
    picked = jnp.sum(spread * pick_y, axis=1).reshape(devices * capacity, 16)
    returned = route_tiles(picked.reshape(devices, capacity, 16), (5, 7))
    own_vals = contract("ps,sk->pk", placing, returned.reshape(devices * capacity, 16))
    grad_widths = DELTA_EPS * jnp.sum(intersection * own_vals, axis=1)
    return (jnp.concatenate([e_steps[NT - 1], h_last]), focal_power, grad_widths)


def solution(mesh):
    placed = (
        P(None, "gx", "gy", None),
        P("gx", "gy", None),
        P(),
        P(("gx", "gy")),
        P(("gx", "gy"), None),
        P(("gx", "gy"), None),
        P(("gx", "gy"), None),
    )
    return jax.shard_map(
        shards,
        mesh=mesh,
        in_specs=placed,
        out_specs=(P(None, "gx", "gy", None), P(("gx", "gy"), None), P(("gx", "gy"))),
        check_vma=False,
    )
```

```python
import math

import jax
import jax.numpy as jnp
from jax import lax
from jax.sharding import PartitionSpec as P
from jax.experimental import pallas as pl
from jax.experimental.pallas import tpu as pltpu

TILE = 32
P_DEV = 128
NT = 4
ZP = 4
U = 256
V = 256
ZM = 64


COURANT = 0.5
ANGULAR_STEP = 0.9
DELTA_EPS = 4.0


def passed_along(shard, axis, by):
    count = lax.axis_size(axis)
    pairs = [(i, i + by) for i in range(count) if 0 <= i + by < count]
    return lax.ppermute(shard, axis, pairs)


def plus_diff(field, rim_layer, axis):
    extended = jnp.concatenate([field, rim_layer], axis=axis)
    return lax.slice_in_dim(extended, 1, extended.shape[axis], axis=axis) - field


def minus_diff(field, rim_layer, axis):
    extended = jnp.concatenate([rim_layer, field], axis=axis)
    return field - lax.slice_in_dim(extended, 0, field.shape[axis], axis=axis)


def leap_step(fields_now, inv_eps, sources):
    elec_x, elec_y, elec_z, magn_x, magn_y, magn_z = fields_now
    z_blank = jnp.zeros_like(elec_x[:, :, :1])
    rim_east = passed_along(jnp.stack([elec_y[:1], elec_z[:1]]), "gx", -1)
    rim_north = passed_along(jnp.stack([elec_x[:, :1], elec_z[:, :1]]), "gy", -1)
    curl_x = plus_diff(elec_z, rim_north[1], 1) - plus_diff(elec_y, z_blank, 2)
    curl_y = plus_diff(elec_x, z_blank, 2) - plus_diff(elec_z, rim_east[1], 0)
    curl_z = plus_diff(elec_y, rim_east[0], 0) - plus_diff(elec_x, rim_north[0], 1)
    magn_x = magn_x - COURANT * curl_x
    magn_y = magn_y - COURANT * curl_y
    magn_z = magn_z - COURANT * curl_z
    rim_west = passed_along(jnp.stack([magn_y[-1:], magn_z[-1:]]), "gx", 1)
    rim_south = passed_along(jnp.stack([magn_x[:, -1:], magn_z[:, -1:]]), "gy", 1)
    curl_x = minus_diff(magn_z, rim_south[1], 1) - minus_diff(magn_y, z_blank, 2)
    curl_y = minus_diff(magn_x, z_blank, 2) - minus_diff(magn_z, rim_west[1], 0)
    curl_z = minus_diff(magn_y, rim_west[0], 0) - minus_diff(magn_x, rim_south[0], 1)
    elec_x = elec_x + COURANT * (curl_x - sources[0]) * inv_eps
    elec_y = elec_y + COURANT * (curl_y - sources[1]) * inv_eps
    elec_z = elec_z + COURANT * curl_z * inv_eps
    return (elec_x, elec_y, elec_z, magn_x, magn_y, magn_z)


def run_leaps(e_start, h_start, inv_eps, drive, tag):
    span_x = lax.axis_size("gx")
    span_y = lax.axis_size("gy")
    size_x, size_y, size_z = inv_eps.shape
    zero_start = e_start is None
    with_drive = drive is not None
    mesh_id = pl.DeviceIdType.MESH

    def kernel(*refs):
        refs = list(refs)
        if zero_start:
            e_in = h_in = None
        else:
            e_in, h_in = refs.pop(0), refs.pop(0)
        eps_ref = refs.pop(0)
        drv = refs.pop(0) if with_drive else None
        e_out, h_out, east, north, west, south, xs_e, ys_e, xs_h, ys_h, ssem, rsem = refs
        px = lax.axis_index("gx")
        py = lax.axis_index("gy")
        barrier = pltpu.get_barrier_semaphore()
        for peer in (
            (lax.rem(px + 1, span_x), py),
            (lax.rem(px + span_x - 1, span_x), py),
            (px, lax.rem(py + 1, span_y)),
            (px, lax.rem(py + span_y - 1, span_y)),
        ):
            pl.semaphore_signal(barrier, 1, device_id=peer, device_id_type=mesh_id)
        pl.semaphore_wait(barrier, 4)
        has_east = px < span_x - 1
        has_west = px > 0
        has_north = py < span_y - 1
        has_south = py > 0
        zero_slab = jnp.zeros((size_y, size_z), jnp.float32)
        iy = lax.broadcasted_iota(jnp.int32, (size_y, size_z), 0)
        iz = lax.broadcasted_iota(jnp.int32, (size_y, size_z), 1)

        def up_y(slab, row):
            return jnp.where(iy == size_y - 1, row, pltpu.roll(slab, size_y - 1, 0))

        def down_y(slab, row):
            return jnp.where(iy == 0, row, pltpu.roll(slab, 1, 0))

        def up_z(slab):
            return jnp.where(iz == size_z - 1, 0.0, pltpu.roll(slab, size_z - 1, 1))

        def down_z(slab):
            return jnp.where(iz == 0, 0.0, pltpu.roll(slab, 1, 1))

        def load_e(step, comp, x):
            if step == 0:
                return zero_slab if zero_start else e_in[comp, x]
            return e_out[step - 1, comp, x]

        def load_h(step, comp, x):
            if step == 0:
                return zero_slab if zero_start else h_in[comp, x]
            return h_out[comp, x]

        def swap(src_x, dst_x, src_y, dst_y, sem, to_x, to_y, sends_x, sends_y, gets_x, gets_y):
            copy_x = pltpu.make_async_remote_copy(
                src_ref=src_x, dst_ref=dst_x, send_sem=ssem.at[sem], recv_sem=rsem.at[sem],
                device_id=(to_x, py), device_id_type=mesh_id,
            )
            copy_y = pltpu.make_async_remote_copy(
                src_ref=src_y, dst_ref=dst_y, send_sem=ssem.at[sem + 1], recv_sem=rsem.at[sem + 1],
                device_id=(px, to_y), device_id_type=mesh_id,
            )
            pl.when(sends_x)(copy_x.start)
            pl.when(sends_y)(copy_y.start)

            @pl.when(jnp.logical_not(gets_x))
            def _():
                dst_x[...] = jnp.zeros(dst_x.shape, jnp.float32)

            @pl.when(jnp.logical_not(gets_y))
            def _():
                dst_y[...] = jnp.zeros(dst_y.shape, jnp.float32)

            pl.when(gets_x)(copy_x.wait_recv)
            pl.when(gets_y)(copy_y.wait_recv)
            pl.when(sends_x)(copy_x.wait_send)
            pl.when(sends_y)(copy_y.wait_send)

        if not zero_start:
            xs_e[0, 0] = e_in[1, 0]
            xs_e[0, 1] = e_in[2, 0]

            def stage_first(x, carry):
                ys_e[0, 0, pl.ds(x, 1), :] = e_in[0, x][0:1, :]
                ys_e[0, 1, pl.ds(x, 1), :] = e_in[2, x][0:1, :]
                return carry

            lax.fori_loop(0, size_x, stage_first, 0)

        for step in range(NT):
            if step == 0 and zero_start:
                east[0] = jnp.zeros(east.shape[1:], jnp.float32)
                north[0] = jnp.zeros(north.shape[1:], jnp.float32)
            else:
                swap(
                    xs_e.at[step], east.at[step], ys_e.at[step], north.at[step], 4 * step,
                    lax.rem(px + span_x - 1, span_x), lax.rem(py + span_y - 1, span_y),
                    has_west, has_south, has_east, has_north,
                )

            def magnetic(x, ey_next, ez_next, step=step):
                ex = load_e(step, 0, x)
                ey = load_e(step, 1, x)
                ez = load_e(step, 2, x)
                nx_row = north[step, 0, pl.ds(x, 1), :]
                nz_row = north[step, 1, pl.ds(x, 1), :]
                curl_x = (up_y(ez, nz_row) - ez) - (up_z(ey) - ey)
                curl_y = (up_z(ex) - ex) - (ez_next - ez)
                curl_z = (ey_next - ey) - (up_y(ex, nx_row) - ex)
                hx = load_h(step, 0, x) - COURANT * curl_x
                hy = load_h(step, 1, x) - COURANT * curl_y
                hz = load_h(step, 2, x) - COURANT * curl_z
                h_out[0, x] = hx
                h_out[1, x] = hy
                h_out[2, x] = hz
                ys_h[step, 0, pl.ds(x, 1), :] = hx[size_y - 1 : size_y, :]
                ys_h[step, 1, pl.ds(x, 1), :] = hz[size_y - 1 : size_y, :]
                return hy, hz

            def magnetic_body(x, carry, step=step):
                magnetic(x, load_e(step, 1, x + 1), load_e(step, 2, x + 1))
                return carry

            lax.fori_loop(0, size_x - 1, magnetic_body, 0, unroll=True)
            hy_last, hz_last = magnetic(size_x - 1, east[step, 0], east[step, 1])
            xs_h[step, 0] = hy_last
            xs_h[step, 1] = hz_last
            swap(
                xs_h.at[step], west.at[step], ys_h.at[step], south.at[step], 4 * step + 2,
                lax.rem(px + 1, span_x), lax.rem(py + 1, span_y),
                has_east, has_north, has_west, has_south,
            )

            def electric(x, hy_prev, hz_prev, step=step):
                hx = h_out[0, x]
                hy = h_out[1, x]
                hz = h_out[2, x]
                sx_row = south[step, 0, pl.ds(x, 1), :]
                sz_row = south[step, 1, pl.ds(x, 1), :]
                curl_x = (hz - down_y(hz, sz_row)) - (hy - down_z(hy))
                curl_y = (hx - down_z(hx)) - (hz - hz_prev)
                curl_z = (hy - hy_prev) - (hx - down_y(hx, sx_row))
                if with_drive:
                    curl_x = curl_x - drv[step, 0, x]
                    curl_y = curl_y - drv[step, 1, x]
                scale = eps_ref[x]
                ex = load_e(step, 0, x) + COURANT * curl_x * scale
                ey = load_e(step, 1, x) + COURANT * curl_y * scale
                ez = load_e(step, 2, x) + COURANT * curl_z * scale
                e_out[step, 0, x] = ex
                e_out[step, 1, x] = ey
                e_out[step, 2, x] = ez
                if step + 1 < NT:
                    ys_e[step + 1, 0, pl.ds(x, 1), :] = ex[0:1, :]
                    ys_e[step + 1, 1, pl.ds(x, 1), :] = ez[0:1, :]
                return ey, ez

            ey_first, ez_first = electric(0, west[step, 0], west[step, 1])
            if step + 1 < NT:
                xs_e[step + 1, 0] = ey_first
                xs_e[step + 1, 1] = ez_first

            def electric_body(x, carry, step=step):
                electric(x, h_out[1, x - 1], h_out[2, x - 1])
                return carry

            lax.fori_loop(1, size_x, electric_body, 0, unroll=True)

    rim_x = pltpu.VMEM((NT, 2, size_y, size_z), jnp.float32)
    rim_y = pltpu.VMEM((NT, 2, size_x, size_z), jnp.float32)
    operands = ([] if zero_start else [e_start, h_start]) + [inv_eps] + ([drive] if with_drive else [])
    return pl.pallas_call(
        kernel,
        out_shape=(
            jax.ShapeDtypeStruct((NT, 3, size_x, size_y, size_z), jnp.float32),
            jax.ShapeDtypeStruct((3, size_x, size_y, size_z), jnp.float32),
        ),
        in_specs=[pl.BlockSpec(memory_space=pltpu.VMEM)] * len(operands),
        out_specs=(pl.BlockSpec(memory_space=pltpu.VMEM),) * 2,
        scratch_shapes=[
            rim_x, rim_y, rim_x, rim_y, rim_x, rim_y, rim_x, rim_y,
            pltpu.SemaphoreType.DMA((4 * NT,)),
            pltpu.SemaphoreType.DMA((4 * NT,)),
        ],
        compiler_params=pltpu.CompilerParams(
            collective_id=tag, has_side_effects=True, vmem_limit_bytes=48 * 1024 * 1024
        ),
    )(*operands)


def group_of(axes):
    sizes = [lax.axis_size(a) for a in axes]
    count = math.prod(sizes)
    return count, sizes


def group_place(axes, sizes):
    place = 0
    for axis, size in zip(axes, sizes):
        place = place * size + lax.axis_index(axis)
    return place


def group_device(axes, sizes, peer):
    coords = {}
    rest = peer
    for axis, size in reversed(list(zip(axes, sizes))):
        coords[axis] = rest % size
        rest = rest // size
    return tuple(coords[a] if a in coords else lax.axis_index(a) for a in ("gx", "gy"))


def exchange(pieces, axes, gather, tag):
    count, sizes = group_of(axes)
    piece_shape = pieces.shape if gather else pieces.shape[1:]

    def kernel(x_ref, o_ref, send_sem, recv_sem):
        me = group_place(axes, sizes)
        barrier = pltpu.get_barrier_semaphore()
        for step in range(1, count):
            peer = lax.rem(me + step, count)
            pl.semaphore_signal(
                barrier, 1, device_id=group_device(axes, sizes, peer),
                device_id_type=pl.DeviceIdType.MESH,
            )
        pl.semaphore_wait(barrier, count - 1)
        copies = []
        for step in range(1, count):
            peer = lax.rem(me + step, count)
            copy = pltpu.make_async_remote_copy(
                src_ref=x_ref if gather else x_ref.at[peer],
                dst_ref=o_ref.at[me],
                send_sem=send_sem.at[step],
                recv_sem=recv_sem.at[step],
                device_id=group_device(axes, sizes, peer),
                device_id_type=pl.DeviceIdType.MESH,
            )
            copy.start()
            copies.append(copy)
        own = x_ref[...] if gather else x_ref[me]
        o_ref[me] = own
        for copy in copies:
            copy.wait_send()
        for step in range(1, count):
            source = lax.rem(me + count - step, count)
            pltpu.make_async_remote_copy(
                src_ref=x_ref if gather else x_ref.at[source],
                dst_ref=o_ref.at[source],
                send_sem=send_sem.at[step],
                recv_sem=recv_sem.at[step],
                device_id=group_device(axes, sizes, source),
                device_id_type=pl.DeviceIdType.MESH,
            ).wait_recv()

    return pl.pallas_call(
        kernel,
        out_shape=jax.ShapeDtypeStruct((count,) + tuple(piece_shape), pieces.dtype),
        in_specs=[pl.BlockSpec(memory_space=pltpu.VMEM)],
        out_specs=pl.BlockSpec(memory_space=pltpu.VMEM),
        scratch_shapes=[pltpu.SemaphoreType.DMA((count,)), pltpu.SemaphoreType.DMA((count,))],
        compiler_params=pltpu.CompilerParams(collective_id=tag, has_side_effects=True),
    )(pieces)


def focal_rows(pieces, weights, norm_scale, tag):
    count, sizes = group_of(("gy",))
    rows, width = pieces.shape[1:]

    def kernel(x_ref, t_ref, far_ref, o_ref, got, held, send_sem, recv_sem):
        me = lax.axis_index("gy")
        barrier = pltpu.get_barrier_semaphore()
        for step in range(1, count):
            pl.semaphore_signal(
                barrier, 1, device_id=(lax.axis_index("gx"), lax.rem(me + step, count)),
                device_id_type=pl.DeviceIdType.MESH,
            )
        pl.semaphore_wait(barrier, count - 1)

        def spread(phase, source_of):
            copies = []
            for step in range(1, count):
                peer = lax.rem(me + step, count)
                copy = pltpu.make_async_remote_copy(
                    src_ref=source_of(peer),
                    dst_ref=(got if phase == 0 else o_ref).at[me],
                    send_sem=send_sem.at[phase * count + step],
                    recv_sem=recv_sem.at[phase * count + step],
                    device_id=(lax.axis_index("gx"), peer),
                    device_id_type=pl.DeviceIdType.MESH,
                )
                copy.start()
                copies.append(copy)
            for copy in copies:
                copy.wait_send()
            for step in range(1, count):
                source = lax.rem(me + count - step, count)
                pltpu.make_async_remote_copy(
                    src_ref=source_of(source),
                    dst_ref=(got if phase == 0 else o_ref).at[source],
                    send_sem=send_sem.at[phase * count + step],
                    recv_sem=recv_sem.at[phase * count + step],
                    device_id=(lax.axis_index("gx"), source),
                    device_id_type=pl.DeviceIdType.MESH,
                ).wait_recv()

        got[me] = x_ref[me]
        spread(0, lambda peer: x_ref.at[peer])
        total = got[0]
        for source in range(1, count):
            total = total + got[source]
        far = norm_scale * total
        far_ref[...] = far
        odd = lax.broadcasted_iota(jnp.int32, far.shape, 0) % 2 == 1
        scaled = t_ref[...] * far
        weighted = jnp.where(odd, -scaled, scaled)
        held[...] = weighted
        o_ref[me] = weighted
        spread(1, lambda peer: held)

    return pl.pallas_call(
        kernel,
        out_shape=(
            jax.ShapeDtypeStruct((rows, width), jnp.float32),
            jax.ShapeDtypeStruct((count, rows, width), jnp.float32),
        ),
        in_specs=[pl.BlockSpec(memory_space=pltpu.VMEM)] * 2,
        out_specs=(pl.BlockSpec(memory_space=pltpu.VMEM),) * 2,
        scratch_shapes=[
            pltpu.VMEM((count, rows, width), jnp.float32),
            pltpu.VMEM((rows, width), jnp.float32),
            pltpu.SemaphoreType.DMA((2 * count,)),
            pltpu.SemaphoreType.DMA((2 * count,)),
        ],
        compiler_params=pltpu.CompilerParams(collective_id=tag, has_side_effects=True),
    )(pieces, weights)


def kernel_table(count_out, count_in, offset, length):
    focal_pos = (jnp.arange(count_out, dtype=jnp.float32) + 0.5) / count_out - 0.5
    cell_pos = (
        offset.astype(jnp.float32) + jnp.arange(length, dtype=jnp.float32) + 0.5
    ) / count_in - 0.5
    phase = math.pi * count_out * (focal_pos[:, None] - cell_pos[None, :]) ** 2
    return (jnp.cos(phase), jnp.sin(phase))


def contract(pattern, first_op, second_op):
    return jnp.einsum(pattern, first_op, second_op, precision=lax.Precision.HIGHEST)


def route_pillars(rows, slot_ids, devices, capacity):
    slots = devices * capacity
    placing = (slot_ids[:, None] == jnp.arange(slots, dtype=jnp.int32)[None, :]).astype(
        jnp.float32
    )
    packed = contract("ps,pk->sk", placing, rows)
    got = exchange(packed.reshape(devices, capacity, rows.shape[1]), ("gx", "gy"), False, 0)
    return placing, got.reshape(slots, rows.shape[1])


def shards(fields, eps_background, target, widths, intersection, pillar_tile, anchors):
    span_x = lax.axis_size("gx")
    span_y = lax.axis_size("gy")
    devices = span_x * span_y
    place_x = lax.axis_index("gx")
    place_y = lax.axis_index("gy")
    linear = place_x * span_y + place_y
    offsets = jnp.arange(16, dtype=jnp.int32)
    capacity = 2 * max(1, P_DEV // devices)
    target_tile = pillar_tile[:, 0]
    onehot = (target_tile[:, None] == jnp.arange(devices, dtype=jnp.int32)[None, :]).astype(
        jnp.int32
    )
    earlier = jnp.cumsum(onehot, axis=0) - onehot
    order_in = jnp.sum(earlier * onehot, axis=1)
    slot_ids = target_tile * capacity + order_in
    rows = jnp.concatenate(
        [intersection * widths[:, None], anchors.astype(jnp.float32)], axis=1
    )
    placing, got = route_pillars(rows, slot_ids, devices, capacity)
    local_vals = got[:, :16]
    local_at = got[:, 16:18].astype(jnp.int32)
    cells_x = (local_at[:, 0:1] + (offsets // 4)[None, :]).reshape(-1)
    cells_y = (local_at[:, 1:2] + (offsets % 4)[None, :]).reshape(-1)
    lanes = jnp.arange(TILE, dtype=jnp.int32)
    pick_x = (cells_x[:, None] == lanes[None, :]).astype(jnp.float32)
    pick_y = (cells_y[:, None] == lanes[None, :]).astype(jnp.float32)
    filling = contract("sx,sy->xy", pick_x, pick_y * local_vals.reshape(-1)[:, None])
    z_index = jnp.arange(fields.shape[3], dtype=jnp.int32)
    layers = ((z_index >= ZM - ZP) & (z_index < ZM)).astype(jnp.float32)
    permittivity = eps_background + DELTA_EPS * filling[:, :, None] * layers[None, None, :]
    inv_eps = 1.0 / permittivity
    fields_now = tuple((fields[component] for component in range(6)))
    e_steps, h_last = run_leaps(fields[:3], fields[3:], inv_eps, None, 10)
    mon_re = jnp.zeros((2, TILE, TILE), jnp.float32)
    mon_im = jnp.zeros((2, TILE, TILE), jnp.float32)
    changes = []
    before = fields[:3]
    for moment in range(1, NT + 1):
        after = e_steps[moment - 1]
        monitor = after[0:2, :, :, ZM]
        mon_re = mon_re + math.cos(ANGULAR_STEP * moment) * monitor
        mon_im = mon_im - math.sin(ANGULAR_STEP * moment) * monitor
        changes.append((after - before)[:, :, :, ZM - ZP : ZM])
        before = after
    norm_scale = (TILE * span_x * TILE * span_y) ** (-0.5)
    x_re, x_im = kernel_table(U, TILE * span_x, place_x * TILE, TILE)
    y_re, y_im = kernel_table(V, TILE * span_y, place_y * TILE, TILE)
    part = jnp.stack(
        [
            contract("ux,cxy->ucy", x_re, mon_re) - contract("ux,cxy->ucy", x_im, mon_im),
            contract("ux,cxy->ucy", x_re, mon_im) + contract("ux,cxy->ucy", x_im, mon_re),
        ]
    )
    chunk_u = U // span_x
    part = part.reshape(2, span_x, chunk_u, 2, TILE).transpose(1, 2, 0, 3, 4)
    part = exchange(part.reshape(span_x, chunk_u, 4 * TILE), ("gx",), False, 1)
    part = jnp.sum(part, axis=0).reshape(chunk_u, 2, 2, TILE)
    part_re, part_im = part[:, 0], part[:, 1]
    far = jnp.stack(
        [
            contract("ucy,vy->cuv", part_re, y_re) - contract("ucy,vy->cuv", part_im, y_im),
            contract("ucy,vy->cuv", part_re, y_im) + contract("ucy,vy->cuv", part_im, y_re),
        ],
        axis=2,
    )
    row_count = U // devices
    far = far.reshape(2, span_y, row_count, 2, V).transpose(1, 0, 2, 3, 4)
    mine_target = lax.dynamic_slice_in_dim(target, linear * row_count, row_count, 0)
    row_weights = jnp.broadcast_to(mine_target[None, :, None, :], (2, row_count, 2, V))
    far, weighted = focal_rows(
        far.reshape(span_y, 2 * row_count * 2, V),
        row_weights.reshape(2 * row_count * 2, V),
        norm_scale,
        2,
    )
    far = far.reshape(2, row_count, 2, V)
    focal_power = jnp.sum(far * far, axis=(0, 2))
    weighted = weighted.reshape(span_y, 2, row_count, 2, V).transpose(1, 0, 2, 3, 4)
    weighted = weighted.reshape(2, span_y * row_count, 2, V)
    w_re, w_im = weighted[:, :, 0], weighted[:, :, 1]
    half = jnp.stack(
        [
            contract("cuv,vy->cuy", w_re, y_re) - contract("cuv,vy->cuy", w_im, y_im),
            contract("cuv,vy->cuy", w_re, y_im) + contract("cuv,vy->cuy", w_im, y_re),
        ]
    )
    half = half.transpose(2, 0, 1, 3).reshape(chunk_u, 4 * TILE)
    half = exchange(half, ("gx",), True, 4)
    half = half.reshape(span_x * chunk_u, 2, 2, TILE).transpose(1, 2, 0, 3)
    half_re, half_im = half[0], half[1]
    back_re = 2.0 * norm_scale * (
        contract("ux,cuy->cxy", x_re, half_re) - contract("ux,cuy->cxy", x_im, half_im)
    )
    back_im = 2.0 * norm_scale * (
        contract("ux,cuy->cxy", x_re, half_im) + contract("ux,cuy->cxy", x_im, half_re)
    )
    inv_layer = inv_eps[:, :, ZM - ZP : ZM]
    drives = []
    for moment in range(1, NT + 1):
        source_step = NT + 1 - moment
        adj_drive = (
            math.cos(ANGULAR_STEP * source_step) * back_re
            + math.sin(ANGULAR_STEP * source_step) * back_im
        )
        drives.append(adj_drive)
    drive = jnp.stack(drives)
    z_index = jnp.arange(fields.shape[3], dtype=jnp.int32)
    drive = jnp.where(z_index == ZM, drive[..., None], 0.0)
    a_steps, _ = run_leaps(None, None, inv_eps, drive, 11)
    grad_eps = jnp.zeros((TILE, TILE, ZP), jnp.float32)
    for moment in range(1, NT + 1):
        source_step = NT + 1 - moment
        change = changes[source_step - 1]
        adjoint = a_steps[moment - 1][:, :, :, ZM - ZP : ZM]
        product = adjoint[0] * change[0] + adjoint[1] * change[1] + adjoint[2] * change[2]
        grad_eps = grad_eps - product * inv_layer
    column_grad = jnp.sum(grad_eps, axis=2)
    spread = contract("sx,xy->sy", pick_x, column_grad)
    picked = jnp.sum(spread * pick_y, axis=1).reshape(devices * capacity, 16)
    returned = exchange(picked.reshape(devices, capacity, 16), ("gx", "gy"), False, 5)
    own_vals = contract("ps,sk->pk", placing, returned.reshape(devices * capacity, 16))
    grad_widths = DELTA_EPS * jnp.sum(intersection * own_vals, axis=1)
    return (jnp.concatenate([e_steps[NT - 1], h_last]), focal_power, grad_widths)


def solution(mesh):
    placed = (
        P(None, "gx", "gy", None),
        P("gx", "gy", None),
        P(),
        P(("gx", "gy")),
        P(("gx", "gy"), None),
        P(("gx", "gy"), None),
        P(("gx", "gy"), None),
    )
    return jax.shard_map(
        shards,
        mesh=mesh,
        in_specs=placed,
        out_specs=(P(None, "gx", "gy", None), P(("gx", "gy"), None), P(("gx", "gy"))),
        check_vma=False,
    )
```

```python
import math

import jax
import jax.numpy as jnp
from jax import lax
from jax.sharding import PartitionSpec as P
from jax.experimental import pallas as pl
from jax.experimental.pallas import tpu as pltpu

TILE = 32
P_DEV = 128
NT = 4
ZP = 4
U = 256
V = 256
ZM = 64


COURANT = 0.5
ANGULAR_STEP = 0.9
DELTA_EPS = 4.0


def passed_along(shard, axis, by):
    count = lax.axis_size(axis)
    pairs = [(i, i + by) for i in range(count) if 0 <= i + by < count]
    return lax.ppermute(shard, axis, pairs)


def plus_diff(field, rim_layer, axis):
    extended = jnp.concatenate([field, rim_layer], axis=axis)
    return lax.slice_in_dim(extended, 1, extended.shape[axis], axis=axis) - field


def minus_diff(field, rim_layer, axis):
    extended = jnp.concatenate([rim_layer, field], axis=axis)
    return field - lax.slice_in_dim(extended, 0, field.shape[axis], axis=axis)


def leap_step(fields_now, inv_eps, sources):
    elec_x, elec_y, elec_z, magn_x, magn_y, magn_z = fields_now
    z_blank = jnp.zeros_like(elec_x[:, :, :1])
    rim_east = passed_along(jnp.stack([elec_y[:1], elec_z[:1]]), "gx", -1)
    rim_north = passed_along(jnp.stack([elec_x[:, :1], elec_z[:, :1]]), "gy", -1)
    curl_x = plus_diff(elec_z, rim_north[1], 1) - plus_diff(elec_y, z_blank, 2)
    curl_y = plus_diff(elec_x, z_blank, 2) - plus_diff(elec_z, rim_east[1], 0)
    curl_z = plus_diff(elec_y, rim_east[0], 0) - plus_diff(elec_x, rim_north[0], 1)
    magn_x = magn_x - COURANT * curl_x
    magn_y = magn_y - COURANT * curl_y
    magn_z = magn_z - COURANT * curl_z
    rim_west = passed_along(jnp.stack([magn_y[-1:], magn_z[-1:]]), "gx", 1)
    rim_south = passed_along(jnp.stack([magn_x[:, -1:], magn_z[:, -1:]]), "gy", 1)
    curl_x = minus_diff(magn_z, rim_south[1], 1) - minus_diff(magn_y, z_blank, 2)
    curl_y = minus_diff(magn_x, z_blank, 2) - minus_diff(magn_z, rim_west[1], 0)
    curl_z = minus_diff(magn_y, rim_west[0], 0) - minus_diff(magn_x, rim_south[0], 1)
    elec_x = elec_x + COURANT * (curl_x - sources[0]) * inv_eps
    elec_y = elec_y + COURANT * (curl_y - sources[1]) * inv_eps
    elec_z = elec_z + COURANT * curl_z * inv_eps
    return (elec_x, elec_y, elec_z, magn_x, magn_y, magn_z)


def run_leaps(fields, inv_eps, history, drive, tag):
    span_x = lax.axis_size("gx")
    span_y = lax.axis_size("gy")
    size_x, size_y, size_z = inv_eps.shape
    adjoint = history is not None
    mesh_id = pl.DeviceIdType.MESH

    def kernel(*refs):
        refs = list(refs)
        if adjoint:
            f_in, hist, eps_ref, drv, acc = refs[:5]
            a_hist, h_state = refs[5:7]
            rest = refs[7:]
        else:
            f_in, eps_ref, final, e_hist = refs[:4]
            rest = refs[4:]
        east, north, west, south, xs_e, ys_e, xs_h, ys_h, ssem, rsem = rest
        px = lax.axis_index("gx")
        py = lax.axis_index("gy")
        barrier = pltpu.get_barrier_semaphore()
        for peer in (
            (lax.rem(px + 1, span_x), py),
            (lax.rem(px + span_x - 1, span_x), py),
            (px, lax.rem(py + 1, span_y)),
            (px, lax.rem(py + span_y - 1, span_y)),
        ):
            pl.semaphore_signal(barrier, 1, device_id=peer, device_id_type=mesh_id)
        pl.semaphore_wait(barrier, 4)
        has_east = px < span_x - 1
        has_west = px > 0
        has_north = py < span_y - 1
        has_south = py > 0
        zero_slab = jnp.zeros((size_y, size_z), jnp.float32)
        iy = lax.broadcasted_iota(jnp.int32, (size_y, size_z), 0)
        iz = lax.broadcasted_iota(jnp.int32, (size_y, size_z), 1)

        def up_y(slab, row):
            return jnp.where(iy == size_y - 1, row, pltpu.roll(slab, size_y - 1, 0))

        def down_y(slab, row):
            return jnp.where(iy == 0, row, pltpu.roll(slab, 1, 0))

        def up_z(slab):
            return jnp.where(iz == size_z - 1, 0.0, pltpu.roll(slab, size_z - 1, 1))

        def down_z(slab):
            return jnp.where(iz == 0, 0.0, pltpu.roll(slab, 1, 1))

        def load_e(step, comp, x):
            if step == 0:
                return zero_slab if adjoint else f_in[comp, x]
            if adjoint:
                return a_hist[(step - 1) % 2, comp, x]
            return e_hist[step - 1, comp, x]

        def store_e(step, comp, x, value):
            if adjoint:
                a_hist[step % 2, comp, x] = value
            else:
                e_hist[step, comp, x] = value
                if step == NT - 1:
                    final[comp, x] = value

        def load_h(step, comp, x):
            if step == 0:
                return zero_slab if adjoint else f_in[3 + comp, x]
            return h_state[comp, x] if adjoint else final[3 + comp, x]

        def store_h(comp, x, value):
            if adjoint:
                h_state[comp, x] = value
            else:
                final[3 + comp, x] = value

        def forward_e(n, comp, x):
            return f_in[comp, x] if n == 0 else hist[n - 1, comp, x]

        def swap(src_x, dst_x, src_y, dst_y, sem, to_x, to_y, sends_x, sends_y, gets_x, gets_y):
            copy_x = pltpu.make_async_remote_copy(
                src_ref=src_x, dst_ref=dst_x, send_sem=ssem.at[sem], recv_sem=rsem.at[sem],
                device_id=(to_x, py), device_id_type=mesh_id,
            )
            copy_y = pltpu.make_async_remote_copy(
                src_ref=src_y, dst_ref=dst_y, send_sem=ssem.at[sem + 1], recv_sem=rsem.at[sem + 1],
                device_id=(px, to_y), device_id_type=mesh_id,
            )
            pl.when(sends_x)(copy_x.start)
            pl.when(sends_y)(copy_y.start)

            @pl.when(jnp.logical_not(gets_x))
            def _():
                dst_x[...] = jnp.zeros(dst_x.shape, jnp.float32)

            @pl.when(jnp.logical_not(gets_y))
            def _():
                dst_y[...] = jnp.zeros(dst_y.shape, jnp.float32)

            pl.when(gets_x)(copy_x.wait_recv)
            pl.when(gets_y)(copy_y.wait_recv)
            pl.when(sends_x)(copy_x.wait_send)
            pl.when(sends_y)(copy_y.wait_send)

        if not adjoint:
            xs_e[0, 0] = f_in[1, 0]
            xs_e[0, 1] = f_in[2, 0]

            def stage_first(x, carry):
                ys_e[0, 0, pl.ds(x, 1), :] = f_in[0, x][0:1, :]
                ys_e[0, 1, pl.ds(x, 1), :] = f_in[2, x][0:1, :]
                return carry

            lax.fori_loop(0, size_x, stage_first, 0)

        for step in range(NT):
            if step == 0 and adjoint:
                east[0] = jnp.zeros(east.shape[1:], jnp.float32)
                north[0] = jnp.zeros(north.shape[1:], jnp.float32)
            else:
                swap(
                    xs_e.at[step], east.at[step], ys_e.at[step], north.at[step], 4 * step,
                    lax.rem(px + span_x - 1, span_x), lax.rem(py + span_y - 1, span_y),
                    has_west, has_south, has_east, has_north,
                )

            def magnetic(x, ey_next, ez_next, step=step):
                ex = load_e(step, 0, x)
                ey = load_e(step, 1, x)
                ez = load_e(step, 2, x)
                nx_row = north[step, 0, pl.ds(x, 1), :]
                nz_row = north[step, 1, pl.ds(x, 1), :]
                curl_x = (up_y(ez, nz_row) - ez) - (up_z(ey) - ey)
                curl_y = (up_z(ex) - ex) - (ez_next - ez)
                curl_z = (ey_next - ey) - (up_y(ex, nx_row) - ex)
                hx = load_h(step, 0, x) - COURANT * curl_x
                hy = load_h(step, 1, x) - COURANT * curl_y
                hz = load_h(step, 2, x) - COURANT * curl_z
                store_h(0, x, hx)
                store_h(1, x, hy)
                store_h(2, x, hz)
                ys_h[step, 0, pl.ds(x, 1), :] = hx[size_y - 1 : size_y, :]
                ys_h[step, 1, pl.ds(x, 1), :] = hz[size_y - 1 : size_y, :]
                return hy, hz

            def magnetic_body(x, carry, step=step):
                magnetic(x, load_e(step, 1, x + 1), load_e(step, 2, x + 1))
                return carry

            lax.fori_loop(0, size_x - 1, magnetic_body, 0, unroll=True)
            hy_last, hz_last = magnetic(size_x - 1, east[step, 0], east[step, 1])
            xs_h[step, 0] = hy_last
            xs_h[step, 1] = hz_last
            swap(
                xs_h.at[step], west.at[step], ys_h.at[step], south.at[step], 4 * step + 2,
                lax.rem(px + 1, span_x), lax.rem(py + 1, span_y),
                has_east, has_north, has_west, has_south,
            )

            def electric(x, hy_prev, hz_prev, step=step):
                hx = load_h(step + 1, 0, x)
                hy = load_h(step + 1, 1, x)
                hz = load_h(step + 1, 2, x)
                sx_row = south[step, 0, pl.ds(x, 1), :]
                sz_row = south[step, 1, pl.ds(x, 1), :]
                curl_x = (hz - down_y(hz, sz_row)) - (hy - down_z(hy))
                curl_y = (hx - down_z(hx)) - (hz - hz_prev)
                curl_z = (hy - hy_prev) - (hx - down_y(hx, sx_row))
                if adjoint:
                    curl_x = curl_x - drv[step, 0, x]
                    curl_y = curl_y - drv[step, 1, x]
                scale = eps_ref[x]
                ex = load_e(step, 0, x) + COURANT * curl_x * scale
                ey = load_e(step, 1, x) + COURANT * curl_y * scale
                ez = load_e(step, 2, x) + COURANT * curl_z * scale
                store_e(step, 0, x, ex)
                store_e(step, 1, x, ey)
                store_e(step, 2, x, ez)
                if adjoint:
                    moment = NT - step
                    product = (
                        ex * (forward_e(moment, 0, x) - forward_e(moment - 1, 0, x))
                        + ey * (forward_e(moment, 1, x) - forward_e(moment - 1, 1, x))
                        + ez * (forward_e(moment, 2, x) - forward_e(moment - 1, 2, x))
                    )
                    before = zero_slab if step == 0 else acc[x]
                    acc[x] = before - product * scale
                if step + 1 < NT:
                    ys_e[step + 1, 0, pl.ds(x, 1), :] = ex[0:1, :]
                    ys_e[step + 1, 1, pl.ds(x, 1), :] = ez[0:1, :]
                return ey, ez

            ey_first, ez_first = electric(0, west[step, 0], west[step, 1])
            if step + 1 < NT:
                xs_e[step + 1, 0] = ey_first
                xs_e[step + 1, 1] = ez_first

            def electric_body(x, carry, step=step):
                electric(x, load_h(step + 1, 1, x - 1), load_h(step + 1, 2, x - 1))
                return carry

            lax.fori_loop(1, size_x, electric_body, 0, unroll=True)

    rim_x = pltpu.VMEM((NT, 2, size_y, size_z), jnp.float32)
    rim_y = pltpu.VMEM((NT, 2, size_x, size_z), jnp.float32)
    field_shape = (size_x, size_y, size_z)
    if adjoint:
        operands = [fields, history, inv_eps, drive]
        out_shape = jax.ShapeDtypeStruct(field_shape, jnp.float32)
        out_specs = pl.BlockSpec(memory_space=pltpu.VMEM)
        state = [
            pltpu.VMEM((2, 3) + field_shape, jnp.float32),
            pltpu.VMEM((3,) + field_shape, jnp.float32),
        ]
    else:
        operands = [fields, inv_eps]
        out_shape = (
            jax.ShapeDtypeStruct((6,) + field_shape, jnp.float32),
            jax.ShapeDtypeStruct((NT, 3) + field_shape, jnp.float32),
        )
        out_specs = (pl.BlockSpec(memory_space=pltpu.VMEM),) * 2
        state = []
    return pl.pallas_call(
        kernel,
        out_shape=out_shape,
        in_specs=[pl.BlockSpec(memory_space=pltpu.VMEM)] * len(operands),
        out_specs=out_specs,
        scratch_shapes=state + [
            rim_x, rim_y, rim_x, rim_y, rim_x, rim_y, rim_x, rim_y,
            pltpu.SemaphoreType.DMA((4 * NT,)),
            pltpu.SemaphoreType.DMA((4 * NT,)),
        ],
        compiler_params=pltpu.CompilerParams(
            collective_id=tag, has_side_effects=True, vmem_limit_bytes=56 * 1024 * 1024
        ),
    )(*operands)


def group_of(axes):
    sizes = [lax.axis_size(a) for a in axes]
    count = math.prod(sizes)
    return count, sizes


def group_place(axes, sizes):
    place = 0
    for axis, size in zip(axes, sizes):
        place = place * size + lax.axis_index(axis)
    return place


def group_device(axes, sizes, peer):
    coords = {}
    rest = peer
    for axis, size in reversed(list(zip(axes, sizes))):
        coords[axis] = rest % size
        rest = rest // size
    return tuple(coords[a] if a in coords else lax.axis_index(a) for a in ("gx", "gy"))


def exchange(pieces, axes, gather, tag):
    count, sizes = group_of(axes)
    piece_shape = pieces.shape if gather else pieces.shape[1:]

    def kernel(x_ref, o_ref, send_sem, recv_sem):
        me = group_place(axes, sizes)
        barrier = pltpu.get_barrier_semaphore()
        for step in range(1, count):
            peer = lax.rem(me + step, count)
            pl.semaphore_signal(
                barrier, 1, device_id=group_device(axes, sizes, peer),
                device_id_type=pl.DeviceIdType.MESH,
            )
        pl.semaphore_wait(barrier, count - 1)
        copies = []
        for step in range(1, count):
            peer = lax.rem(me + step, count)
            copy = pltpu.make_async_remote_copy(
                src_ref=x_ref if gather else x_ref.at[peer],
                dst_ref=o_ref.at[me],
                send_sem=send_sem.at[step],
                recv_sem=recv_sem.at[step],
                device_id=group_device(axes, sizes, peer),
                device_id_type=pl.DeviceIdType.MESH,
            )
            copy.start()
            copies.append(copy)
        own = x_ref[...] if gather else x_ref[me]
        o_ref[me] = own
        for copy in copies:
            copy.wait_send()
        for step in range(1, count):
            source = lax.rem(me + count - step, count)
            pltpu.make_async_remote_copy(
                src_ref=x_ref if gather else x_ref.at[source],
                dst_ref=o_ref.at[source],
                send_sem=send_sem.at[step],
                recv_sem=recv_sem.at[step],
                device_id=group_device(axes, sizes, source),
                device_id_type=pl.DeviceIdType.MESH,
            ).wait_recv()

    return pl.pallas_call(
        kernel,
        out_shape=jax.ShapeDtypeStruct((count,) + tuple(piece_shape), pieces.dtype),
        in_specs=[pl.BlockSpec(memory_space=pltpu.VMEM)],
        out_specs=pl.BlockSpec(memory_space=pltpu.VMEM),
        scratch_shapes=[pltpu.SemaphoreType.DMA((count,)), pltpu.SemaphoreType.DMA((count,))],
        compiler_params=pltpu.CompilerParams(collective_id=tag, has_side_effects=True),
    )(pieces)


def focal_rows(pieces, weights, norm_scale, tag):
    count, sizes = group_of(("gy",))
    rows, width = pieces.shape[1:]

    def kernel(x_ref, t_ref, far_ref, o_ref, got, held, send_sem, recv_sem):
        me = lax.axis_index("gy")
        barrier = pltpu.get_barrier_semaphore()
        for step in range(1, count):
            pl.semaphore_signal(
                barrier, 1, device_id=(lax.axis_index("gx"), lax.rem(me + step, count)),
                device_id_type=pl.DeviceIdType.MESH,
            )
        pl.semaphore_wait(barrier, count - 1)

        def spread(phase, source_of):
            copies = []
            for step in range(1, count):
                peer = lax.rem(me + step, count)
                copy = pltpu.make_async_remote_copy(
                    src_ref=source_of(peer),
                    dst_ref=(got if phase == 0 else o_ref).at[me],
                    send_sem=send_sem.at[phase * count + step],
                    recv_sem=recv_sem.at[phase * count + step],
                    device_id=(lax.axis_index("gx"), peer),
                    device_id_type=pl.DeviceIdType.MESH,
                )
                copy.start()
                copies.append(copy)
            for copy in copies:
                copy.wait_send()
            for step in range(1, count):
                source = lax.rem(me + count - step, count)
                pltpu.make_async_remote_copy(
                    src_ref=source_of(source),
                    dst_ref=(got if phase == 0 else o_ref).at[source],
                    send_sem=send_sem.at[phase * count + step],
                    recv_sem=recv_sem.at[phase * count + step],
                    device_id=(lax.axis_index("gx"), source),
                    device_id_type=pl.DeviceIdType.MESH,
                ).wait_recv()

        got[me] = x_ref[me]
        spread(0, lambda peer: x_ref.at[peer])
        total = got[0]
        for source in range(1, count):
            total = total + got[source]
        far = norm_scale * total
        far_ref[...] = far
        odd = lax.broadcasted_iota(jnp.int32, far.shape, 0) % 2 == 1
        scaled = t_ref[...] * far
        weighted = jnp.where(odd, -scaled, scaled)
        held[...] = weighted
        o_ref[me] = weighted
        spread(1, lambda peer: held)

    return pl.pallas_call(
        kernel,
        out_shape=(
            jax.ShapeDtypeStruct((rows, width), jnp.float32),
            jax.ShapeDtypeStruct((count, rows, width), jnp.float32),
        ),
        in_specs=[pl.BlockSpec(memory_space=pltpu.VMEM)] * 2,
        out_specs=(pl.BlockSpec(memory_space=pltpu.VMEM),) * 2,
        scratch_shapes=[
            pltpu.VMEM((count, rows, width), jnp.float32),
            pltpu.VMEM((rows, width), jnp.float32),
            pltpu.SemaphoreType.DMA((2 * count,)),
            pltpu.SemaphoreType.DMA((2 * count,)),
        ],
        compiler_params=pltpu.CompilerParams(collective_id=tag, has_side_effects=True),
    )(pieces, weights)


def kernel_table(count_out, count_in, offset, length):
    focal_pos = (jnp.arange(count_out, dtype=jnp.float32) + 0.5) / count_out - 0.5
    cell_pos = (
        offset.astype(jnp.float32) + jnp.arange(length, dtype=jnp.float32) + 0.5
    ) / count_in - 0.5
    phase = math.pi * count_out * (focal_pos[:, None] - cell_pos[None, :]) ** 2
    return (jnp.cos(phase), jnp.sin(phase))


def contract(pattern, first_op, second_op):
    return jnp.einsum(pattern, first_op, second_op, precision=lax.Precision.HIGHEST)


def route_pillars(rows, slot_ids, devices, capacity):
    slots = devices * capacity
    placing = (slot_ids[:, None] == jnp.arange(slots, dtype=jnp.int32)[None, :]).astype(
        jnp.float32
    )
    packed = contract("ps,pk->sk", placing, rows)
    got = exchange(packed.reshape(devices, capacity, rows.shape[1]), ("gx", "gy"), False, 0)
    return placing, got.reshape(slots, rows.shape[1])


def shards(fields, eps_background, target, widths, intersection, pillar_tile, anchors):
    span_x = lax.axis_size("gx")
    span_y = lax.axis_size("gy")
    devices = span_x * span_y
    place_x = lax.axis_index("gx")
    place_y = lax.axis_index("gy")
    linear = place_x * span_y + place_y
    offsets = jnp.arange(16, dtype=jnp.int32)
    capacity = 2 * max(1, P_DEV // devices)
    target_tile = pillar_tile[:, 0]
    onehot = (target_tile[:, None] == jnp.arange(devices, dtype=jnp.int32)[None, :]).astype(
        jnp.int32
    )
    earlier = jnp.cumsum(onehot, axis=0) - onehot
    order_in = jnp.sum(earlier * onehot, axis=1)
    slot_ids = target_tile * capacity + order_in
    rows = jnp.concatenate(
        [intersection * widths[:, None], anchors.astype(jnp.float32)], axis=1
    )
    placing, got = route_pillars(rows, slot_ids, devices, capacity)
    local_vals = got[:, :16]
    local_at = got[:, 16:18].astype(jnp.int32)
    cells_x = (local_at[:, 0:1] + (offsets // 4)[None, :]).reshape(-1)
    cells_y = (local_at[:, 1:2] + (offsets % 4)[None, :]).reshape(-1)
    lanes = jnp.arange(TILE, dtype=jnp.int32)
    pick_x = (cells_x[:, None] == lanes[None, :]).astype(jnp.float32)
    pick_y = (cells_y[:, None] == lanes[None, :]).astype(jnp.float32)
    filling = contract("sx,sy->xy", pick_x, pick_y * local_vals.reshape(-1)[:, None])
    z_index = jnp.arange(fields.shape[3], dtype=jnp.int32)
    layers = ((z_index >= ZM - ZP) & (z_index < ZM)).astype(jnp.float32)
    permittivity = eps_background + DELTA_EPS * filling[:, :, None] * layers[None, None, :]
    inv_eps = 1.0 / permittivity
    final_fields, e_steps = run_leaps(fields, inv_eps, None, None, 10)
    mon_re = jnp.zeros((2, TILE, TILE), jnp.float32)
    mon_im = jnp.zeros((2, TILE, TILE), jnp.float32)
    for moment in range(1, NT + 1):
        monitor = e_steps[moment - 1, 0:2, :, :, ZM]
        mon_re = mon_re + math.cos(ANGULAR_STEP * moment) * monitor
        mon_im = mon_im - math.sin(ANGULAR_STEP * moment) * monitor
    norm_scale = (TILE * span_x * TILE * span_y) ** (-0.5)
    x_re, x_im = kernel_table(U, TILE * span_x, place_x * TILE, TILE)
    y_re, y_im = kernel_table(V, TILE * span_y, place_y * TILE, TILE)
    part = jnp.stack(
        [
            contract("ux,cxy->ucy", x_re, mon_re) - contract("ux,cxy->ucy", x_im, mon_im),
            contract("ux,cxy->ucy", x_re, mon_im) + contract("ux,cxy->ucy", x_im, mon_re),
        ]
    )
    chunk_u = U // span_x
    part = part.reshape(2, span_x, chunk_u, 2, TILE).transpose(1, 2, 0, 3, 4)
    part = exchange(part.reshape(span_x, chunk_u, 4 * TILE), ("gx",), False, 1)
    part = jnp.sum(part, axis=0).reshape(chunk_u, 2, 2, TILE)
    part_re, part_im = part[:, 0], part[:, 1]
    far = jnp.stack(
        [
            contract("ucy,vy->cuv", part_re, y_re) - contract("ucy,vy->cuv", part_im, y_im),
            contract("ucy,vy->cuv", part_re, y_im) + contract("ucy,vy->cuv", part_im, y_re),
        ],
        axis=2,
    )
    row_count = U // devices
    far = far.reshape(2, span_y, row_count, 2, V).transpose(1, 0, 2, 3, 4)
    mine_target = lax.dynamic_slice_in_dim(target, linear * row_count, row_count, 0)
    row_weights = jnp.broadcast_to(mine_target[None, :, None, :], (2, row_count, 2, V))
    far, weighted = focal_rows(
        far.reshape(span_y, 2 * row_count * 2, V),
        row_weights.reshape(2 * row_count * 2, V),
        norm_scale,
        2,
    )
    far = far.reshape(2, row_count, 2, V)
    focal_power = jnp.sum(far * far, axis=(0, 2))
    weighted = weighted.reshape(span_y, 2, row_count, 2, V).transpose(1, 0, 2, 3, 4)
    weighted = weighted.reshape(2, span_y * row_count, 2, V)
    w_re, w_im = weighted[:, :, 0], weighted[:, :, 1]
    half = jnp.stack(
        [
            contract("cuv,vy->cuy", w_re, y_re) - contract("cuv,vy->cuy", w_im, y_im),
            contract("cuv,vy->cuy", w_re, y_im) + contract("cuv,vy->cuy", w_im, y_re),
        ]
    )
    half = half.transpose(2, 0, 1, 3).reshape(chunk_u, 4 * TILE)
    half = exchange(half, ("gx",), True, 4)
    half = half.reshape(span_x * chunk_u, 2, 2, TILE).transpose(1, 2, 0, 3)
    half_re, half_im = half[0], half[1]
    back_re = 2.0 * norm_scale * (
        contract("ux,cuy->cxy", x_re, half_re) - contract("ux,cuy->cxy", x_im, half_im)
    )
    back_im = 2.0 * norm_scale * (
        contract("ux,cuy->cxy", x_re, half_im) + contract("ux,cuy->cxy", x_im, half_re)
    )
    drives = []
    for moment in range(1, NT + 1):
        source_step = NT + 1 - moment
        adj_drive = (
            math.cos(ANGULAR_STEP * source_step) * back_re
            + math.sin(ANGULAR_STEP * source_step) * back_im
        )
        drives.append(adj_drive)
    drive = jnp.stack(drives)
    z_index = jnp.arange(fields.shape[3], dtype=jnp.int32)
    drive = jnp.where(z_index == ZM, drive[..., None], 0.0)
    grad_eps = run_leaps(fields, inv_eps, e_steps, drive, 11)
    column_grad = jnp.sum(grad_eps[:, :, ZM - ZP : ZM], axis=2)
    spread = contract("sx,xy->sy", pick_x, column_grad)
    picked = jnp.sum(spread * pick_y, axis=1).reshape(devices * capacity, 16)
    returned = exchange(picked.reshape(devices, capacity, 16), ("gx", "gy"), False, 5)
    own_vals = contract("ps,sk->pk", placing, returned.reshape(devices * capacity, 16))
    grad_widths = DELTA_EPS * jnp.sum(intersection * own_vals, axis=1)
    return (final_fields, focal_power, grad_widths)


def solution(mesh):
    placed = (
        P(None, "gx", "gy", None),
        P("gx", "gy", None),
        P(),
        P(("gx", "gy")),
        P(("gx", "gy"), None),
        P(("gx", "gy"), None),
        P(("gx", "gy"), None),
    )
    return jax.shard_map(
        shards,
        mesh=mesh,
        in_specs=placed,
        out_specs=(P(None, "gx", "gy", None), P(("gx", "gy"), None), P(("gx", "gy"))),
        check_vma=False,
    )
```

```python
import math

import jax
import jax.numpy as jnp
from jax import lax
from jax.sharding import PartitionSpec as P
from jax.experimental import pallas as pl
from jax.experimental.pallas import tpu as pltpu

TILE = 32
P_DEV = 128
NT = 4
ZP = 4
U = 256
V = 256
ZM = 64


COURANT = 0.5
ANGULAR_STEP = 0.9
DELTA_EPS = 4.0


def passed_along(shard, axis, by):
    count = lax.axis_size(axis)
    pairs = [(i, i + by) for i in range(count) if 0 <= i + by < count]
    return lax.ppermute(shard, axis, pairs)


def plus_diff(field, rim_layer, axis):
    extended = jnp.concatenate([field, rim_layer], axis=axis)
    return lax.slice_in_dim(extended, 1, extended.shape[axis], axis=axis) - field


def minus_diff(field, rim_layer, axis):
    extended = jnp.concatenate([rim_layer, field], axis=axis)
    return field - lax.slice_in_dim(extended, 0, field.shape[axis], axis=axis)


def leap_step(fields_now, inv_eps, sources):
    elec_x, elec_y, elec_z, magn_x, magn_y, magn_z = fields_now
    z_blank = jnp.zeros_like(elec_x[:, :, :1])
    rim_east = passed_along(jnp.stack([elec_y[:1], elec_z[:1]]), "gx", -1)
    rim_north = passed_along(jnp.stack([elec_x[:, :1], elec_z[:, :1]]), "gy", -1)
    curl_x = plus_diff(elec_z, rim_north[1], 1) - plus_diff(elec_y, z_blank, 2)
    curl_y = plus_diff(elec_x, z_blank, 2) - plus_diff(elec_z, rim_east[1], 0)
    curl_z = plus_diff(elec_y, rim_east[0], 0) - plus_diff(elec_x, rim_north[0], 1)
    magn_x = magn_x - COURANT * curl_x
    magn_y = magn_y - COURANT * curl_y
    magn_z = magn_z - COURANT * curl_z
    rim_west = passed_along(jnp.stack([magn_y[-1:], magn_z[-1:]]), "gx", 1)
    rim_south = passed_along(jnp.stack([magn_x[:, -1:], magn_z[:, -1:]]), "gy", 1)
    curl_x = minus_diff(magn_z, rim_south[1], 1) - minus_diff(magn_y, z_blank, 2)
    curl_y = minus_diff(magn_x, z_blank, 2) - minus_diff(magn_z, rim_west[1], 0)
    curl_z = minus_diff(magn_y, rim_west[0], 0) - minus_diff(magn_x, rim_south[0], 1)
    elec_x = elec_x + COURANT * (curl_x - sources[0]) * inv_eps
    elec_y = elec_y + COURANT * (curl_y - sources[1]) * inv_eps
    elec_z = elec_z + COURANT * curl_z * inv_eps
    return (elec_x, elec_y, elec_z, magn_x, magn_y, magn_z)


def run_leaps(fields, inv_eps, history, drive, tag):
    span_x = lax.axis_size("gx")
    span_y = lax.axis_size("gy")
    size_x, size_y, size_z = inv_eps.shape
    adjoint = history is not None
    mesh_id = pl.DeviceIdType.MESH

    def kernel(*refs):
        refs = list(refs)
        if adjoint:
            f_in, hist, eps_ref, drv, acc = refs[:5]
            a_hist, h_state = refs[5:7]
            rest = refs[7:]
        else:
            f_in, eps_ref, final, e_hist = refs[:4]
            rest = refs[4:]
        east, north, west, south, xs_e, ys_e, xs_h, ys_h, ssem, rsem = rest
        px = lax.axis_index("gx")
        py = lax.axis_index("gy")
        barrier = pltpu.get_barrier_semaphore()
        for peer in (
            (lax.rem(px + 1, span_x), py),
            (lax.rem(px + span_x - 1, span_x), py),
            (px, lax.rem(py + 1, span_y)),
            (px, lax.rem(py + span_y - 1, span_y)),
        ):
            pl.semaphore_signal(barrier, 1, device_id=peer, device_id_type=mesh_id)
        pl.semaphore_wait(barrier, 4)
        has_east = px < span_x - 1
        has_west = px > 0
        has_north = py < span_y - 1
        has_south = py > 0
        zero_slab = jnp.zeros((size_y, size_z), jnp.float32)
        iy = lax.broadcasted_iota(jnp.int32, (size_y, size_z), 0)
        iz = lax.broadcasted_iota(jnp.int32, (size_y, size_z), 1)

        def up_y(slab, row):
            return jnp.where(iy == size_y - 1, row, pltpu.roll(slab, size_y - 1, 0))

        def down_y(slab, row):
            return jnp.where(iy == 0, row, pltpu.roll(slab, 1, 0))

        def up_z(slab):
            return jnp.where(iz == size_z - 1, 0.0, pltpu.roll(slab, size_z - 1, 1))

        def down_z(slab):
            return jnp.where(iz == 0, 0.0, pltpu.roll(slab, 1, 1))

        def load_e(step, comp, x):
            if step == 0:
                return zero_slab if adjoint else f_in[comp, x]
            if adjoint:
                return a_hist[(step - 1) % 2, comp, x]
            return e_hist[step - 1, comp, x]

        def store_e(step, comp, x, value):
            if adjoint:
                a_hist[step % 2, comp, x] = value
            else:
                e_hist[step, comp, x] = value
                if step == NT - 1:
                    final[comp, x] = value

        def load_h(step, comp, x):
            if adjoint and step <= 1:
                return zero_slab
            if step == 0:
                return f_in[3 + comp, x]
            return h_state[comp, x] if adjoint else final[3 + comp, x]

        def store_h(comp, x, value):
            if adjoint:
                h_state[comp, x] = value
            else:
                final[3 + comp, x] = value

        def forward_e(n, comp, x):
            return f_in[comp, x] if n == 0 else hist[n - 1, comp, x]

        def swap(src_x, dst_x, src_y, dst_y, sem, to_x, to_y, sends_x, sends_y, gets_x, gets_y):
            copy_x = pltpu.make_async_remote_copy(
                src_ref=src_x, dst_ref=dst_x, send_sem=ssem.at[sem], recv_sem=rsem.at[sem],
                device_id=(to_x, py), device_id_type=mesh_id,
            )
            copy_y = pltpu.make_async_remote_copy(
                src_ref=src_y, dst_ref=dst_y, send_sem=ssem.at[sem + 1], recv_sem=rsem.at[sem + 1],
                device_id=(px, to_y), device_id_type=mesh_id,
            )
            pl.when(sends_x)(copy_x.start)
            pl.when(sends_y)(copy_y.start)

            @pl.when(jnp.logical_not(gets_x))
            def _():
                dst_x[...] = jnp.zeros(dst_x.shape, jnp.float32)

            @pl.when(jnp.logical_not(gets_y))
            def _():
                dst_y[...] = jnp.zeros(dst_y.shape, jnp.float32)

            pl.when(gets_x)(copy_x.wait_recv)
            pl.when(gets_y)(copy_y.wait_recv)
            pl.when(sends_x)(copy_x.wait_send)
            pl.when(sends_y)(copy_y.wait_send)

        if not adjoint:
            xs_e[0, 0] = f_in[1, 0]
            xs_e[0, 1] = f_in[2, 0]

            def stage_first(x, carry):
                ys_e[0, 0, pl.ds(x, 1), :] = f_in[0, x][0:1, :]
                ys_e[0, 1, pl.ds(x, 1), :] = f_in[2, x][0:1, :]
                return carry

            lax.fori_loop(0, size_x, stage_first, 0)

        for step in range(NT):
            if not (step == 0 and adjoint):
                swap(
                    xs_e.at[step], east.at[step], ys_e.at[step], north.at[step], 4 * step,
                    lax.rem(px + span_x - 1, span_x), lax.rem(py + span_y - 1, span_y),
                    has_west, has_south, has_east, has_north,
                )

            skip_magnetic = adjoint and step == 0
            if not skip_magnetic:
                ey = load_e(step, 1, 0)
                ez = load_e(step, 2, 0)
                for x in range(size_x):
                    ex = load_e(step, 0, x)
                    if x + 1 < size_x:
                        ey_next = load_e(step, 1, x + 1)
                        ez_next = load_e(step, 2, x + 1)
                    else:
                        ey_next = east[step, 0]
                        ez_next = east[step, 1]
                    nx_row = north[step, 0, x : x + 1, :]
                    nz_row = north[step, 1, x : x + 1, :]
                    curl_x = (up_y(ez, nz_row) - ez) - (up_z(ey) - ey)
                    curl_y = (up_z(ex) - ex) - (ez_next - ez)
                    curl_z = (ey_next - ey) - (up_y(ex, nx_row) - ex)
                    hx = load_h(step, 0, x) - COURANT * curl_x
                    hy = load_h(step, 1, x) - COURANT * curl_y
                    hz = load_h(step, 2, x) - COURANT * curl_z
                    store_h(0, x, hx)
                    store_h(1, x, hy)
                    store_h(2, x, hz)
                    ys_h[step, 0, x : x + 1, :] = hx[size_y - 1 : size_y, :]
                    ys_h[step, 1, x : x + 1, :] = hz[size_y - 1 : size_y, :]
                    if x == size_x - 1:
                        xs_h[step, 0] = hy
                        xs_h[step, 1] = hz
                    ey, ez = ey_next, ez_next
                swap(
                    xs_h.at[step], west.at[step], ys_h.at[step], south.at[step], 4 * step + 2,
                    lax.rem(px + 1, span_x), lax.rem(py + 1, span_y),
                    has_east, has_north, has_west, has_south,
                )

            hy_prev = None if skip_magnetic else west[step, 0]
            hz_prev = None if skip_magnetic else west[step, 1]
            for x in range(size_x):
                if skip_magnetic:
                    curl_x = curl_y = curl_z = zero_slab
                else:
                    hx = load_h(step + 1, 0, x)
                    hy = load_h(step + 1, 1, x)
                    hz = load_h(step + 1, 2, x)
                    sx_row = south[step, 0, x : x + 1, :]
                    sz_row = south[step, 1, x : x + 1, :]
                    curl_x = (hz - down_y(hz, sz_row)) - (hy - down_z(hy))
                    curl_y = (hx - down_z(hx)) - (hz - hz_prev)
                    curl_z = (hy - hy_prev) - (hx - down_y(hx, sx_row))
                    hy_prev, hz_prev = hy, hz
                if adjoint:
                    curl_x = curl_x - drv[step, 0, x]
                    curl_y = curl_y - drv[step, 1, x]
                scale = eps_ref[x]
                ex = load_e(step, 0, x) + COURANT * curl_x * scale
                ey = load_e(step, 1, x) + COURANT * curl_y * scale
                ez = load_e(step, 2, x) + COURANT * curl_z * scale
                store_e(step, 0, x, ex)
                store_e(step, 1, x, ey)
                store_e(step, 2, x, ez)
                if adjoint:
                    moment = NT - step
                    product = (
                        ex * (forward_e(moment, 0, x) - forward_e(moment - 1, 0, x))
                        + ey * (forward_e(moment, 1, x) - forward_e(moment - 1, 1, x))
                        + ez * (forward_e(moment, 2, x) - forward_e(moment - 1, 2, x))
                    )
                    before = zero_slab if step == 0 else acc[x]
                    acc[x] = before - product * scale
                if step + 1 < NT:
                    ys_e[step + 1, 0, x : x + 1, :] = ex[0:1, :]
                    ys_e[step + 1, 1, x : x + 1, :] = ez[0:1, :]
                    if x == 0:
                        xs_e[step + 1, 0] = ey
                        xs_e[step + 1, 1] = ez

    rim_x = pltpu.VMEM((NT, 2, size_y, size_z), jnp.float32)
    rim_y = pltpu.VMEM((NT, 2, size_x, size_z), jnp.float32)
    field_shape = (size_x, size_y, size_z)
    if adjoint:
        operands = [fields, history, inv_eps, drive]
        out_shape = jax.ShapeDtypeStruct(field_shape, jnp.float32)
        out_specs = pl.BlockSpec(memory_space=pltpu.VMEM)
        state = [
            pltpu.VMEM((2, 3) + field_shape, jnp.float32),
            pltpu.VMEM((3,) + field_shape, jnp.float32),
        ]
    else:
        operands = [fields, inv_eps]
        out_shape = (
            jax.ShapeDtypeStruct((6,) + field_shape, jnp.float32),
            jax.ShapeDtypeStruct((NT, 3) + field_shape, jnp.float32),
        )
        out_specs = (pl.BlockSpec(memory_space=pltpu.VMEM),) * 2
        state = []
    return pl.pallas_call(
        kernel,
        out_shape=out_shape,
        in_specs=[pl.BlockSpec(memory_space=pltpu.VMEM)] * len(operands),
        out_specs=out_specs,
        scratch_shapes=state + [
            rim_x, rim_y, rim_x, rim_y, rim_x, rim_y, rim_x, rim_y,
            pltpu.SemaphoreType.DMA((4 * NT,)),
            pltpu.SemaphoreType.DMA((4 * NT,)),
        ],
        compiler_params=pltpu.CompilerParams(
            collective_id=tag, has_side_effects=True, vmem_limit_bytes=56 * 1024 * 1024
        ),
    )(*operands)


def group_of(axes):
    sizes = [lax.axis_size(a) for a in axes]
    count = math.prod(sizes)
    return count, sizes


def group_place(axes, sizes):
    place = 0
    for axis, size in zip(axes, sizes):
        place = place * size + lax.axis_index(axis)
    return place


def group_device(axes, sizes, peer):
    coords = {}
    rest = peer
    for axis, size in reversed(list(zip(axes, sizes))):
        coords[axis] = rest % size
        rest = rest // size
    return tuple(coords[a] if a in coords else lax.axis_index(a) for a in ("gx", "gy"))


def exchange(pieces, axes, gather, tag):
    count, sizes = group_of(axes)
    piece_shape = pieces.shape if gather else pieces.shape[1:]

    def kernel(x_ref, o_ref, send_sem, recv_sem):
        me = group_place(axes, sizes)
        barrier = pltpu.get_barrier_semaphore()
        for step in range(1, count):
            peer = lax.rem(me + step, count)
            pl.semaphore_signal(
                barrier, 1, device_id=group_device(axes, sizes, peer),
                device_id_type=pl.DeviceIdType.MESH,
            )
        pl.semaphore_wait(barrier, count - 1)
        copies = []
        for step in range(1, count):
            peer = lax.rem(me + step, count)
            copy = pltpu.make_async_remote_copy(
                src_ref=x_ref if gather else x_ref.at[peer],
                dst_ref=o_ref.at[me],
                send_sem=send_sem.at[step],
                recv_sem=recv_sem.at[step],
                device_id=group_device(axes, sizes, peer),
                device_id_type=pl.DeviceIdType.MESH,
            )
            copy.start()
            copies.append(copy)
        own = x_ref[...] if gather else x_ref[me]
        o_ref[me] = own
        for copy in copies:
            copy.wait_send()
        for step in range(1, count):
            source = lax.rem(me + count - step, count)
            pltpu.make_async_remote_copy(
                src_ref=x_ref if gather else x_ref.at[source],
                dst_ref=o_ref.at[source],
                send_sem=send_sem.at[step],
                recv_sem=recv_sem.at[step],
                device_id=group_device(axes, sizes, source),
                device_id_type=pl.DeviceIdType.MESH,
            ).wait_recv()

    return pl.pallas_call(
        kernel,
        out_shape=jax.ShapeDtypeStruct((count,) + tuple(piece_shape), pieces.dtype),
        in_specs=[pl.BlockSpec(memory_space=pltpu.VMEM)],
        out_specs=pl.BlockSpec(memory_space=pltpu.VMEM),
        scratch_shapes=[pltpu.SemaphoreType.DMA((count,)), pltpu.SemaphoreType.DMA((count,))],
        compiler_params=pltpu.CompilerParams(collective_id=tag, has_side_effects=True),
    )(pieces)


def focal_rows(pieces, weights, norm_scale, tag):
    count, sizes = group_of(("gy",))
    rows, width = pieces.shape[1:]

    def kernel(x_ref, t_ref, far_ref, o_ref, got, held, send_sem, recv_sem):
        me = lax.axis_index("gy")
        barrier = pltpu.get_barrier_semaphore()
        for step in range(1, count):
            pl.semaphore_signal(
                barrier, 1, device_id=(lax.axis_index("gx"), lax.rem(me + step, count)),
                device_id_type=pl.DeviceIdType.MESH,
            )
        pl.semaphore_wait(barrier, count - 1)

        def spread(phase, source_of):
            copies = []
            for step in range(1, count):
                peer = lax.rem(me + step, count)
                copy = pltpu.make_async_remote_copy(
                    src_ref=source_of(peer),
                    dst_ref=(got if phase == 0 else o_ref).at[me],
                    send_sem=send_sem.at[phase * count + step],
                    recv_sem=recv_sem.at[phase * count + step],
                    device_id=(lax.axis_index("gx"), peer),
                    device_id_type=pl.DeviceIdType.MESH,
                )
                copy.start()
                copies.append(copy)
            for copy in copies:
                copy.wait_send()
            for step in range(1, count):
                source = lax.rem(me + count - step, count)
                pltpu.make_async_remote_copy(
                    src_ref=source_of(source),
                    dst_ref=(got if phase == 0 else o_ref).at[source],
                    send_sem=send_sem.at[phase * count + step],
                    recv_sem=recv_sem.at[phase * count + step],
                    device_id=(lax.axis_index("gx"), source),
                    device_id_type=pl.DeviceIdType.MESH,
                ).wait_recv()

        got[me] = x_ref[me]
        spread(0, lambda peer: x_ref.at[peer])
        total = got[0]
        for source in range(1, count):
            total = total + got[source]
        far = norm_scale * total
        far_ref[...] = far
        odd = lax.broadcasted_iota(jnp.int32, far.shape, 0) % 2 == 1
        scaled = t_ref[...] * far
        weighted = jnp.where(odd, -scaled, scaled)
        held[...] = weighted
        o_ref[me] = weighted
        spread(1, lambda peer: held)

    return pl.pallas_call(
        kernel,
        out_shape=(
            jax.ShapeDtypeStruct((rows, width), jnp.float32),
            jax.ShapeDtypeStruct((count, rows, width), jnp.float32),
        ),
        in_specs=[pl.BlockSpec(memory_space=pltpu.VMEM)] * 2,
        out_specs=(pl.BlockSpec(memory_space=pltpu.VMEM),) * 2,
        scratch_shapes=[
            pltpu.VMEM((count, rows, width), jnp.float32),
            pltpu.VMEM((rows, width), jnp.float32),
            pltpu.SemaphoreType.DMA((2 * count,)),
            pltpu.SemaphoreType.DMA((2 * count,)),
        ],
        compiler_params=pltpu.CompilerParams(collective_id=tag, has_side_effects=True),
    )(pieces, weights)


def kernel_table(count_out, count_in, offset, length):
    focal_pos = (jnp.arange(count_out, dtype=jnp.float32) + 0.5) / count_out - 0.5
    cell_pos = (
        offset.astype(jnp.float32) + jnp.arange(length, dtype=jnp.float32) + 0.5
    ) / count_in - 0.5
    phase = math.pi * count_out * (focal_pos[:, None] - cell_pos[None, :]) ** 2
    return (jnp.cos(phase), jnp.sin(phase))


def contract(pattern, first_op, second_op):
    return jnp.einsum(pattern, first_op, second_op, precision=lax.Precision.HIGHEST)


def route_pillars(rows, slot_ids, devices, capacity):
    slots = devices * capacity
    placing = (slot_ids[:, None] == jnp.arange(slots, dtype=jnp.int32)[None, :]).astype(
        jnp.float32
    )
    packed = contract("ps,pk->sk", placing, rows)
    got = exchange(packed.reshape(devices, capacity, rows.shape[1]), ("gx", "gy"), False, 0)
    return placing, got.reshape(slots, rows.shape[1])


def shards(fields, eps_background, target, widths, intersection, pillar_tile, anchors):
    span_x = lax.axis_size("gx")
    span_y = lax.axis_size("gy")
    devices = span_x * span_y
    place_x = lax.axis_index("gx")
    place_y = lax.axis_index("gy")
    linear = place_x * span_y + place_y
    offsets = jnp.arange(16, dtype=jnp.int32)
    capacity = 2 * max(1, P_DEV // devices)
    target_tile = pillar_tile[:, 0]
    onehot = (target_tile[:, None] == jnp.arange(devices, dtype=jnp.int32)[None, :]).astype(
        jnp.int32
    )
    earlier = jnp.cumsum(onehot, axis=0) - onehot
    order_in = jnp.sum(earlier * onehot, axis=1)
    slot_ids = target_tile * capacity + order_in
    rows = jnp.concatenate(
        [intersection * widths[:, None], anchors.astype(jnp.float32)], axis=1
    )
    placing, got = route_pillars(rows, slot_ids, devices, capacity)
    local_vals = got[:, :16]
    local_at = got[:, 16:18].astype(jnp.int32)
    cells_x = (local_at[:, 0:1] + (offsets // 4)[None, :]).reshape(-1)
    cells_y = (local_at[:, 1:2] + (offsets % 4)[None, :]).reshape(-1)
    lanes = jnp.arange(TILE, dtype=jnp.int32)
    pick_x = (cells_x[:, None] == lanes[None, :]).astype(jnp.float32)
    pick_y = (cells_y[:, None] == lanes[None, :]).astype(jnp.float32)
    filling = contract("sx,sy->xy", pick_x, pick_y * local_vals.reshape(-1)[:, None])
    z_index = jnp.arange(fields.shape[3], dtype=jnp.int32)
    layers = ((z_index >= ZM - ZP) & (z_index < ZM)).astype(jnp.float32)
    permittivity = eps_background + DELTA_EPS * filling[:, :, None] * layers[None, None, :]
    inv_eps = 1.0 / permittivity
    final_fields, e_steps = run_leaps(fields, inv_eps, None, None, 10)
    mon_re = jnp.zeros((2, TILE, TILE), jnp.float32)
    mon_im = jnp.zeros((2, TILE, TILE), jnp.float32)
    for moment in range(1, NT + 1):
        monitor = e_steps[moment - 1, 0:2, :, :, ZM]
        mon_re = mon_re + math.cos(ANGULAR_STEP * moment) * monitor
        mon_im = mon_im - math.sin(ANGULAR_STEP * moment) * monitor
    norm_scale = (TILE * span_x * TILE * span_y) ** (-0.5)
    x_re, x_im = kernel_table(U, TILE * span_x, place_x * TILE, TILE)
    y_re, y_im = kernel_table(V, TILE * span_y, place_y * TILE, TILE)
    part = jnp.stack(
        [
            contract("ux,cxy->ucy", x_re, mon_re) - contract("ux,cxy->ucy", x_im, mon_im),
            contract("ux,cxy->ucy", x_re, mon_im) + contract("ux,cxy->ucy", x_im, mon_re),
        ]
    )
    chunk_u = U // span_x
    part = part.reshape(2, span_x, chunk_u, 2, TILE).transpose(1, 2, 0, 3, 4)
    part = exchange(part.reshape(span_x, chunk_u, 4 * TILE), ("gx",), False, 1)
    part = jnp.sum(part, axis=0).reshape(chunk_u, 2, 2, TILE)
    part_re, part_im = part[:, 0], part[:, 1]
    far = jnp.stack(
        [
            contract("ucy,vy->cuv", part_re, y_re) - contract("ucy,vy->cuv", part_im, y_im),
            contract("ucy,vy->cuv", part_re, y_im) + contract("ucy,vy->cuv", part_im, y_re),
        ],
        axis=2,
    )
    row_count = U // devices
    far = far.reshape(2, span_y, row_count, 2, V).transpose(1, 0, 2, 3, 4)
    mine_target = lax.dynamic_slice_in_dim(target, linear * row_count, row_count, 0)
    row_weights = jnp.broadcast_to(mine_target[None, :, None, :], (2, row_count, 2, V))
    far, weighted = focal_rows(
        far.reshape(span_y, 2 * row_count * 2, V),
        row_weights.reshape(2 * row_count * 2, V),
        norm_scale,
        2,
    )
    far = far.reshape(2, row_count, 2, V)
    focal_power = jnp.sum(far * far, axis=(0, 2))
    weighted = weighted.reshape(span_y, 2, row_count, 2, V).transpose(1, 0, 2, 3, 4)
    weighted = weighted.reshape(2, span_y * row_count, 2, V)
    w_re, w_im = weighted[:, :, 0], weighted[:, :, 1]
    half = jnp.stack(
        [
            contract("cuv,vy->cuy", w_re, y_re) - contract("cuv,vy->cuy", w_im, y_im),
            contract("cuv,vy->cuy", w_re, y_im) + contract("cuv,vy->cuy", w_im, y_re),
        ]
    )
    half = half.transpose(2, 0, 1, 3).reshape(chunk_u, 4 * TILE)
    half = exchange(half, ("gx",), True, 4)
    half = half.reshape(span_x * chunk_u, 2, 2, TILE).transpose(1, 2, 0, 3)
    half_re, half_im = half[0], half[1]
    back_re = 2.0 * norm_scale * (
        contract("ux,cuy->cxy", x_re, half_re) - contract("ux,cuy->cxy", x_im, half_im)
    )
    back_im = 2.0 * norm_scale * (
        contract("ux,cuy->cxy", x_re, half_im) + contract("ux,cuy->cxy", x_im, half_re)
    )
    drives = []
    for moment in range(1, NT + 1):
        source_step = NT + 1 - moment
        adj_drive = (
            math.cos(ANGULAR_STEP * source_step) * back_re
            + math.sin(ANGULAR_STEP * source_step) * back_im
        )
        drives.append(adj_drive)
    drive = jnp.stack(drives)
    z_index = jnp.arange(fields.shape[3], dtype=jnp.int32)
    drive = jnp.where(z_index == ZM, drive[..., None], 0.0)
    grad_eps = run_leaps(fields, inv_eps, e_steps, drive, 11)
    column_grad = jnp.sum(grad_eps[:, :, ZM - ZP : ZM], axis=2)
    spread = contract("sx,xy->sy", pick_x, column_grad)
    picked = jnp.sum(spread * pick_y, axis=1).reshape(devices * capacity, 16)
    returned = exchange(picked.reshape(devices, capacity, 16), ("gx", "gy"), False, 5)
    own_vals = contract("ps,sk->pk", placing, returned.reshape(devices * capacity, 16))
    grad_widths = DELTA_EPS * jnp.sum(intersection * own_vals, axis=1)
    return (final_fields, focal_power, grad_widths)


def solution(mesh):
    placed = (
        P(None, "gx", "gy", None),
        P("gx", "gy", None),
        P(),
        P(("gx", "gy")),
        P(("gx", "gy"), None),
        P(("gx", "gy"), None),
        P(("gx", "gy"), None),
    )
    return jax.shard_map(
        shards,
        mesh=mesh,
        in_specs=placed,
        out_specs=(P(None, "gx", "gy", None), P(("gx", "gy"), None), P(("gx", "gy"))),
        check_vma=False,
    )
```

```python
import math

import jax
import jax.numpy as jnp
from jax import lax
from jax.sharding import PartitionSpec as P
from jax.experimental import pallas as pl
from jax.experimental.pallas import tpu as pltpu

TILE = 32
P_DEV = 128
NT = 4
ZP = 4
U = 256
V = 256
ZM = 64


COURANT = 0.5
ANGULAR_STEP = 0.9
DELTA_EPS = 4.0


def passed_along(shard, axis, by):
    count = lax.axis_size(axis)
    pairs = [(i, i + by) for i in range(count) if 0 <= i + by < count]
    return lax.ppermute(shard, axis, pairs)


def plus_diff(field, rim_layer, axis):
    extended = jnp.concatenate([field, rim_layer], axis=axis)
    return lax.slice_in_dim(extended, 1, extended.shape[axis], axis=axis) - field


def minus_diff(field, rim_layer, axis):
    extended = jnp.concatenate([rim_layer, field], axis=axis)
    return field - lax.slice_in_dim(extended, 0, field.shape[axis], axis=axis)


def leap_step(fields_now, inv_eps, sources):
    elec_x, elec_y, elec_z, magn_x, magn_y, magn_z = fields_now
    z_blank = jnp.zeros_like(elec_x[:, :, :1])
    rim_east = passed_along(jnp.stack([elec_y[:1], elec_z[:1]]), "gx", -1)
    rim_north = passed_along(jnp.stack([elec_x[:, :1], elec_z[:, :1]]), "gy", -1)
    curl_x = plus_diff(elec_z, rim_north[1], 1) - plus_diff(elec_y, z_blank, 2)
    curl_y = plus_diff(elec_x, z_blank, 2) - plus_diff(elec_z, rim_east[1], 0)
    curl_z = plus_diff(elec_y, rim_east[0], 0) - plus_diff(elec_x, rim_north[0], 1)
    magn_x = magn_x - COURANT * curl_x
    magn_y = magn_y - COURANT * curl_y
    magn_z = magn_z - COURANT * curl_z
    rim_west = passed_along(jnp.stack([magn_y[-1:], magn_z[-1:]]), "gx", 1)
    rim_south = passed_along(jnp.stack([magn_x[:, -1:], magn_z[:, -1:]]), "gy", 1)
    curl_x = minus_diff(magn_z, rim_south[1], 1) - minus_diff(magn_y, z_blank, 2)
    curl_y = minus_diff(magn_x, z_blank, 2) - minus_diff(magn_z, rim_west[1], 0)
    curl_z = minus_diff(magn_y, rim_west[0], 0) - minus_diff(magn_x, rim_south[0], 1)
    elec_x = elec_x + COURANT * (curl_x - sources[0]) * inv_eps
    elec_y = elec_y + COURANT * (curl_y - sources[1]) * inv_eps
    elec_z = elec_z + COURANT * curl_z * inv_eps
    return (elec_x, elec_y, elec_z, magn_x, magn_y, magn_z)


def run_leaps(fields, inv_eps, history, drive, tag):
    span_x = lax.axis_size("gx")
    span_y = lax.axis_size("gy")
    size_x, size_y, size_z = inv_eps.shape
    half = size_x // 2
    adjoint = history is not None
    mesh_id = pl.DeviceIdType.MESH
    order_h = list(range(half - 1, size_x - 1)) + list(range(0, half - 1)) + [size_x - 1]
    order_e = list(range(half - 1, size_x - 1)) + list(range(1, half - 1)) + [size_x - 1, 0]
    slot_h = {x: i for i, x in enumerate(order_h)}
    slot_e = {x: i for i, x in enumerate(order_e)}

    def kernel(*refs):
        refs = list(refs)
        if adjoint:
            f_in, hist, eps_ref, drv, acc = refs[:5]
            a_hist, h_state = refs[5:7]
            rest = refs[7:]
        else:
            f_in, eps_ref, final, e_hist = refs[:4]
            rest = refs[4:]
        east, north, west, south, xs_e, ys_e, xs_h, ys_h, ssem, rsem = rest
        px = lax.axis_index("gx")
        py = lax.axis_index("gy")
        barrier = pltpu.get_barrier_semaphore()
        for peer in (
            (lax.rem(px + 1, span_x), py),
            (lax.rem(px + span_x - 1, span_x), py),
            (px, lax.rem(py + 1, span_y)),
            (px, lax.rem(py + span_y - 1, span_y)),
        ):
            pl.semaphore_signal(barrier, 1, device_id=peer, device_id_type=mesh_id)
        pl.semaphore_wait(barrier, 4)
        has_east = px < span_x - 1
        has_west = px > 0
        has_north = py < span_y - 1
        has_south = py > 0
        west_dev = (lax.rem(px + span_x - 1, span_x), py)
        east_dev = (lax.rem(px + 1, span_x), py)
        south_dev = (px, lax.rem(py + span_y - 1, span_y))
        north_dev = (px, lax.rem(py + 1, span_y))
        zero_slab = jnp.zeros((size_y, size_z), jnp.float32)
        iy = lax.broadcasted_iota(jnp.int32, (size_y, size_z), 0)
        iz = lax.broadcasted_iota(jnp.int32, (size_y, size_z), 1)

        for flag, buf in ((has_east, east), (has_north, north), (has_west, west), (has_south, south)):
            @pl.when(jnp.logical_not(flag))
            def _(buf=buf):
                buf[...] = jnp.zeros(buf.shape, jnp.float32)

        def up_y(slab, row):
            return jnp.where(iy == size_y - 1, row, pltpu.roll(slab, size_y - 1, 0))

        def down_y(slab, row):
            return jnp.where(iy == 0, row, pltpu.roll(slab, 1, 0))

        def up_z(slab):
            return jnp.where(iz == size_z - 1, 0.0, pltpu.roll(slab, size_z - 1, 1))

        def down_z(slab):
            return jnp.where(iz == 0, 0.0, pltpu.roll(slab, 1, 1))

        def load_e(step, comp, x):
            if step == 0:
                return zero_slab if adjoint else f_in[comp, x]
            if adjoint:
                return a_hist[(step - 1) % 2, comp, x]
            return e_hist[step - 1, comp, x]

        def store_e(step, comp, x, value):
            if adjoint:
                a_hist[step % 2, comp, x] = value
            else:
                e_hist[step, comp, x] = value
                if step == NT - 1:
                    final[comp, x] = value

        def load_h(step, comp, x):
            if adjoint and step <= 1:
                return zero_slab
            if step == 0:
                return f_in[3 + comp, x]
            return h_state[comp, x] if adjoint else final[3 + comp, x]

        def store_h(comp, x, value):
            if adjoint:
                h_state[comp, x] = value
            else:
                final[3 + comp, x] = value

        def forward_e(n, comp, x):
            return f_in[comp, x] if n == 0 else hist[n - 1, comp, x]

        sent = []

        def link(src, dst, sem, device, sends):
            copy = pltpu.make_async_remote_copy(
                src_ref=src, dst_ref=dst, send_sem=ssem.at[sem], recv_sem=rsem.at[sem],
                device_id=device, device_id_type=mesh_id,
            )
            pl.when(sends)(copy.start)
            sent.append((copy, sends))
            return copy

        def wait_for(src, dst, sem, device, gets):
            copy = pltpu.make_async_remote_copy(
                src_ref=src, dst_ref=dst, send_sem=ssem.at[sem], recv_sem=rsem.at[sem],
                device_id=device, device_id_type=mesh_id,
            )
            pl.when(gets)(copy.wait_recv)

        def send_e_rows(step, chunk):
            link(ys_e.at[step, chunk], north.at[step, chunk], 6 * step + chunk, south_dev, has_south)

        def send_e_slab(step):
            link(xs_e.at[step], east.at[step], 6 * step + 2, west_dev, has_west)

        def get_e_rows(step, chunk):
            wait_for(ys_e.at[step, chunk], north.at[step, chunk], 6 * step + chunk, north_dev, has_north)

        def get_e_slab(step):
            wait_for(xs_e.at[step], east.at[step], 6 * step + 2, east_dev, has_east)

        def send_h_rows(step, chunk):
            link(ys_h.at[step, chunk], south.at[step, chunk], 6 * step + 3 + chunk, north_dev, has_north)

        def send_h_slab(step):
            link(xs_h.at[step], west.at[step], 6 * step + 5, east_dev, has_east)

        def get_h_rows(step, chunk):
            wait_for(ys_h.at[step, chunk], south.at[step, chunk], 6 * step + 3 + chunk, south_dev, has_south)

        def get_h_slab(step):
            wait_for(xs_h.at[step], west.at[step], 6 * step + 5, west_dev, has_west)

        def e_row_ref(buf, step, comp, x):
            slot = slot_e[x]
            return buf[step, slot // half, comp, pl.ds(slot % half, 1), :]

        def h_row_ref(buf, step, comp, x):
            slot = slot_h[x]
            return buf[step, slot // half, comp, pl.ds(slot % half, 1), :]

        def stage_e_rows(step, x, ex, ez):
            slot = slot_e[x]
            ys_e[step, slot // half, 0, pl.ds(slot % half, 1), :] = ex[0:1, :]
            ys_e[step, slot // half, 1, pl.ds(slot % half, 1), :] = ez[0:1, :]

        if not adjoint:
            xs_e[0, 0] = f_in[1, 0]
            xs_e[0, 1] = f_in[2, 0]
            for x in order_e:
                stage_e_rows(0, x, f_in[0, x], f_in[2, x])
            send_e_rows(0, 0)
            send_e_rows(0, 1)
            send_e_slab(0)

        def magnetic(step, x):
            ex = load_e(step, 0, x)
            ey = load_e(step, 1, x)
            ez = load_e(step, 2, x)
            if x + 1 < size_x:
                ey_next = load_e(step, 1, x + 1)
                ez_next = load_e(step, 2, x + 1)
            else:
                ey_next = east[step, 0]
                ez_next = east[step, 1]
            nx_row = e_row_ref(north, step, 0, x)
            nz_row = e_row_ref(north, step, 1, x)
            curl_x = (up_y(ez, nz_row) - ez) - (up_z(ey) - ey)
            curl_y = (up_z(ex) - ex) - (ez_next - ez)
            curl_z = (ey_next - ey) - (up_y(ex, nx_row) - ex)
            hx = load_h(step, 0, x) - COURANT * curl_x
            hy = load_h(step, 1, x) - COURANT * curl_y
            hz = load_h(step, 2, x) - COURANT * curl_z
            store_h(0, x, hx)
            store_h(1, x, hy)
            store_h(2, x, hz)
            slot = slot_h[x]
            ys_h[step, slot // half, 0, pl.ds(slot % half, 1), :] = hx[size_y - 1 : size_y, :]
            ys_h[step, slot // half, 1, pl.ds(slot % half, 1), :] = hz[size_y - 1 : size_y, :]
            if x == size_x - 1:
                xs_h[step, 0] = hy
                xs_h[step, 1] = hz

        def electric(step, x, skip_magnetic):
            if skip_magnetic:
                curl_x = curl_y = curl_z = zero_slab
            else:
                hx = load_h(step + 1, 0, x)
                hy = load_h(step + 1, 1, x)
                hz = load_h(step + 1, 2, x)
                if x > 0:
                    hy_prev = load_h(step + 1, 1, x - 1)
                    hz_prev = load_h(step + 1, 2, x - 1)
                else:
                    hy_prev = west[step, 0]
                    hz_prev = west[step, 1]
                sx_row = h_row_ref(south, step, 0, x)
                sz_row = h_row_ref(south, step, 1, x)
                curl_x = (hz - down_y(hz, sz_row)) - (hy - down_z(hy))
                curl_y = (hx - down_z(hx)) - (hz - hz_prev)
                curl_z = (hy - hy_prev) - (hx - down_y(hx, sx_row))
            if adjoint:
                curl_x = curl_x - drv[step, 0, x]
                curl_y = curl_y - drv[step, 1, x]
            scale = eps_ref[x]
            ex = load_e(step, 0, x) + COURANT * curl_x * scale
            ey = load_e(step, 1, x) + COURANT * curl_y * scale
            ez = load_e(step, 2, x) + COURANT * curl_z * scale
            store_e(step, 0, x, ex)
            store_e(step, 1, x, ey)
            store_e(step, 2, x, ez)
            if adjoint:
                moment = NT - step
                product = (
                    ex * (forward_e(moment, 0, x) - forward_e(moment - 1, 0, x))
                    + ey * (forward_e(moment, 1, x) - forward_e(moment - 1, 1, x))
                    + ez * (forward_e(moment, 2, x) - forward_e(moment - 1, 2, x))
                )
                before = zero_slab if step == 0 else acc[x]
                acc[x] = before - product * scale
            if step + 1 < NT:
                stage_e_rows(step + 1, x, ex, ez)
                if x == 0:
                    xs_e[step + 1, 0] = ey
                    xs_e[step + 1, 1] = ez

        for step in range(NT):
            skip_magnetic = adjoint and step == 0
            if not skip_magnetic:
                get_e_rows(step, 0)
                for x in order_h[:half]:
                    magnetic(step, x)
                send_h_rows(step, 0)
                get_e_rows(step, 1)
                for x in order_h[half:-1]:
                    magnetic(step, x)
                get_e_slab(step)
                magnetic(step, order_h[-1])
                send_h_rows(step, 1)
                send_h_slab(step)
                get_h_rows(step, 0)
            for x in order_e[:half]:
                electric(step, x, skip_magnetic)
            if step + 1 < NT:
                send_e_rows(step + 1, 0)
            if not skip_magnetic:
                get_h_rows(step, 1)
            for x in order_e[half:-1]:
                electric(step, x, skip_magnetic)
            if not skip_magnetic:
                get_h_slab(step)
            electric(step, order_e[-1], skip_magnetic)
            if step + 1 < NT:
                send_e_rows(step + 1, 1)
                send_e_slab(step + 1)

        for copy, sends in sent:
            pl.when(sends)(copy.wait_send)

    rim_x = pltpu.VMEM((NT, 2, size_y, size_z), jnp.float32)
    rim_y = pltpu.VMEM((NT, 2, 2, half, size_z), jnp.float32)
    field_shape = (size_x, size_y, size_z)
    if adjoint:
        operands = [fields, history, inv_eps, drive]
        out_shape = jax.ShapeDtypeStruct(field_shape, jnp.float32)
        out_specs = pl.BlockSpec(memory_space=pltpu.VMEM)
        state = [
            pltpu.VMEM((2, 3) + field_shape, jnp.float32),
            pltpu.VMEM((3,) + field_shape, jnp.float32),
        ]
    else:
        operands = [fields, inv_eps]
        out_shape = (
            jax.ShapeDtypeStruct((6,) + field_shape, jnp.float32),
            jax.ShapeDtypeStruct((NT, 3) + field_shape, jnp.float32),
        )
        out_specs = (pl.BlockSpec(memory_space=pltpu.VMEM),) * 2
        state = []
    return pl.pallas_call(
        kernel,
        out_shape=out_shape,
        in_specs=[pl.BlockSpec(memory_space=pltpu.VMEM)] * len(operands),
        out_specs=out_specs,
        scratch_shapes=state + [
            rim_x, rim_y, rim_x, rim_y, rim_x, rim_y, rim_x, rim_y,
            pltpu.SemaphoreType.DMA((6 * NT,)),
            pltpu.SemaphoreType.DMA((6 * NT,)),
        ],
        compiler_params=pltpu.CompilerParams(
            collective_id=tag, has_side_effects=True, vmem_limit_bytes=56 * 1024 * 1024
        ),
    )(*operands)


def group_of(axes):
    sizes = [lax.axis_size(a) for a in axes]
    count = math.prod(sizes)
    return count, sizes


def group_place(axes, sizes):
    place = 0
    for axis, size in zip(axes, sizes):
        place = place * size + lax.axis_index(axis)
    return place


def group_device(axes, sizes, peer):
    coords = {}
    rest = peer
    for axis, size in reversed(list(zip(axes, sizes))):
        coords[axis] = rest % size
        rest = rest // size
    return tuple(coords[a] if a in coords else lax.axis_index(a) for a in ("gx", "gy"))


def exchange(pieces, axes, gather, tag):
    count, sizes = group_of(axes)
    piece_shape = pieces.shape if gather else pieces.shape[1:]

    def kernel(x_ref, o_ref, send_sem, recv_sem):
        me = group_place(axes, sizes)
        barrier = pltpu.get_barrier_semaphore()
        for step in range(1, count):
            peer = lax.rem(me + step, count)
            pl.semaphore_signal(
                barrier, 1, device_id=group_device(axes, sizes, peer),
                device_id_type=pl.DeviceIdType.MESH,
            )
        pl.semaphore_wait(barrier, count - 1)
        copies = []
        for step in range(1, count):
            peer = lax.rem(me + step, count)
            copy = pltpu.make_async_remote_copy(
                src_ref=x_ref if gather else x_ref.at[peer],
                dst_ref=o_ref.at[me],
                send_sem=send_sem.at[step],
                recv_sem=recv_sem.at[step],
                device_id=group_device(axes, sizes, peer),
                device_id_type=pl.DeviceIdType.MESH,
            )
            copy.start()
            copies.append(copy)
        own = x_ref[...] if gather else x_ref[me]
        o_ref[me] = own
        for copy in copies:
            copy.wait_send()
        for step in range(1, count):
            source = lax.rem(me + count - step, count)
            pltpu.make_async_remote_copy(
                src_ref=x_ref if gather else x_ref.at[source],
                dst_ref=o_ref.at[source],
                send_sem=send_sem.at[step],
                recv_sem=recv_sem.at[step],
                device_id=group_device(axes, sizes, source),
                device_id_type=pl.DeviceIdType.MESH,
            ).wait_recv()

    return pl.pallas_call(
        kernel,
        out_shape=jax.ShapeDtypeStruct((count,) + tuple(piece_shape), pieces.dtype),
        in_specs=[pl.BlockSpec(memory_space=pltpu.VMEM)],
        out_specs=pl.BlockSpec(memory_space=pltpu.VMEM),
        scratch_shapes=[pltpu.SemaphoreType.DMA((count,)), pltpu.SemaphoreType.DMA((count,))],
        compiler_params=pltpu.CompilerParams(collective_id=tag, has_side_effects=True),
    )(pieces)


def focal_rows(pieces, weights, norm_scale, tag):
    count, sizes = group_of(("gy",))
    rows, width = pieces.shape[1:]

    def kernel(x_ref, t_ref, far_ref, o_ref, got, held, send_sem, recv_sem):
        me = lax.axis_index("gy")
        barrier = pltpu.get_barrier_semaphore()
        for step in range(1, count):
            pl.semaphore_signal(
                barrier, 1, device_id=(lax.axis_index("gx"), lax.rem(me + step, count)),
                device_id_type=pl.DeviceIdType.MESH,
            )
        pl.semaphore_wait(barrier, count - 1)

        def spread(phase, source_of):
            copies = []
            for step in range(1, count):
                peer = lax.rem(me + step, count)
                copy = pltpu.make_async_remote_copy(
                    src_ref=source_of(peer),
                    dst_ref=(got if phase == 0 else o_ref).at[me],
                    send_sem=send_sem.at[phase * count + step],
                    recv_sem=recv_sem.at[phase * count + step],
                    device_id=(lax.axis_index("gx"), peer),
                    device_id_type=pl.DeviceIdType.MESH,
                )
                copy.start()
                copies.append(copy)
            for copy in copies:
                copy.wait_send()
            for step in range(1, count):
                source = lax.rem(me + count - step, count)
                pltpu.make_async_remote_copy(
                    src_ref=source_of(source),
                    dst_ref=(got if phase == 0 else o_ref).at[source],
                    send_sem=send_sem.at[phase * count + step],
                    recv_sem=recv_sem.at[phase * count + step],
                    device_id=(lax.axis_index("gx"), source),
                    device_id_type=pl.DeviceIdType.MESH,
                ).wait_recv()

        got[me] = x_ref[me]
        spread(0, lambda peer: x_ref.at[peer])
        total = got[0]
        for source in range(1, count):
            total = total + got[source]
        far = norm_scale * total
        far_ref[...] = far
        odd = lax.broadcasted_iota(jnp.int32, far.shape, 0) % 2 == 1
        scaled = t_ref[...] * far
        weighted = jnp.where(odd, -scaled, scaled)
        held[...] = weighted
        o_ref[me] = weighted
        spread(1, lambda peer: held)

    return pl.pallas_call(
        kernel,
        out_shape=(
            jax.ShapeDtypeStruct((rows, width), jnp.float32),
            jax.ShapeDtypeStruct((count, rows, width), jnp.float32),
        ),
        in_specs=[pl.BlockSpec(memory_space=pltpu.VMEM)] * 2,
        out_specs=(pl.BlockSpec(memory_space=pltpu.VMEM),) * 2,
        scratch_shapes=[
            pltpu.VMEM((count, rows, width), jnp.float32),
            pltpu.VMEM((rows, width), jnp.float32),
            pltpu.SemaphoreType.DMA((2 * count,)),
            pltpu.SemaphoreType.DMA((2 * count,)),
        ],
        compiler_params=pltpu.CompilerParams(collective_id=tag, has_side_effects=True),
    )(pieces, weights)


def kernel_table(count_out, count_in, offset, length):
    focal_pos = (jnp.arange(count_out, dtype=jnp.float32) + 0.5) / count_out - 0.5
    cell_pos = (
        offset.astype(jnp.float32) + jnp.arange(length, dtype=jnp.float32) + 0.5
    ) / count_in - 0.5
    phase = math.pi * count_out * (focal_pos[:, None] - cell_pos[None, :]) ** 2
    return (jnp.cos(phase), jnp.sin(phase))


def contract(pattern, first_op, second_op):
    return jnp.einsum(pattern, first_op, second_op, precision=lax.Precision.HIGHEST)


def route_pillars(rows, slot_ids, devices, capacity):
    slots = devices * capacity
    placing = (slot_ids[:, None] == jnp.arange(slots, dtype=jnp.int32)[None, :]).astype(
        jnp.float32
    )
    packed = contract("ps,pk->sk", placing, rows)
    got = exchange(packed.reshape(devices, capacity, rows.shape[1]), ("gx", "gy"), False, 0)
    return placing, got.reshape(slots, rows.shape[1])


def shards(fields, eps_background, target, widths, intersection, pillar_tile, anchors):
    span_x = lax.axis_size("gx")
    span_y = lax.axis_size("gy")
    devices = span_x * span_y
    place_x = lax.axis_index("gx")
    place_y = lax.axis_index("gy")
    linear = place_x * span_y + place_y
    offsets = jnp.arange(16, dtype=jnp.int32)
    capacity = 2 * max(1, P_DEV // devices)
    target_tile = pillar_tile[:, 0]
    onehot = (target_tile[:, None] == jnp.arange(devices, dtype=jnp.int32)[None, :]).astype(
        jnp.int32
    )
    earlier = jnp.cumsum(onehot, axis=0) - onehot
    order_in = jnp.sum(earlier * onehot, axis=1)
    slot_ids = target_tile * capacity + order_in
    rows = jnp.concatenate(
        [intersection * widths[:, None], anchors.astype(jnp.float32)], axis=1
    )
    placing, got = route_pillars(rows, slot_ids, devices, capacity)
    local_vals = got[:, :16]
    local_at = got[:, 16:18].astype(jnp.int32)
    cells_x = (local_at[:, 0:1] + (offsets // 4)[None, :]).reshape(-1)
    cells_y = (local_at[:, 1:2] + (offsets % 4)[None, :]).reshape(-1)
    lanes = jnp.arange(TILE, dtype=jnp.int32)
    pick_x = (cells_x[:, None] == lanes[None, :]).astype(jnp.float32)
    pick_y = (cells_y[:, None] == lanes[None, :]).astype(jnp.float32)
    filling = contract("sx,sy->xy", pick_x, pick_y * local_vals.reshape(-1)[:, None])
    z_index = jnp.arange(fields.shape[3], dtype=jnp.int32)
    layers = ((z_index >= ZM - ZP) & (z_index < ZM)).astype(jnp.float32)
    permittivity = eps_background + DELTA_EPS * filling[:, :, None] * layers[None, None, :]
    inv_eps = 1.0 / permittivity
    final_fields, e_steps = run_leaps(fields, inv_eps, None, None, 10)
    mon_re = jnp.zeros((2, TILE, TILE), jnp.float32)
    mon_im = jnp.zeros((2, TILE, TILE), jnp.float32)
    for moment in range(1, NT + 1):
        monitor = e_steps[moment - 1, 0:2, :, :, ZM]
        mon_re = mon_re + math.cos(ANGULAR_STEP * moment) * monitor
        mon_im = mon_im - math.sin(ANGULAR_STEP * moment) * monitor
    norm_scale = (TILE * span_x * TILE * span_y) ** (-0.5)
    x_re, x_im = kernel_table(U, TILE * span_x, place_x * TILE, TILE)
    y_re, y_im = kernel_table(V, TILE * span_y, place_y * TILE, TILE)
    part = jnp.stack(
        [
            contract("ux,cxy->ucy", x_re, mon_re) - contract("ux,cxy->ucy", x_im, mon_im),
            contract("ux,cxy->ucy", x_re, mon_im) + contract("ux,cxy->ucy", x_im, mon_re),
        ]
    )
    chunk_u = U // span_x
    part = part.reshape(2, span_x, chunk_u, 2, TILE).transpose(1, 2, 0, 3, 4)
    part = exchange(part.reshape(span_x, chunk_u, 4 * TILE), ("gx",), False, 1)
    part = jnp.sum(part, axis=0).reshape(chunk_u, 2, 2, TILE)
    part_re, part_im = part[:, 0], part[:, 1]
    far = jnp.stack(
        [
            contract("ucy,vy->cuv", part_re, y_re) - contract("ucy,vy->cuv", part_im, y_im),
            contract("ucy,vy->cuv", part_re, y_im) + contract("ucy,vy->cuv", part_im, y_re),
        ],
        axis=2,
    )
    row_count = U // devices
    far = far.reshape(2, span_y, row_count, 2, V).transpose(1, 0, 2, 3, 4)
    mine_target = lax.dynamic_slice_in_dim(target, linear * row_count, row_count, 0)
    row_weights = jnp.broadcast_to(mine_target[None, :, None, :], (2, row_count, 2, V))
    far, weighted = focal_rows(
        far.reshape(span_y, 2 * row_count * 2, V),
        row_weights.reshape(2 * row_count * 2, V),
        norm_scale,
        2,
    )
    far = far.reshape(2, row_count, 2, V)
    focal_power = jnp.sum(far * far, axis=(0, 2))
    weighted = weighted.reshape(span_y, 2, row_count, 2, V).transpose(1, 0, 2, 3, 4)
    weighted = weighted.reshape(2, span_y * row_count, 2, V)
    w_re, w_im = weighted[:, :, 0], weighted[:, :, 1]
    half = jnp.stack(
        [
            contract("cuv,vy->cuy", w_re, y_re) - contract("cuv,vy->cuy", w_im, y_im),
            contract("cuv,vy->cuy", w_re, y_im) + contract("cuv,vy->cuy", w_im, y_re),
        ]
    )
    half = half.transpose(2, 0, 1, 3).reshape(chunk_u, 4 * TILE)
    half = exchange(half, ("gx",), True, 4)
    half = half.reshape(span_x * chunk_u, 2, 2, TILE).transpose(1, 2, 0, 3)
    half_re, half_im = half[0], half[1]
    back_re = 2.0 * norm_scale * (
        contract("ux,cuy->cxy", x_re, half_re) - contract("ux,cuy->cxy", x_im, half_im)
    )
    back_im = 2.0 * norm_scale * (
        contract("ux,cuy->cxy", x_re, half_im) + contract("ux,cuy->cxy", x_im, half_re)
    )
    drives = []
    for moment in range(1, NT + 1):
        source_step = NT + 1 - moment
        adj_drive = (
            math.cos(ANGULAR_STEP * source_step) * back_re
            + math.sin(ANGULAR_STEP * source_step) * back_im
        )
        drives.append(adj_drive)
    drive = jnp.stack(drives)
    z_index = jnp.arange(fields.shape[3], dtype=jnp.int32)
    drive = jnp.where(z_index == ZM, drive[..., None], 0.0)
    grad_eps = run_leaps(fields, inv_eps, e_steps, drive, 11)
    column_grad = jnp.sum(grad_eps[:, :, ZM - ZP : ZM], axis=2)
    spread = contract("sx,xy->sy", pick_x, column_grad)
    picked = jnp.sum(spread * pick_y, axis=1).reshape(devices * capacity, 16)
    returned = exchange(picked.reshape(devices, capacity, 16), ("gx", "gy"), False, 5)
    own_vals = contract("ps,sk->pk", placing, returned.reshape(devices * capacity, 16))
    grad_widths = DELTA_EPS * jnp.sum(intersection * own_vals, axis=1)
    return (final_fields, focal_power, grad_widths)


def solution(mesh):
    placed = (
        P(None, "gx", "gy", None),
        P("gx", "gy", None),
        P(),
        P(("gx", "gy")),
        P(("gx", "gy"), None),
        P(("gx", "gy"), None),
        P(("gx", "gy"), None),
    )
    return jax.shard_map(
        shards,
        mesh=mesh,
        in_specs=placed,
        out_specs=(P(None, "gx", "gy", None), P(("gx", "gy"), None), P(("gx", "gy"))),
        check_vma=False,
    )
```

```python
import math

import jax
import jax.numpy as jnp
from jax import lax
from jax.sharding import PartitionSpec as P
from jax.experimental import pallas as pl
from jax.experimental.pallas import tpu as pltpu

TILE = 32
P_DEV = 128
NT = 4
ZP = 4
U = 256
V = 256
ZM = 64


COURANT = 0.5
ANGULAR_STEP = 0.9
DELTA_EPS = 4.0


def passed_along(shard, axis, by):
    count = lax.axis_size(axis)
    pairs = [(i, i + by) for i in range(count) if 0 <= i + by < count]
    return lax.ppermute(shard, axis, pairs)


def plus_diff(field, rim_layer, axis):
    extended = jnp.concatenate([field, rim_layer], axis=axis)
    return lax.slice_in_dim(extended, 1, extended.shape[axis], axis=axis) - field


def minus_diff(field, rim_layer, axis):
    extended = jnp.concatenate([rim_layer, field], axis=axis)
    return field - lax.slice_in_dim(extended, 0, field.shape[axis], axis=axis)


def leap_step(fields_now, inv_eps, sources):
    elec_x, elec_y, elec_z, magn_x, magn_y, magn_z = fields_now
    z_blank = jnp.zeros_like(elec_x[:, :, :1])
    rim_east = passed_along(jnp.stack([elec_y[:1], elec_z[:1]]), "gx", -1)
    rim_north = passed_along(jnp.stack([elec_x[:, :1], elec_z[:, :1]]), "gy", -1)
    curl_x = plus_diff(elec_z, rim_north[1], 1) - plus_diff(elec_y, z_blank, 2)
    curl_y = plus_diff(elec_x, z_blank, 2) - plus_diff(elec_z, rim_east[1], 0)
    curl_z = plus_diff(elec_y, rim_east[0], 0) - plus_diff(elec_x, rim_north[0], 1)
    magn_x = magn_x - COURANT * curl_x
    magn_y = magn_y - COURANT * curl_y
    magn_z = magn_z - COURANT * curl_z
    rim_west = passed_along(jnp.stack([magn_y[-1:], magn_z[-1:]]), "gx", 1)
    rim_south = passed_along(jnp.stack([magn_x[:, -1:], magn_z[:, -1:]]), "gy", 1)
    curl_x = minus_diff(magn_z, rim_south[1], 1) - minus_diff(magn_y, z_blank, 2)
    curl_y = minus_diff(magn_x, z_blank, 2) - minus_diff(magn_z, rim_west[1], 0)
    curl_z = minus_diff(magn_y, rim_west[0], 0) - minus_diff(magn_x, rim_south[0], 1)
    elec_x = elec_x + COURANT * (curl_x - sources[0]) * inv_eps
    elec_y = elec_y + COURANT * (curl_y - sources[1]) * inv_eps
    elec_z = elec_z + COURANT * curl_z * inv_eps
    return (elec_x, elec_y, elec_z, magn_x, magn_y, magn_z)


def run_leaps(fields, inv_eps, history, drive, tag):
    span_x = lax.axis_size("gx")
    span_y = lax.axis_size("gy")
    size_x, size_y, size_z = inv_eps.shape
    half = size_x // 2
    adjoint = history is not None
    mesh_id = pl.DeviceIdType.MESH
    order_h = list(range(half - 1, size_x - 1)) + list(range(0, half - 1)) + [size_x - 1]
    order_e = list(range(half - 1, size_x - 1)) + list(range(1, half - 1)) + [size_x - 1, 0]
    slot_h = {x: i for i, x in enumerate(order_h)}
    slot_e = {x: i for i, x in enumerate(order_e)}

    def kernel(*refs):
        refs = list(refs)
        if adjoint:
            hist, eps_ref, drv, acc = refs[:4]
            a_hist, h_state = refs[4:6]
            rest = refs[6:]
        else:
            f_in, eps_ref, final, chg, mon = refs[:5]
            a_hist = refs[5]
            rest = refs[6:]
        east, north, west, south, xs_e, ys_e, xs_h, ys_h, ssem, rsem = rest
        px = lax.axis_index("gx")
        py = lax.axis_index("gy")
        barrier = pltpu.get_barrier_semaphore()
        for peer in (
            (lax.rem(px + 1, span_x), py),
            (lax.rem(px + span_x - 1, span_x), py),
            (px, lax.rem(py + 1, span_y)),
            (px, lax.rem(py + span_y - 1, span_y)),
        ):
            pl.semaphore_signal(barrier, 1, device_id=peer, device_id_type=mesh_id)
        pl.semaphore_wait(barrier, 4)
        has_east = px < span_x - 1
        has_west = px > 0
        has_north = py < span_y - 1
        has_south = py > 0
        west_dev = (lax.rem(px + span_x - 1, span_x), py)
        east_dev = (lax.rem(px + 1, span_x), py)
        south_dev = (px, lax.rem(py + span_y - 1, span_y))
        north_dev = (px, lax.rem(py + 1, span_y))
        zero_slab = jnp.zeros((size_y, size_z), jnp.float32)
        iy = lax.broadcasted_iota(jnp.int32, (size_y, size_z), 0)
        iz = lax.broadcasted_iota(jnp.int32, (size_y, size_z), 1)

        for flag, buf in ((has_east, east), (has_north, north), (has_west, west), (has_south, south)):
            @pl.when(jnp.logical_not(flag))
            def _(buf=buf):
                buf[...] = jnp.zeros(buf.shape, jnp.float32)

        def up_y(slab, row):
            return jnp.where(iy == size_y - 1, row, pltpu.roll(slab, size_y - 1, 0))

        def down_y(slab, row):
            return jnp.where(iy == 0, row, pltpu.roll(slab, 1, 0))

        def up_z(slab):
            return jnp.where(iz == size_z - 1, 0.0, pltpu.roll(slab, size_z - 1, 1))

        def down_z(slab):
            return jnp.where(iz == 0, 0.0, pltpu.roll(slab, 1, 1))

        def load_e(step, comp, x):
            if step == 0:
                return zero_slab if adjoint else f_in[comp, x]
            return a_hist[(step - 1) % 2, comp, x]

        def store_e(step, comp, x, value):
            if step == NT - 1 and not adjoint:
                final[comp, x] = value
            else:
                a_hist[step % 2, comp, x] = value

        def load_h(step, comp, x):
            if adjoint and step <= 1:
                return zero_slab
            if step == 0:
                return f_in[3 + comp, x]
            return h_state[comp, x] if adjoint else final[3 + comp, x]

        def store_h(comp, x, value):
            if adjoint:
                h_state[comp, x] = value
            else:
                final[3 + comp, x] = value

        sent = []

        def link(src, dst, sem, device, sends):
            copy = pltpu.make_async_remote_copy(
                src_ref=src, dst_ref=dst, send_sem=ssem.at[sem], recv_sem=rsem.at[sem],
                device_id=device, device_id_type=mesh_id,
            )
            pl.when(sends)(copy.start)
            sent.append((copy, sends))
            return copy

        def wait_for(src, dst, sem, device, gets):
            copy = pltpu.make_async_remote_copy(
                src_ref=src, dst_ref=dst, send_sem=ssem.at[sem], recv_sem=rsem.at[sem],
                device_id=device, device_id_type=mesh_id,
            )
            pl.when(gets)(copy.wait_recv)

        def send_e_rows(step, chunk):
            link(ys_e.at[step, chunk], north.at[step, chunk], 6 * step + chunk, south_dev, has_south)

        def send_e_slab(step):
            link(xs_e.at[step], east.at[step], 6 * step + 2, west_dev, has_west)

        def get_e_rows(step, chunk):
            wait_for(ys_e.at[step, chunk], north.at[step, chunk], 6 * step + chunk, north_dev, has_north)

        def get_e_slab(step):
            wait_for(xs_e.at[step], east.at[step], 6 * step + 2, east_dev, has_east)

        def send_h_rows(step, chunk):
            link(ys_h.at[step, chunk], south.at[step, chunk], 6 * step + 3 + chunk, north_dev, has_north)

        def send_h_slab(step):
            link(xs_h.at[step], west.at[step], 6 * step + 5, east_dev, has_east)

        def get_h_rows(step, chunk):
            wait_for(ys_h.at[step, chunk], south.at[step, chunk], 6 * step + 3 + chunk, south_dev, has_south)

        def get_h_slab(step):
            wait_for(xs_h.at[step], west.at[step], 6 * step + 5, west_dev, has_west)

        def e_row_ref(buf, step, comp, x):
            slot = slot_e[x]
            return buf[step, slot // half, comp, pl.ds(slot % half, 1), :]

        def h_row_ref(buf, step, comp, x):
            slot = slot_h[x]
            return buf[step, slot // half, comp, pl.ds(slot % half, 1), :]

        def stage_e_rows(step, x, ex, ez):
            slot = slot_e[x]
            ys_e[step, slot // half, 0, pl.ds(slot % half, 1), :] = ex[0:1, :]
            ys_e[step, slot // half, 1, pl.ds(slot % half, 1), :] = ez[0:1, :]

        if not adjoint:
            xs_e[0, 0] = f_in[1, 0]
            xs_e[0, 1] = f_in[2, 0]
            for x in order_e:
                stage_e_rows(0, x, f_in[0, x], f_in[2, x])
            send_e_rows(0, 0)
            send_e_rows(0, 1)
            send_e_slab(0)

        def magnetic(step, x):
            ex = load_e(step, 0, x)
            ey = load_e(step, 1, x)
            ez = load_e(step, 2, x)
            if x + 1 < size_x:
                ey_next = load_e(step, 1, x + 1)
                ez_next = load_e(step, 2, x + 1)
            else:
                ey_next = east[step, 0]
                ez_next = east[step, 1]
            nx_row = e_row_ref(north, step, 0, x)
            nz_row = e_row_ref(north, step, 1, x)
            curl_x = (up_y(ez, nz_row) - ez) - (up_z(ey) - ey)
            curl_y = (up_z(ex) - ex) - (ez_next - ez)
            curl_z = (ey_next - ey) - (up_y(ex, nx_row) - ex)
            hx = load_h(step, 0, x) - COURANT * curl_x
            hy = load_h(step, 1, x) - COURANT * curl_y
            hz = load_h(step, 2, x) - COURANT * curl_z
            store_h(0, x, hx)
            store_h(1, x, hy)
            store_h(2, x, hz)
            slot = slot_h[x]
            ys_h[step, slot // half, 0, pl.ds(slot % half, 1), :] = hx[size_y - 1 : size_y, :]
            ys_h[step, slot // half, 1, pl.ds(slot % half, 1), :] = hz[size_y - 1 : size_y, :]
            if x == size_x - 1:
                xs_h[step, 0] = hy
                xs_h[step, 1] = hz

        def electric(step, x, skip_magnetic):
            if skip_magnetic:
                curl_x = curl_y = curl_z = zero_slab
            else:
                hx = load_h(step + 1, 0, x)
                hy = load_h(step + 1, 1, x)
                hz = load_h(step + 1, 2, x)
                if x > 0:
                    hy_prev = load_h(step + 1, 1, x - 1)
                    hz_prev = load_h(step + 1, 2, x - 1)
                else:
                    hy_prev = west[step, 0]
                    hz_prev = west[step, 1]
                sx_row = h_row_ref(south, step, 0, x)
                sz_row = h_row_ref(south, step, 1, x)
                curl_x = (hz - down_y(hz, sz_row)) - (hy - down_z(hy))
                curl_y = (hx - down_z(hx)) - (hz - hz_prev)
                curl_z = (hy - hy_prev) - (hx - down_y(hx, sx_row))
            if adjoint:
                to_layer = (ZM - x) % size_z
                curl_x = curl_x - jnp.where(iz == ZM, pltpu.roll(drv[step, 0], to_layer, 1), 0.0)
                curl_y = curl_y - jnp.where(iz == ZM, pltpu.roll(drv[step, 1], to_layer, 1), 0.0)
            scale = eps_ref[x]
            e_old = [load_e(step, comp, x) for comp in range(3)]
            ex = e_old[0] + COURANT * curl_x * scale
            ey = e_old[1] + COURANT * curl_y * scale
            ez = e_old[2] + COURANT * curl_z * scale
            store_e(step, 0, x, ex)
            store_e(step, 1, x, ey)
            store_e(step, 2, x, ez)
            if adjoint:
                moment = NT - step
                product = (
                    ex * hist[moment - 1, 0, x]
                    + ey * hist[moment - 1, 1, x]
                    + ez * hist[moment - 1, 2, x]
                )
                before = zero_slab if step == 0 else acc[x]
                acc[x] = before - product * scale
            else:
                for comp, value in enumerate((ex, ey, ez)):
                    chg[step, comp, x] = value - e_old[comp]
                from_layer = (x - ZM) % size_z
                for comp, value in enumerate((ex, ey)):
                    packed[comp] = jnp.where(iz == x, pltpu.roll(value, from_layer, 1), packed[comp])
            if step + 1 < NT:
                stage_e_rows(step + 1, x, ex, ez)
                if x == 0:
                    xs_e[step + 1, 0] = ey
                    xs_e[step + 1, 1] = ez

        packed = [zero_slab, zero_slab]
        for step in range(NT):
            skip_magnetic = adjoint and step == 0
            if not skip_magnetic:
                get_e_rows(step, 0)
                for x in order_h[:half]:
                    magnetic(step, x)
                send_h_rows(step, 0)
                get_e_rows(step, 1)
                for x in order_h[half:-1]:
                    magnetic(step, x)
                get_e_slab(step)
                magnetic(step, order_h[-1])
                send_h_rows(step, 1)
                send_h_slab(step)
                get_h_rows(step, 0)
            for x in order_e[:half]:
                electric(step, x, skip_magnetic)
            if step + 1 < NT:
                send_e_rows(step + 1, 0)
            if not skip_magnetic:
                get_h_rows(step, 1)
            for x in order_e[half:-1]:
                electric(step, x, skip_magnetic)
            if not skip_magnetic:
                get_h_slab(step)
            electric(step, order_e[-1], skip_magnetic)
            if step + 1 < NT:
                send_e_rows(step + 1, 1)
                send_e_slab(step + 1)
            if not adjoint:
                mon[step, 0] = packed[0]
                mon[step, 1] = packed[1]

        for copy, sends in sent:
            pl.when(sends)(copy.wait_send)

    rim_x = pltpu.VMEM((NT, 2, size_y, size_z), jnp.float32)
    rim_y = pltpu.VMEM((NT, 2, 2, half, size_z), jnp.float32)
    field_shape = (size_x, size_y, size_z)
    if adjoint:
        operands = [history, inv_eps, drive]
        out_shape = jax.ShapeDtypeStruct(field_shape, jnp.float32)
        out_specs = pl.BlockSpec(memory_space=pltpu.VMEM)
        state = [
            pltpu.VMEM((2, 3) + field_shape, jnp.float32),
            pltpu.VMEM((3,) + field_shape, jnp.float32),
        ]
    else:
        operands = [fields, inv_eps]
        out_shape = (
            jax.ShapeDtypeStruct((6,) + field_shape, jnp.float32),
            jax.ShapeDtypeStruct((NT, 3) + field_shape, jnp.float32),
            jax.ShapeDtypeStruct((NT, 2, size_y, size_z), jnp.float32),
        )
        out_specs = (pl.BlockSpec(memory_space=pltpu.VMEM),) * 3
        state = [pltpu.VMEM((2, 3) + field_shape, jnp.float32)]
    return pl.pallas_call(
        kernel,
        out_shape=out_shape,
        in_specs=[pl.BlockSpec(memory_space=pltpu.VMEM)] * len(operands),
        out_specs=out_specs,
        scratch_shapes=state + [
            rim_x, rim_y, rim_x, rim_y, rim_x, rim_y, rim_x, rim_y,
            pltpu.SemaphoreType.DMA((6 * NT,)),
            pltpu.SemaphoreType.DMA((6 * NT,)),
        ],
        compiler_params=pltpu.CompilerParams(
            collective_id=tag, has_side_effects=True, vmem_limit_bytes=56 * 1024 * 1024
        ),
    )(*operands)


def group_of(axes):
    sizes = [lax.axis_size(a) for a in axes]
    count = math.prod(sizes)
    return count, sizes


def group_place(axes, sizes):
    place = 0
    for axis, size in zip(axes, sizes):
        place = place * size + lax.axis_index(axis)
    return place


def group_device(axes, sizes, peer):
    coords = {}
    rest = peer
    for axis, size in reversed(list(zip(axes, sizes))):
        coords[axis] = rest % size
        rest = rest // size
    return tuple(coords[a] if a in coords else lax.axis_index(a) for a in ("gx", "gy"))


def exchange(pieces, axes, gather, tag):
    count, sizes = group_of(axes)
    piece_shape = pieces.shape if gather else pieces.shape[1:]

    def kernel(x_ref, o_ref, send_sem, recv_sem):
        me = group_place(axes, sizes)
        barrier = pltpu.get_barrier_semaphore()
        for step in range(1, count):
            peer = lax.rem(me + step, count)
            pl.semaphore_signal(
                barrier, 1, device_id=group_device(axes, sizes, peer),
                device_id_type=pl.DeviceIdType.MESH,
            )
        pl.semaphore_wait(barrier, count - 1)
        copies = []
        for step in range(1, count):
            peer = lax.rem(me + step, count)
            copy = pltpu.make_async_remote_copy(
                src_ref=x_ref if gather else x_ref.at[peer],
                dst_ref=o_ref.at[me],
                send_sem=send_sem.at[step],
                recv_sem=recv_sem.at[step],
                device_id=group_device(axes, sizes, peer),
                device_id_type=pl.DeviceIdType.MESH,
            )
            copy.start()
            copies.append(copy)
        own = x_ref[...] if gather else x_ref[me]
        o_ref[me] = own
        for copy in copies:
            copy.wait_send()
        for step in range(1, count):
            source = lax.rem(me + count - step, count)
            pltpu.make_async_remote_copy(
                src_ref=x_ref if gather else x_ref.at[source],
                dst_ref=o_ref.at[source],
                send_sem=send_sem.at[step],
                recv_sem=recv_sem.at[step],
                device_id=group_device(axes, sizes, source),
                device_id_type=pl.DeviceIdType.MESH,
            ).wait_recv()

    return pl.pallas_call(
        kernel,
        out_shape=jax.ShapeDtypeStruct((count,) + tuple(piece_shape), pieces.dtype),
        in_specs=[pl.BlockSpec(memory_space=pltpu.VMEM)],
        out_specs=pl.BlockSpec(memory_space=pltpu.VMEM),
        scratch_shapes=[pltpu.SemaphoreType.DMA((count,)), pltpu.SemaphoreType.DMA((count,))],
        compiler_params=pltpu.CompilerParams(collective_id=tag, has_side_effects=True),
    )(pieces)


def focal_rows(pieces, weights, norm_scale, tag):
    count, sizes = group_of(("gy",))
    rows, width = pieces.shape[1:]

    def kernel(x_ref, t_ref, far_ref, o_ref, got, held, send_sem, recv_sem):
        me = lax.axis_index("gy")
        barrier = pltpu.get_barrier_semaphore()
        for step in range(1, count):
            pl.semaphore_signal(
                barrier, 1, device_id=(lax.axis_index("gx"), lax.rem(me + step, count)),
                device_id_type=pl.DeviceIdType.MESH,
            )
        pl.semaphore_wait(barrier, count - 1)

        def spread(phase, source_of):
            copies = []
            for step in range(1, count):
                peer = lax.rem(me + step, count)
                copy = pltpu.make_async_remote_copy(
                    src_ref=source_of(peer),
                    dst_ref=(got if phase == 0 else o_ref).at[me],
                    send_sem=send_sem.at[phase * count + step],
                    recv_sem=recv_sem.at[phase * count + step],
                    device_id=(lax.axis_index("gx"), peer),
                    device_id_type=pl.DeviceIdType.MESH,
                )
                copy.start()
                copies.append(copy)
            for copy in copies:
                copy.wait_send()
            for step in range(1, count):
                source = lax.rem(me + count - step, count)
                pltpu.make_async_remote_copy(
                    src_ref=source_of(source),
                    dst_ref=(got if phase == 0 else o_ref).at[source],
                    send_sem=send_sem.at[phase * count + step],
                    recv_sem=recv_sem.at[phase * count + step],
                    device_id=(lax.axis_index("gx"), source),
                    device_id_type=pl.DeviceIdType.MESH,
                ).wait_recv()

        got[me] = x_ref[me]
        spread(0, lambda peer: x_ref.at[peer])
        total = got[0]
        for source in range(1, count):
            total = total + got[source]
        far = norm_scale * total
        far_ref[...] = far
        odd = lax.broadcasted_iota(jnp.int32, far.shape, 0) % 2 == 1
        scaled = t_ref[...] * far
        weighted = jnp.where(odd, -scaled, scaled)
        held[...] = weighted
        o_ref[me] = weighted
        spread(1, lambda peer: held)

    return pl.pallas_call(
        kernel,
        out_shape=(
            jax.ShapeDtypeStruct((rows, width), jnp.float32),
            jax.ShapeDtypeStruct((count, rows, width), jnp.float32),
        ),
        in_specs=[pl.BlockSpec(memory_space=pltpu.VMEM)] * 2,
        out_specs=(pl.BlockSpec(memory_space=pltpu.VMEM),) * 2,
        scratch_shapes=[
            pltpu.VMEM((count, rows, width), jnp.float32),
            pltpu.VMEM((rows, width), jnp.float32),
            pltpu.SemaphoreType.DMA((2 * count,)),
            pltpu.SemaphoreType.DMA((2 * count,)),
        ],
        compiler_params=pltpu.CompilerParams(collective_id=tag, has_side_effects=True),
    )(pieces, weights)


def kernel_table(count_out, count_in, offset, length):
    focal_pos = (jnp.arange(count_out, dtype=jnp.float32) + 0.5) / count_out - 0.5
    cell_pos = (
        offset.astype(jnp.float32) + jnp.arange(length, dtype=jnp.float32) + 0.5
    ) / count_in - 0.5
    phase = math.pi * count_out * (focal_pos[:, None] - cell_pos[None, :]) ** 2
    return (jnp.cos(phase), jnp.sin(phase))


def contract(pattern, first_op, second_op):
    return jnp.einsum(pattern, first_op, second_op, precision=lax.Precision.HIGHEST)


def route_pillars(rows, slot_ids, devices, capacity):
    slots = devices * capacity
    placing = (slot_ids[:, None] == jnp.arange(slots, dtype=jnp.int32)[None, :]).astype(
        jnp.float32
    )
    packed = contract("ps,pk->sk", placing, rows)
    got = exchange(packed.reshape(devices, capacity, rows.shape[1]), ("gx", "gy"), False, 0)
    return placing, got.reshape(slots, rows.shape[1])


def shards(fields, eps_background, target, widths, intersection, pillar_tile, anchors):
    span_x = lax.axis_size("gx")
    span_y = lax.axis_size("gy")
    devices = span_x * span_y
    place_x = lax.axis_index("gx")
    place_y = lax.axis_index("gy")
    linear = place_x * span_y + place_y
    offsets = jnp.arange(16, dtype=jnp.int32)
    capacity = 2 * max(1, P_DEV // devices)
    target_tile = pillar_tile[:, 0]
    onehot = (target_tile[:, None] == jnp.arange(devices, dtype=jnp.int32)[None, :]).astype(
        jnp.int32
    )
    earlier = jnp.cumsum(onehot, axis=0) - onehot
    order_in = jnp.sum(earlier * onehot, axis=1)
    slot_ids = target_tile * capacity + order_in
    rows = jnp.concatenate(
        [intersection * widths[:, None], anchors.astype(jnp.float32)], axis=1
    )
    placing, got = route_pillars(rows, slot_ids, devices, capacity)
    local_vals = got[:, :16]
    local_at = got[:, 16:18].astype(jnp.int32)
    cells_x = (local_at[:, 0:1] + (offsets // 4)[None, :]).reshape(-1)
    cells_y = (local_at[:, 1:2] + (offsets % 4)[None, :]).reshape(-1)
    lanes = jnp.arange(TILE, dtype=jnp.int32)
    pick_x = (cells_x[:, None] == lanes[None, :]).astype(jnp.float32)
    pick_y = (cells_y[:, None] == lanes[None, :]).astype(jnp.float32)
    filling = contract("sx,sy->xy", pick_x, pick_y * local_vals.reshape(-1)[:, None])
    z_index = jnp.arange(fields.shape[3], dtype=jnp.int32)
    layers = ((z_index >= ZM - ZP) & (z_index < ZM)).astype(jnp.float32)
    permittivity = eps_background + DELTA_EPS * filling[:, :, None] * layers[None, None, :]
    inv_eps = 1.0 / permittivity
    final_fields, e_changes, packed_mon = run_leaps(fields, inv_eps, None, None, 10)
    packed_mon = packed_mon[:, :, :, :TILE].swapaxes(2, 3)
    mon_re = jnp.zeros((2, TILE, TILE), jnp.float32)
    mon_im = jnp.zeros((2, TILE, TILE), jnp.float32)
    for moment in range(1, NT + 1):
        monitor = packed_mon[moment - 1]
        mon_re = mon_re + math.cos(ANGULAR_STEP * moment) * monitor
        mon_im = mon_im - math.sin(ANGULAR_STEP * moment) * monitor
    norm_scale = (TILE * span_x * TILE * span_y) ** (-0.5)
    x_re, x_im = kernel_table(U, TILE * span_x, place_x * TILE, TILE)
    y_re, y_im = kernel_table(V, TILE * span_y, place_y * TILE, TILE)
    part = jnp.stack(
        [
            contract("ux,cxy->ucy", x_re, mon_re) - contract("ux,cxy->ucy", x_im, mon_im),
            contract("ux,cxy->ucy", x_re, mon_im) + contract("ux,cxy->ucy", x_im, mon_re),
        ]
    )
    chunk_u = U // span_x
    part = part.reshape(2, span_x, chunk_u, 2, TILE).transpose(1, 2, 0, 3, 4)
    part = exchange(part.reshape(span_x, chunk_u, 4 * TILE), ("gx",), False, 1)
    part = jnp.sum(part, axis=0).reshape(chunk_u, 2, 2, TILE)
    part_re, part_im = part[:, 0], part[:, 1]
    far = jnp.stack(
        [
            contract("ucy,vy->cuv", part_re, y_re) - contract("ucy,vy->cuv", part_im, y_im),
            contract("ucy,vy->cuv", part_re, y_im) + contract("ucy,vy->cuv", part_im, y_re),
        ],
        axis=2,
    )
    row_count = U // devices
    far = far.reshape(2, span_y, row_count, 2, V).transpose(1, 0, 2, 3, 4)
    mine_target = lax.dynamic_slice_in_dim(target, linear * row_count, row_count, 0)
    row_weights = jnp.broadcast_to(mine_target[None, :, None, :], (2, row_count, 2, V))
    far, weighted = focal_rows(
        far.reshape(span_y, 2 * row_count * 2, V),
        row_weights.reshape(2 * row_count * 2, V),
        norm_scale,
        2,
    )
    far = far.reshape(2, row_count, 2, V)
    focal_power = jnp.sum(far * far, axis=(0, 2))
    weighted = weighted.reshape(span_y, 2, row_count, 2, V).transpose(1, 0, 2, 3, 4)
    weighted = weighted.reshape(2, span_y * row_count, 2, V)
    w_re, w_im = weighted[:, :, 0], weighted[:, :, 1]
    half = jnp.stack(
        [
            contract("cuv,vy->cuy", w_re, y_re) - contract("cuv,vy->cuy", w_im, y_im),
            contract("cuv,vy->cuy", w_re, y_im) + contract("cuv,vy->cuy", w_im, y_re),
        ]
    )
    half = half.transpose(2, 0, 1, 3).reshape(chunk_u, 4 * TILE)
    half = exchange(half, ("gx",), True, 4)
    half = half.reshape(span_x * chunk_u, 2, 2, TILE).transpose(1, 2, 0, 3)
    half_re, half_im = half[0], half[1]
    back_re = 2.0 * norm_scale * (
        contract("ux,cuy->cxy", x_re, half_re) - contract("ux,cuy->cxy", x_im, half_im)
    )
    back_im = 2.0 * norm_scale * (
        contract("ux,cuy->cxy", x_re, half_im) + contract("ux,cuy->cxy", x_im, half_re)
    )
    drives = []
    for moment in range(1, NT + 1):
        source_step = NT + 1 - moment
        adj_drive = (
            math.cos(ANGULAR_STEP * source_step) * back_re
            + math.sin(ANGULAR_STEP * source_step) * back_im
        )
        drives.append(adj_drive)
    drive = jnp.stack(drives).swapaxes(2, 3)
    drive = jnp.pad(drive, ((0, 0), (0, 0), (0, 0), (0, fields.shape[3] - TILE)))
    grad_eps = run_leaps(None, inv_eps, e_changes, drive, 11)
    column_grad = jnp.sum(grad_eps[:, :, ZM - ZP : ZM], axis=2)
    spread = contract("sx,xy->sy", pick_x, column_grad)
    picked = jnp.sum(spread * pick_y, axis=1).reshape(devices * capacity, 16)
    returned = exchange(picked.reshape(devices, capacity, 16), ("gx", "gy"), False, 5)
    own_vals = contract("ps,sk->pk", placing, returned.reshape(devices * capacity, 16))
    grad_widths = DELTA_EPS * jnp.sum(intersection * own_vals, axis=1)
    return (final_fields, focal_power, grad_widths)


def solution(mesh):
    placed = (
        P(None, "gx", "gy", None),
        P("gx", "gy", None),
        P(),
        P(("gx", "gy")),
        P(("gx", "gy"), None),
        P(("gx", "gy"), None),
        P(("gx", "gy"), None),
    )
    return jax.shard_map(
        shards,
        mesh=mesh,
        in_specs=placed,
        out_specs=(P(None, "gx", "gy", None), P(("gx", "gy"), None), P(("gx", "gy"))),
        check_vma=False,
    )
```

```python
import math

import jax
import jax.numpy as jnp
from jax import lax
from jax.sharding import PartitionSpec as P
from jax.experimental import pallas as pl
from jax.experimental.pallas import tpu as pltpu

TILE = 32
P_DEV = 128
NT = 4
ZP = 4
U = 256
V = 256
ZM = 64


COURANT = 0.5
ANGULAR_STEP = 0.9
DELTA_EPS = 4.0


def passed_along(shard, axis, by):
    count = lax.axis_size(axis)
    pairs = [(i, i + by) for i in range(count) if 0 <= i + by < count]
    return lax.ppermute(shard, axis, pairs)


def plus_diff(field, rim_layer, axis):
    extended = jnp.concatenate([field, rim_layer], axis=axis)
    return lax.slice_in_dim(extended, 1, extended.shape[axis], axis=axis) - field


def minus_diff(field, rim_layer, axis):
    extended = jnp.concatenate([rim_layer, field], axis=axis)
    return field - lax.slice_in_dim(extended, 0, field.shape[axis], axis=axis)


def leap_step(fields_now, inv_eps, sources):
    elec_x, elec_y, elec_z, magn_x, magn_y, magn_z = fields_now
    z_blank = jnp.zeros_like(elec_x[:, :, :1])
    rim_east = passed_along(jnp.stack([elec_y[:1], elec_z[:1]]), "gx", -1)
    rim_north = passed_along(jnp.stack([elec_x[:, :1], elec_z[:, :1]]), "gy", -1)
    curl_x = plus_diff(elec_z, rim_north[1], 1) - plus_diff(elec_y, z_blank, 2)
    curl_y = plus_diff(elec_x, z_blank, 2) - plus_diff(elec_z, rim_east[1], 0)
    curl_z = plus_diff(elec_y, rim_east[0], 0) - plus_diff(elec_x, rim_north[0], 1)
    magn_x = magn_x - COURANT * curl_x
    magn_y = magn_y - COURANT * curl_y
    magn_z = magn_z - COURANT * curl_z
    rim_west = passed_along(jnp.stack([magn_y[-1:], magn_z[-1:]]), "gx", 1)
    rim_south = passed_along(jnp.stack([magn_x[:, -1:], magn_z[:, -1:]]), "gy", 1)
    curl_x = minus_diff(magn_z, rim_south[1], 1) - minus_diff(magn_y, z_blank, 2)
    curl_y = minus_diff(magn_x, z_blank, 2) - minus_diff(magn_z, rim_west[1], 0)
    curl_z = minus_diff(magn_y, rim_west[0], 0) - minus_diff(magn_x, rim_south[0], 1)
    elec_x = elec_x + COURANT * (curl_x - sources[0]) * inv_eps
    elec_y = elec_y + COURANT * (curl_y - sources[1]) * inv_eps
    elec_z = elec_z + COURANT * curl_z * inv_eps
    return (elec_x, elec_y, elec_z, magn_x, magn_y, magn_z)


def run_leaps(fields, inv_eps, history, drive, tag):
    span_x = lax.axis_size("gx")
    span_y = lax.axis_size("gy")
    size_x, size_y, size_z = inv_eps.shape
    half = size_x // 2
    adjoint = history is not None
    mesh_id = pl.DeviceIdType.MESH
    order_h = list(range(half - 1, size_x - 1)) + list(range(0, half - 1)) + [size_x - 1]
    order_e = list(range(half - 1, size_x - 1)) + list(range(1, half - 1)) + [size_x - 1, 0]
    slot_h = {x: i for i, x in enumerate(order_h)}
    slot_e = {x: i for i, x in enumerate(order_e)}

    def kernel(*refs):
        refs = list(refs)
        if adjoint:
            hist, eps_ref, drv, acc = refs[:4]
            a_hist, h_state = refs[4:6]
            rest = refs[6:]
        else:
            f_in, eps_ref, final, chg, mon = refs[:5]
            a_hist = refs[5]
            rest = refs[6:]
        east, north, west, south, xs_e, ys_e, xs_h, ys_h, ssem, rsem = rest
        px = lax.axis_index("gx")
        py = lax.axis_index("gy")
        barrier = pltpu.get_barrier_semaphore()
        for peer in (
            (lax.rem(px + 1, span_x), py),
            (lax.rem(px + span_x - 1, span_x), py),
            (px, lax.rem(py + 1, span_y)),
            (px, lax.rem(py + span_y - 1, span_y)),
        ):
            pl.semaphore_signal(barrier, 1, device_id=peer, device_id_type=mesh_id)
        pl.semaphore_wait(barrier, 4)
        has_east = px < span_x - 1
        has_west = px > 0
        has_north = py < span_y - 1
        has_south = py > 0
        west_dev = (lax.rem(px + span_x - 1, span_x), py)
        east_dev = (lax.rem(px + 1, span_x), py)
        south_dev = (px, lax.rem(py + span_y - 1, span_y))
        north_dev = (px, lax.rem(py + 1, span_y))
        zero_slab = jnp.zeros((size_y, size_z), jnp.float32)
        iy = lax.broadcasted_iota(jnp.int32, (size_y, size_z), 0)
        iz = lax.broadcasted_iota(jnp.int32, (size_y, size_z), 1)

        for flag, buf in ((has_east, east), (has_north, north), (has_west, west), (has_south, south)):
            @pl.when(jnp.logical_not(flag))
            def _(buf=buf):
                buf[...] = jnp.zeros(buf.shape, jnp.float32)

        def up_y(slab, row):
            return jnp.where(iy == size_y - 1, row, pltpu.roll(slab, size_y - 1, 0))

        def down_y(slab, row):
            return jnp.where(iy == 0, row, pltpu.roll(slab, 1, 0))

        def up_z(slab):
            return jnp.where(iz == size_z - 1, 0.0, pltpu.roll(slab, size_z - 1, 1))

        def down_z(slab):
            return jnp.where(iz == 0, 0.0, pltpu.roll(slab, 1, 1))

        def load_e(step, comp, x):
            if step == 0:
                return zero_slab if adjoint else f_in[comp, x]
            return a_hist[(step - 1) % 2, comp, x]

        def store_e(step, comp, x, value):
            if step == NT - 1 and not adjoint:
                final[comp, x] = value
            else:
                a_hist[step % 2, comp, x] = value

        def load_h(step, comp, x):
            if adjoint and step <= 1:
                return zero_slab
            if step == 0:
                return f_in[3 + comp, x]
            return h_state[comp, x] if adjoint else final[3 + comp, x]

        def store_h(comp, x, value):
            if adjoint:
                h_state[comp, x] = value
            else:
                final[3 + comp, x] = value

        sent = []

        def link(src, dst, sem, device, sends):
            copy = pltpu.make_async_remote_copy(
                src_ref=src, dst_ref=dst, send_sem=ssem.at[sem], recv_sem=rsem.at[sem],
                device_id=device, device_id_type=mesh_id,
            )
            pl.when(sends)(copy.start)
            sent.append((copy, sends))
            return copy

        def wait_for(src, dst, sem, device, gets):
            copy = pltpu.make_async_remote_copy(
                src_ref=src, dst_ref=dst, send_sem=ssem.at[sem], recv_sem=rsem.at[sem],
                device_id=device, device_id_type=mesh_id,
            )
            pl.when(gets)(copy.wait_recv)

        def send_e_rows(step, chunk):
            link(ys_e.at[step, chunk], north.at[step, chunk], 6 * step + chunk, south_dev, has_south)

        def send_e_slab(step):
            link(xs_e.at[step], east.at[step], 6 * step + 2, west_dev, has_west)

        def get_e_rows(step, chunk):
            wait_for(ys_e.at[step, chunk], north.at[step, chunk], 6 * step + chunk, north_dev, has_north)

        def get_e_slab(step):
            wait_for(xs_e.at[step], east.at[step], 6 * step + 2, east_dev, has_east)

        def send_h_rows(step, chunk):
            link(ys_h.at[step, chunk], south.at[step, chunk], 6 * step + 3 + chunk, north_dev, has_north)

        def send_h_slab(step):
            link(xs_h.at[step], west.at[step], 6 * step + 5, east_dev, has_east)

        def get_h_rows(step, chunk):
            wait_for(ys_h.at[step, chunk], south.at[step, chunk], 6 * step + 3 + chunk, south_dev, has_south)

        def get_h_slab(step):
            wait_for(xs_h.at[step], west.at[step], 6 * step + 5, west_dev, has_west)

        def e_row_ref(buf, step, comp, x):
            slot = slot_e[x]
            return buf[step, slot // half, comp, pl.ds(slot % half, 1), :]

        def h_row_ref(buf, step, comp, x):
            slot = slot_h[x]
            return buf[step, slot // half, comp, pl.ds(slot % half, 1), :]

        def stage_e_rows(step, x, ex, ez):
            slot = slot_e[x]
            ys_e[step, slot // half, 0, pl.ds(slot % half, 1), :] = ex[0:1, :]
            ys_e[step, slot // half, 1, pl.ds(slot % half, 1), :] = ez[0:1, :]

        if not adjoint:
            xs_e[0, 0] = f_in[1, 0]
            xs_e[0, 1] = f_in[2, 0]
            for x in order_e:
                stage_e_rows(0, x, f_in[0, x], f_in[2, x])
            send_e_rows(0, 0)
            send_e_rows(0, 1)
            send_e_slab(0)

        def magnetic(step, x):
            ex = load_e(step, 0, x)
            ey = load_e(step, 1, x)
            ez = load_e(step, 2, x)
            if x + 1 < size_x:
                ey_next = load_e(step, 1, x + 1)
                ez_next = load_e(step, 2, x + 1)
            else:
                ey_next = east[step, 0]
                ez_next = east[step, 1]
            nx_row = e_row_ref(north, step, 0, x)
            nz_row = e_row_ref(north, step, 1, x)
            curl_x = (up_y(ez, nz_row) - ez) - (up_z(ey) - ey)
            curl_y = (up_z(ex) - ex) - (ez_next - ez)
            curl_z = (ey_next - ey) - (up_y(ex, nx_row) - ex)
            hx = load_h(step, 0, x) - COURANT * curl_x
            hy = load_h(step, 1, x) - COURANT * curl_y
            hz = load_h(step, 2, x) - COURANT * curl_z
            store_h(0, x, hx)
            store_h(1, x, hy)
            store_h(2, x, hz)
            slot = slot_h[x]
            ys_h[step, slot // half, 0, pl.ds(slot % half, 1), :] = hx[size_y - 1 : size_y, :]
            ys_h[step, slot // half, 1, pl.ds(slot % half, 1), :] = hz[size_y - 1 : size_y, :]
            if x == size_x - 1:
                xs_h[step, 0] = hy
                xs_h[step, 1] = hz

        def electric(step, x, skip_magnetic):
            if skip_magnetic:
                curl_x = curl_y = curl_z = zero_slab
            else:
                hx = load_h(step + 1, 0, x)
                hy = load_h(step + 1, 1, x)
                hz = load_h(step + 1, 2, x)
                if x > 0:
                    hy_prev = load_h(step + 1, 1, x - 1)
                    hz_prev = load_h(step + 1, 2, x - 1)
                else:
                    hy_prev = west[step, 0]
                    hz_prev = west[step, 1]
                sx_row = h_row_ref(south, step, 0, x)
                sz_row = h_row_ref(south, step, 1, x)
                curl_x = (hz - down_y(hz, sz_row)) - (hy - down_z(hy))
                curl_y = (hx - down_z(hx)) - (hz - hz_prev)
                curl_z = (hy - hy_prev) - (hx - down_y(hx, sx_row))
            if adjoint:
                to_layer = (ZM - x) % size_z
                curl_x = curl_x - jnp.where(iz == ZM, pltpu.roll(drv[step, 0], to_layer, 1), 0.0)
                curl_y = curl_y - jnp.where(iz == ZM, pltpu.roll(drv[step, 1], to_layer, 1), 0.0)
            scale = eps_ref[x]
            e_old = [load_e(step, comp, x) for comp in range(3)]
            ex = e_old[0] + COURANT * curl_x * scale
            ey = e_old[1] + COURANT * curl_y * scale
            ez = e_old[2] + COURANT * curl_z * scale
            store_e(step, 0, x, ex)
            store_e(step, 1, x, ey)
            store_e(step, 2, x, ez)
            if adjoint:
                moment = NT - step
                to_layers = (ZM - ZP - ZP * x) % size_z
                product = (
                    ex * pltpu.roll(hist[moment - 1, 0], to_layers, 1)
                    + ey * pltpu.roll(hist[moment - 1, 1], to_layers, 1)
                    + ez * pltpu.roll(hist[moment - 1, 2], to_layers, 1)
                )
                before = zero_slab if step == 0 else acc[x]
                acc[x] = before - product * scale
            else:
                from_layers = (ZP * x - (ZM - ZP)) % size_z
                for comp, value in enumerate((ex, ey, ez)):
                    moved = pltpu.roll(value - e_old[comp], from_layers, 1)
                    changed[comp] = jnp.where(iz // ZP == x, moved, changed[comp])
                from_layer = (x - ZM) % size_z
                for comp, value in enumerate((ex, ey)):
                    packed[comp] = jnp.where(iz == x, pltpu.roll(value, from_layer, 1), packed[comp])
            if step + 1 < NT:
                stage_e_rows(step + 1, x, ex, ez)
                if x == 0:
                    xs_e[step + 1, 0] = ey
                    xs_e[step + 1, 1] = ez

        packed = [zero_slab, zero_slab]
        changed = [zero_slab, zero_slab, zero_slab]
        for step in range(NT):
            skip_magnetic = adjoint and step == 0
            if not skip_magnetic:
                get_e_rows(step, 0)
                for x in order_h[:half]:
                    magnetic(step, x)
                send_h_rows(step, 0)
                get_e_rows(step, 1)
                for x in order_h[half:-1]:
                    magnetic(step, x)
                get_e_slab(step)
                magnetic(step, order_h[-1])
                send_h_rows(step, 1)
                send_h_slab(step)
                get_h_rows(step, 0)
            for x in order_e[:half]:
                electric(step, x, skip_magnetic)
            if step + 1 < NT:
                send_e_rows(step + 1, 0)
            if not skip_magnetic:
                get_h_rows(step, 1)
            for x in order_e[half:-1]:
                electric(step, x, skip_magnetic)
            if not skip_magnetic:
                get_h_slab(step)
            electric(step, order_e[-1], skip_magnetic)
            if step + 1 < NT:
                send_e_rows(step + 1, 1)
                send_e_slab(step + 1)
            if not adjoint:
                mon[step, 0] = packed[0]
                mon[step, 1] = packed[1]
                for comp in range(3):
                    chg[step, comp] = changed[comp]

        for copy, sends in sent:
            pl.when(sends)(copy.wait_send)

    rim_x = pltpu.VMEM((NT, 2, size_y, size_z), jnp.float32)
    rim_y = pltpu.VMEM((NT, 2, 2, half, size_z), jnp.float32)
    field_shape = (size_x, size_y, size_z)
    if adjoint:
        operands = [history, inv_eps, drive]
        out_shape = jax.ShapeDtypeStruct(field_shape, jnp.float32)
        out_specs = pl.BlockSpec(memory_space=pltpu.VMEM)
        state = [
            pltpu.VMEM((2, 3) + field_shape, jnp.float32),
            pltpu.VMEM((3,) + field_shape, jnp.float32),
        ]
    else:
        operands = [fields, inv_eps]
        out_shape = (
            jax.ShapeDtypeStruct((6,) + field_shape, jnp.float32),
            jax.ShapeDtypeStruct((NT, 3, size_y, size_z), jnp.float32),
            jax.ShapeDtypeStruct((NT, 2, size_y, size_z), jnp.float32),
        )
        out_specs = (pl.BlockSpec(memory_space=pltpu.VMEM),) * 3
        state = [pltpu.VMEM((2, 3) + field_shape, jnp.float32)]
    return pl.pallas_call(
        kernel,
        out_shape=out_shape,
        in_specs=[pl.BlockSpec(memory_space=pltpu.VMEM)] * len(operands),
        out_specs=out_specs,
        scratch_shapes=state + [
            rim_x, rim_y, rim_x, rim_y, rim_x, rim_y, rim_x, rim_y,
            pltpu.SemaphoreType.DMA((6 * NT,)),
            pltpu.SemaphoreType.DMA((6 * NT,)),
        ],
        compiler_params=pltpu.CompilerParams(
            collective_id=tag, has_side_effects=True, vmem_limit_bytes=56 * 1024 * 1024
        ),
    )(*operands)


def group_of(axes):
    sizes = [lax.axis_size(a) for a in axes]
    count = math.prod(sizes)
    return count, sizes


def group_place(axes, sizes):
    place = 0
    for axis, size in zip(axes, sizes):
        place = place * size + lax.axis_index(axis)
    return place


def group_device(axes, sizes, peer):
    coords = {}
    rest = peer
    for axis, size in reversed(list(zip(axes, sizes))):
        coords[axis] = rest % size
        rest = rest // size
    return tuple(coords[a] if a in coords else lax.axis_index(a) for a in ("gx", "gy"))


def exchange(pieces, axes, gather, tag):
    count, sizes = group_of(axes)
    piece_shape = pieces.shape if gather else pieces.shape[1:]

    def kernel(x_ref, o_ref, send_sem, recv_sem):
        me = group_place(axes, sizes)
        barrier = pltpu.get_barrier_semaphore()
        for step in range(1, count):
            peer = lax.rem(me + step, count)
            pl.semaphore_signal(
                barrier, 1, device_id=group_device(axes, sizes, peer),
                device_id_type=pl.DeviceIdType.MESH,
            )
        pl.semaphore_wait(barrier, count - 1)
        copies = []
        for step in range(1, count):
            peer = lax.rem(me + step, count)
            copy = pltpu.make_async_remote_copy(
                src_ref=x_ref if gather else x_ref.at[peer],
                dst_ref=o_ref.at[me],
                send_sem=send_sem.at[step],
                recv_sem=recv_sem.at[step],
                device_id=group_device(axes, sizes, peer),
                device_id_type=pl.DeviceIdType.MESH,
            )
            copy.start()
            copies.append(copy)
        own = x_ref[...] if gather else x_ref[me]
        o_ref[me] = own
        for copy in copies:
            copy.wait_send()
        for step in range(1, count):
            source = lax.rem(me + count - step, count)
            pltpu.make_async_remote_copy(
                src_ref=x_ref if gather else x_ref.at[source],
                dst_ref=o_ref.at[source],
                send_sem=send_sem.at[step],
                recv_sem=recv_sem.at[step],
                device_id=group_device(axes, sizes, source),
                device_id_type=pl.DeviceIdType.MESH,
            ).wait_recv()

    return pl.pallas_call(
        kernel,
        out_shape=jax.ShapeDtypeStruct((count,) + tuple(piece_shape), pieces.dtype),
        in_specs=[pl.BlockSpec(memory_space=pltpu.VMEM)],
        out_specs=pl.BlockSpec(memory_space=pltpu.VMEM),
        scratch_shapes=[pltpu.SemaphoreType.DMA((count,)), pltpu.SemaphoreType.DMA((count,))],
        compiler_params=pltpu.CompilerParams(collective_id=tag, has_side_effects=True),
    )(pieces)


def focal_rows(pieces, weights, norm_scale, tag):
    count, sizes = group_of(("gy",))
    rows, width = pieces.shape[1:]

    def kernel(x_ref, t_ref, far_ref, o_ref, got, held, send_sem, recv_sem):
        me = lax.axis_index("gy")
        barrier = pltpu.get_barrier_semaphore()
        for step in range(1, count):
            pl.semaphore_signal(
                barrier, 1, device_id=(lax.axis_index("gx"), lax.rem(me + step, count)),
                device_id_type=pl.DeviceIdType.MESH,
            )
        pl.semaphore_wait(barrier, count - 1)

        def spread(phase, source_of):
            copies = []
            for step in range(1, count):
                peer = lax.rem(me + step, count)
                copy = pltpu.make_async_remote_copy(
                    src_ref=source_of(peer),
                    dst_ref=(got if phase == 0 else o_ref).at[me],
                    send_sem=send_sem.at[phase * count + step],
                    recv_sem=recv_sem.at[phase * count + step],
                    device_id=(lax.axis_index("gx"), peer),
                    device_id_type=pl.DeviceIdType.MESH,
                )
                copy.start()
                copies.append(copy)
            for copy in copies:
                copy.wait_send()
            for step in range(1, count):
                source = lax.rem(me + count - step, count)
                pltpu.make_async_remote_copy(
                    src_ref=source_of(source),
                    dst_ref=(got if phase == 0 else o_ref).at[source],
                    send_sem=send_sem.at[phase * count + step],
                    recv_sem=recv_sem.at[phase * count + step],
                    device_id=(lax.axis_index("gx"), source),
                    device_id_type=pl.DeviceIdType.MESH,
                ).wait_recv()

        got[me] = x_ref[me]
        spread(0, lambda peer: x_ref.at[peer])
        total = got[0]
        for source in range(1, count):
            total = total + got[source]
        far = norm_scale * total
        far_ref[...] = far
        odd = lax.broadcasted_iota(jnp.int32, far.shape, 0) % 2 == 1
        scaled = t_ref[...] * far
        weighted = jnp.where(odd, -scaled, scaled)
        held[...] = weighted
        o_ref[me] = weighted
        spread(1, lambda peer: held)

    return pl.pallas_call(
        kernel,
        out_shape=(
            jax.ShapeDtypeStruct((rows, width), jnp.float32),
            jax.ShapeDtypeStruct((count, rows, width), jnp.float32),
        ),
        in_specs=[pl.BlockSpec(memory_space=pltpu.VMEM)] * 2,
        out_specs=(pl.BlockSpec(memory_space=pltpu.VMEM),) * 2,
        scratch_shapes=[
            pltpu.VMEM((count, rows, width), jnp.float32),
            pltpu.VMEM((rows, width), jnp.float32),
            pltpu.SemaphoreType.DMA((2 * count,)),
            pltpu.SemaphoreType.DMA((2 * count,)),
        ],
        compiler_params=pltpu.CompilerParams(collective_id=tag, has_side_effects=True),
    )(pieces, weights)


def kernel_table(count_out, count_in, offset, length):
    focal_pos = (jnp.arange(count_out, dtype=jnp.float32) + 0.5) / count_out - 0.5
    cell_pos = (
        offset.astype(jnp.float32) + jnp.arange(length, dtype=jnp.float32) + 0.5
    ) / count_in - 0.5
    phase = math.pi * count_out * (focal_pos[:, None] - cell_pos[None, :]) ** 2
    return (jnp.cos(phase), jnp.sin(phase))


def contract(pattern, first_op, second_op):
    return jnp.einsum(pattern, first_op, second_op, precision=lax.Precision.HIGHEST)


def route_pillars(rows, slot_ids, devices, capacity):
    slots = devices * capacity
    placing = (slot_ids[:, None] == jnp.arange(slots, dtype=jnp.int32)[None, :]).astype(
        jnp.float32
    )
    packed = contract("ps,pk->sk", placing, rows)
    got = exchange(packed.reshape(devices, capacity, rows.shape[1]), ("gx", "gy"), False, 0)
    return placing, got.reshape(slots, rows.shape[1])


def shards(fields, eps_background, target, widths, intersection, pillar_tile, anchors):
    span_x = lax.axis_size("gx")
    span_y = lax.axis_size("gy")
    devices = span_x * span_y
    place_x = lax.axis_index("gx")
    place_y = lax.axis_index("gy")
    linear = place_x * span_y + place_y
    offsets = jnp.arange(16, dtype=jnp.int32)
    capacity = 2 * max(1, P_DEV // devices)
    target_tile = pillar_tile[:, 0]
    onehot = (target_tile[:, None] == jnp.arange(devices, dtype=jnp.int32)[None, :]).astype(
        jnp.int32
    )
    earlier = jnp.cumsum(onehot, axis=0) - onehot
    order_in = jnp.sum(earlier * onehot, axis=1)
    slot_ids = target_tile * capacity + order_in
    rows = jnp.concatenate(
        [intersection * widths[:, None], anchors.astype(jnp.float32)], axis=1
    )
    placing, got = route_pillars(rows, slot_ids, devices, capacity)
    local_vals = got[:, :16]
    local_at = got[:, 16:18].astype(jnp.int32)
    cells_x = (local_at[:, 0:1] + (offsets // 4)[None, :]).reshape(-1)
    cells_y = (local_at[:, 1:2] + (offsets % 4)[None, :]).reshape(-1)
    lanes = jnp.arange(TILE, dtype=jnp.int32)
    pick_x = (cells_x[:, None] == lanes[None, :]).astype(jnp.float32)
    pick_y = (cells_y[:, None] == lanes[None, :]).astype(jnp.float32)
    filling = contract("sx,sy->xy", pick_x, pick_y * local_vals.reshape(-1)[:, None])
    z_index = jnp.arange(fields.shape[3], dtype=jnp.int32)
    layers = ((z_index >= ZM - ZP) & (z_index < ZM)).astype(jnp.float32)
    permittivity = eps_background + DELTA_EPS * filling[:, :, None] * layers[None, None, :]
    inv_eps = 1.0 / permittivity
    final_fields, e_changes, packed_mon = run_leaps(fields, inv_eps, None, None, 10)
    packed_mon = packed_mon[:, :, :, :TILE].swapaxes(2, 3)
    mon_re = jnp.zeros((2, TILE, TILE), jnp.float32)
    mon_im = jnp.zeros((2, TILE, TILE), jnp.float32)
    for moment in range(1, NT + 1):
        monitor = packed_mon[moment - 1]
        mon_re = mon_re + math.cos(ANGULAR_STEP * moment) * monitor
        mon_im = mon_im - math.sin(ANGULAR_STEP * moment) * monitor
    norm_scale = (TILE * span_x * TILE * span_y) ** (-0.5)
    x_re, x_im = kernel_table(U, TILE * span_x, place_x * TILE, TILE)
    y_re, y_im = kernel_table(V, TILE * span_y, place_y * TILE, TILE)
    part = jnp.stack(
        [
            contract("ux,cxy->ucy", x_re, mon_re) - contract("ux,cxy->ucy", x_im, mon_im),
            contract("ux,cxy->ucy", x_re, mon_im) + contract("ux,cxy->ucy", x_im, mon_re),
        ]
    )
    chunk_u = U // span_x
    part = part.reshape(2, span_x, chunk_u, 2, TILE).transpose(1, 2, 0, 3, 4)
    part = exchange(part.reshape(span_x, chunk_u, 4 * TILE), ("gx",), False, 1)
    part = jnp.sum(part, axis=0).reshape(chunk_u, 2, 2, TILE)
    part_re, part_im = part[:, 0], part[:, 1]
    far = jnp.stack(
        [
            contract("ucy,vy->cuv", part_re, y_re) - contract("ucy,vy->cuv", part_im, y_im),
            contract("ucy,vy->cuv", part_re, y_im) + contract("ucy,vy->cuv", part_im, y_re),
        ],
        axis=2,
    )
    row_count = U // devices
    far = far.reshape(2, span_y, row_count, 2, V).transpose(1, 0, 2, 3, 4)
    mine_target = lax.dynamic_slice_in_dim(target, linear * row_count, row_count, 0)
    row_weights = jnp.broadcast_to(mine_target[None, :, None, :], (2, row_count, 2, V))
    far, weighted = focal_rows(
        far.reshape(span_y, 2 * row_count * 2, V),
        row_weights.reshape(2 * row_count * 2, V),
        norm_scale,
        2,
    )
    far = far.reshape(2, row_count, 2, V)
    focal_power = jnp.sum(far * far, axis=(0, 2))
    weighted = weighted.reshape(span_y, 2, row_count, 2, V).transpose(1, 0, 2, 3, 4)
    weighted = weighted.reshape(2, span_y * row_count, 2, V)
    w_re, w_im = weighted[:, :, 0], weighted[:, :, 1]
    half = jnp.stack(
        [
            contract("cuv,vy->cuy", w_re, y_re) - contract("cuv,vy->cuy", w_im, y_im),
            contract("cuv,vy->cuy", w_re, y_im) + contract("cuv,vy->cuy", w_im, y_re),
        ]
    )
    half = half.transpose(2, 0, 1, 3).reshape(chunk_u, 4 * TILE)
    half = exchange(half, ("gx",), True, 4)
    half = half.reshape(span_x * chunk_u, 2, 2, TILE).transpose(1, 2, 0, 3)
    half_re, half_im = half[0], half[1]
    back_re = 2.0 * norm_scale * (
        contract("ux,cuy->cxy", x_re, half_re) - contract("ux,cuy->cxy", x_im, half_im)
    )
    back_im = 2.0 * norm_scale * (
        contract("ux,cuy->cxy", x_re, half_im) + contract("ux,cuy->cxy", x_im, half_re)
    )
    drives = []
    for moment in range(1, NT + 1):
        source_step = NT + 1 - moment
        adj_drive = (
            math.cos(ANGULAR_STEP * source_step) * back_re
            + math.sin(ANGULAR_STEP * source_step) * back_im
        )
        drives.append(adj_drive)
    drive = jnp.stack(drives).swapaxes(2, 3)
    drive = jnp.pad(drive, ((0, 0), (0, 0), (0, 0), (0, fields.shape[3] - TILE)))
    grad_eps = run_leaps(None, inv_eps, e_changes, drive, 11)
    column_grad = jnp.sum(grad_eps[:, :, ZM - ZP : ZM], axis=2)
    spread = contract("sx,xy->sy", pick_x, column_grad)
    picked = jnp.sum(spread * pick_y, axis=1).reshape(devices * capacity, 16)
    returned = exchange(picked.reshape(devices, capacity, 16), ("gx", "gy"), False, 5)
    own_vals = contract("ps,sk->pk", placing, returned.reshape(devices * capacity, 16))
    grad_widths = DELTA_EPS * jnp.sum(intersection * own_vals, axis=1)
    return (final_fields, focal_power, grad_widths)


def solution(mesh):
    placed = (
        P(None, "gx", "gy", None),
        P("gx", "gy", None),
        P(),
        P(("gx", "gy")),
        P(("gx", "gy"), None),
        P(("gx", "gy"), None),
        P(("gx", "gy"), None),
    )
    return jax.shard_map(
        shards,
        mesh=mesh,
        in_specs=placed,
        out_specs=(P(None, "gx", "gy", None), P(("gx", "gy"), None), P(("gx", "gy"))),
        check_vma=False,
    )
```

```python
import math

import jax
import jax.numpy as jnp
from jax import lax
from jax.sharding import PartitionSpec as P
from jax.experimental import pallas as pl
from jax.experimental.pallas import tpu as pltpu

TILE = 32
P_DEV = 128
NT = 4
ZP = 4
U = 256
V = 256
ZM = 64


COURANT = 0.5
ANGULAR_STEP = 0.9
DELTA_EPS = 4.0


def passed_along(shard, axis, by):
    count = lax.axis_size(axis)
    pairs = [(i, i + by) for i in range(count) if 0 <= i + by < count]
    return lax.ppermute(shard, axis, pairs)


def plus_diff(field, rim_layer, axis):
    extended = jnp.concatenate([field, rim_layer], axis=axis)
    return lax.slice_in_dim(extended, 1, extended.shape[axis], axis=axis) - field


def minus_diff(field, rim_layer, axis):
    extended = jnp.concatenate([rim_layer, field], axis=axis)
    return field - lax.slice_in_dim(extended, 0, field.shape[axis], axis=axis)


def leap_step(fields_now, inv_eps, sources):
    elec_x, elec_y, elec_z, magn_x, magn_y, magn_z = fields_now
    z_blank = jnp.zeros_like(elec_x[:, :, :1])
    rim_east = passed_along(jnp.stack([elec_y[:1], elec_z[:1]]), "gx", -1)
    rim_north = passed_along(jnp.stack([elec_x[:, :1], elec_z[:, :1]]), "gy", -1)
    curl_x = plus_diff(elec_z, rim_north[1], 1) - plus_diff(elec_y, z_blank, 2)
    curl_y = plus_diff(elec_x, z_blank, 2) - plus_diff(elec_z, rim_east[1], 0)
    curl_z = plus_diff(elec_y, rim_east[0], 0) - plus_diff(elec_x, rim_north[0], 1)
    magn_x = magn_x - COURANT * curl_x
    magn_y = magn_y - COURANT * curl_y
    magn_z = magn_z - COURANT * curl_z
    rim_west = passed_along(jnp.stack([magn_y[-1:], magn_z[-1:]]), "gx", 1)
    rim_south = passed_along(jnp.stack([magn_x[:, -1:], magn_z[:, -1:]]), "gy", 1)
    curl_x = minus_diff(magn_z, rim_south[1], 1) - minus_diff(magn_y, z_blank, 2)
    curl_y = minus_diff(magn_x, z_blank, 2) - minus_diff(magn_z, rim_west[1], 0)
    curl_z = minus_diff(magn_y, rim_west[0], 0) - minus_diff(magn_x, rim_south[0], 1)
    elec_x = elec_x + COURANT * (curl_x - sources[0]) * inv_eps
    elec_y = elec_y + COURANT * (curl_y - sources[1]) * inv_eps
    elec_z = elec_z + COURANT * curl_z * inv_eps
    return (elec_x, elec_y, elec_z, magn_x, magn_y, magn_z)


def run_leaps(fields, inv_eps, history, drive, tag):
    span_x = lax.axis_size("gx")
    span_y = lax.axis_size("gy")
    size_x, size_y, size_z = inv_eps.shape
    half = size_x // 2
    adjoint = history is not None
    mesh_id = pl.DeviceIdType.MESH
    order_h = list(range(half - 1, size_x - 1)) + list(range(0, half - 1)) + [size_x - 1]
    order_e = list(range(half - 1, size_x - 1)) + list(range(1, half - 1)) + [size_x - 1, 0]
    slot_h = {x: i for i, x in enumerate(order_h)}
    slot_e = {x: i for i, x in enumerate(order_e)}

    def kernel(*refs):
        refs = list(refs)
        if adjoint:
            hist, eps_ref, drv, acc = refs[:4]
            a_hist, h_state = refs[4:6]
            rest = refs[6:]
        else:
            f_in, eps_ref, final, chg, mon = refs[:5]
            a_hist = refs[5]
            rest = refs[6:]
        east, north, west, south, xs_e, ys_e, xs_h, ys_h, ssem, rsem = rest
        px = lax.axis_index("gx")
        py = lax.axis_index("gy")
        barrier = pltpu.get_barrier_semaphore()
        for peer in (
            (lax.rem(px + 1, span_x), py),
            (lax.rem(px + span_x - 1, span_x), py),
            (px, lax.rem(py + 1, span_y)),
            (px, lax.rem(py + span_y - 1, span_y)),
        ):
            pl.semaphore_signal(barrier, 1, device_id=peer, device_id_type=mesh_id)
        pl.semaphore_wait(barrier, 4)
        has_east = px < span_x - 1
        has_west = px > 0
        has_north = py < span_y - 1
        has_south = py > 0
        west_dev = (lax.rem(px + span_x - 1, span_x), py)
        east_dev = (lax.rem(px + 1, span_x), py)
        south_dev = (px, lax.rem(py + span_y - 1, span_y))
        north_dev = (px, lax.rem(py + 1, span_y))
        zero_slab = jnp.zeros((size_y, size_z), jnp.float32)
        iy = lax.broadcasted_iota(jnp.int32, (size_y, size_z), 0)
        iz = lax.broadcasted_iota(jnp.int32, (size_y, size_z), 1)

        for flag, buf in ((has_east, east), (has_north, north), (has_west, west), (has_south, south)):
            @pl.when(jnp.logical_not(flag))
            def _(buf=buf):
                buf[...] = jnp.zeros(buf.shape, jnp.float32)

        def up_y(slab, row):
            return jnp.where(iy == size_y - 1, row, pltpu.roll(slab, size_y - 1, 0))

        def down_y(slab, row):
            return jnp.where(iy == 0, row, pltpu.roll(slab, 1, 0))

        def up_z(slab):
            return jnp.where(iz == size_z - 1, 0.0, pltpu.roll(slab, size_z - 1, 1))

        def down_z(slab):
            return jnp.where(iz == 0, 0.0, pltpu.roll(slab, 1, 1))

        def load_e(step, comp, x):
            if step == 0:
                return zero_slab if adjoint else f_in[comp, x]
            return a_hist[(step - 1) % 2, comp, x]

        def store_e(step, comp, x, value):
            if step == NT - 1 and not adjoint:
                final[comp, x] = value
            else:
                a_hist[step % 2, comp, x] = value

        def load_h(step, comp, x):
            if adjoint and step <= 1:
                return zero_slab
            if step == 0:
                return f_in[3 + comp, x]
            return h_state[comp, x] if adjoint else final[3 + comp, x]

        def store_h(comp, x, value):
            if adjoint:
                h_state[comp, x] = value
            else:
                final[3 + comp, x] = value

        sent = []

        def link(src, dst, sem, device, sends):
            copy = pltpu.make_async_remote_copy(
                src_ref=src, dst_ref=dst, send_sem=ssem.at[sem], recv_sem=rsem.at[sem],
                device_id=device, device_id_type=mesh_id,
            )
            pl.when(sends)(copy.start)
            sent.append((copy, sends))
            return copy

        def wait_for(src, dst, sem, device, gets):
            copy = pltpu.make_async_remote_copy(
                src_ref=src, dst_ref=dst, send_sem=ssem.at[sem], recv_sem=rsem.at[sem],
                device_id=device, device_id_type=mesh_id,
            )
            pl.when(gets)(copy.wait_recv)

        def send_e_rows(step, chunk):
            link(ys_e.at[step, chunk], north.at[step, chunk], 6 * step + chunk, south_dev, has_south)

        def send_e_slab(step):
            link(xs_e.at[step], east.at[step], 6 * step + 2, west_dev, has_west)

        def get_e_rows(step, chunk):
            wait_for(ys_e.at[step, chunk], north.at[step, chunk], 6 * step + chunk, north_dev, has_north)

        def get_e_slab(step):
            wait_for(xs_e.at[step], east.at[step], 6 * step + 2, east_dev, has_east)

        def send_h_rows(step, chunk):
            link(ys_h.at[step, chunk], south.at[step, chunk], 6 * step + 3 + chunk, north_dev, has_north)

        def send_h_slab(step):
            link(xs_h.at[step], west.at[step], 6 * step + 5, east_dev, has_east)

        def get_h_rows(step, chunk):
            wait_for(ys_h.at[step, chunk], south.at[step, chunk], 6 * step + 3 + chunk, south_dev, has_south)

        def get_h_slab(step):
            wait_for(xs_h.at[step], west.at[step], 6 * step + 5, west_dev, has_west)

        def e_row_ref(buf, step, comp, x):
            slot = slot_e[x]
            return buf[step, slot // half, comp, pl.ds(slot % half, 1), :]

        def h_row_ref(buf, step, comp, x):
            slot = slot_h[x]
            return buf[step, slot // half, comp, pl.ds(slot % half, 1), :]

        def stage_e_rows(step, x, ex, ez):
            slot = slot_e[x]
            ys_e[step, slot // half, 0, pl.ds(slot % half, 1), :] = ex[0:1, :]
            ys_e[step, slot // half, 1, pl.ds(slot % half, 1), :] = ez[0:1, :]

        if not adjoint:
            xs_e[0, 0] = f_in[1, 0]
            xs_e[0, 1] = f_in[2, 0]
            for x in order_e:
                stage_e_rows(0, x, f_in[0, x], f_in[2, x])
            send_e_rows(0, 0)
            send_e_rows(0, 1)
            send_e_slab(0)

        def magnetic(step, x):
            ex = load_e(step, 0, x)
            ey = load_e(step, 1, x)
            ez = load_e(step, 2, x)
            if x + 1 < size_x:
                ey_next = load_e(step, 1, x + 1)
                ez_next = load_e(step, 2, x + 1)
            else:
                ey_next = east[step, 0]
                ez_next = east[step, 1]
            nx_row = e_row_ref(north, step, 0, x)
            nz_row = e_row_ref(north, step, 1, x)
            curl_x = (up_y(ez, nz_row) - ez) - (up_z(ey) - ey)
            curl_y = (up_z(ex) - ex) - (ez_next - ez)
            curl_z = (ey_next - ey) - (up_y(ex, nx_row) - ex)
            hx = load_h(step, 0, x) - COURANT * curl_x
            hy = load_h(step, 1, x) - COURANT * curl_y
            hz = load_h(step, 2, x) - COURANT * curl_z
            store_h(0, x, hx)
            store_h(1, x, hy)
            store_h(2, x, hz)
            slot = slot_h[x]
            ys_h[step, slot // half, 0, pl.ds(slot % half, 1), :] = hx[size_y - 1 : size_y, :]
            ys_h[step, slot // half, 1, pl.ds(slot % half, 1), :] = hz[size_y - 1 : size_y, :]
            if x == size_x - 1:
                xs_h[step, 0] = hy
                xs_h[step, 1] = hz

        def electric(step, x, skip_magnetic):
            if skip_magnetic:
                curl_x = curl_y = curl_z = zero_slab
            else:
                hx = load_h(step + 1, 0, x)
                hy = load_h(step + 1, 1, x)
                hz = load_h(step + 1, 2, x)
                if x > 0:
                    hy_prev = load_h(step + 1, 1, x - 1)
                    hz_prev = load_h(step + 1, 2, x - 1)
                else:
                    hy_prev = west[step, 0]
                    hz_prev = west[step, 1]
                sx_row = h_row_ref(south, step, 0, x)
                sz_row = h_row_ref(south, step, 1, x)
                curl_x = (hz - down_y(hz, sz_row)) - (hy - down_z(hy))
                curl_y = (hx - down_z(hx)) - (hz - hz_prev)
                curl_z = (hy - hy_prev) - (hx - down_y(hx, sx_row))
            if adjoint:
                to_layer = (ZM - x) % size_z
                curl_x = curl_x - jnp.where(iz == ZM, pltpu.roll(drv[step, 0], to_layer, 1), 0.0)
                curl_y = curl_y - jnp.where(iz == ZM, pltpu.roll(drv[step, 1], to_layer, 1), 0.0)
            scale = eps_ref[x]
            e_old = [load_e(step, comp, x) for comp in range(3)]
            ex = e_old[0] + COURANT * curl_x * scale
            ey = e_old[1] + COURANT * curl_y * scale
            ez = e_old[2] + COURANT * curl_z * scale
            store_e(step, 0, x, ex)
            store_e(step, 1, x, ey)
            store_e(step, 2, x, ez)
            if adjoint:
                moment = NT - step
                product = (
                    ex * hist[moment - 1, 0, x]
                    + ey * hist[moment - 1, 1, x]
                    + ez * hist[moment - 1, 2, x]
                )
                before = zero_slab if step == 0 else acc[x]
                acc[x] = before - product * scale
            else:
                for comp, value in enumerate((ex, ey, ez)):
                    chg[step, comp, x] = value - e_old[comp]
                from_layer = (x - ZM) % size_z
                for comp, value in enumerate((ex, ey)):
                    packed[comp] = jnp.where(iz == x, pltpu.roll(value, from_layer, 1), packed[comp])
            if step + 1 < NT:
                stage_e_rows(step + 1, x, ex, ez)
                if x == 0:
                    xs_e[step + 1, 0] = ey
                    xs_e[step + 1, 1] = ez

        packed = [zero_slab, zero_slab]
        for step in range(NT):
            skip_magnetic = adjoint and step == 0
            if not skip_magnetic:
                get_e_rows(step, 0)
                for x in order_h[:half]:
                    magnetic(step, x)
                send_h_rows(step, 0)
                get_e_rows(step, 1)
                for x in order_h[half:-1]:
                    magnetic(step, x)
                get_e_slab(step)
                magnetic(step, order_h[-1])
                send_h_rows(step, 1)
                send_h_slab(step)
                get_h_rows(step, 0)
            for x in order_e[:half]:
                electric(step, x, skip_magnetic)
            if step + 1 < NT:
                send_e_rows(step + 1, 0)
            if not skip_magnetic:
                get_h_rows(step, 1)
            for x in order_e[half:-1]:
                electric(step, x, skip_magnetic)
            if not skip_magnetic:
                get_h_slab(step)
            electric(step, order_e[-1], skip_magnetic)
            if step + 1 < NT:
                send_e_rows(step + 1, 1)
                send_e_slab(step + 1)
            if not adjoint:
                mon[step, 0] = packed[0]
                mon[step, 1] = packed[1]

        for copy, sends in sent:
            pl.when(sends)(copy.wait_send)

    rim_x = pltpu.VMEM((NT, 2, size_y, size_z), jnp.float32)
    rim_y = pltpu.VMEM((NT, 2, 2, half, size_z), jnp.float32)
    field_shape = (size_x, size_y, size_z)
    if adjoint:
        operands = [history, inv_eps, drive]
        out_shape = jax.ShapeDtypeStruct(field_shape, jnp.float32)
        out_specs = pl.BlockSpec(memory_space=pltpu.VMEM)
        state = [
            pltpu.VMEM((2, 3) + field_shape, jnp.float32),
            pltpu.VMEM((3,) + field_shape, jnp.float32),
        ]
    else:
        operands = [fields, inv_eps]
        out_shape = (
            jax.ShapeDtypeStruct((6,) + field_shape, jnp.float32),
            jax.ShapeDtypeStruct((NT, 3) + field_shape, jnp.float32),
            jax.ShapeDtypeStruct((NT, 2, size_y, size_z), jnp.float32),
        )
        out_specs = (pl.BlockSpec(memory_space=pltpu.VMEM),) * 3
        state = [pltpu.VMEM((2, 3) + field_shape, jnp.float32)]
    return pl.pallas_call(
        kernel,
        out_shape=out_shape,
        in_specs=[pl.BlockSpec(memory_space=pltpu.VMEM)] * len(operands),
        out_specs=out_specs,
        scratch_shapes=state + [
            rim_x, rim_y, rim_x, rim_y, rim_x, rim_y, rim_x, rim_y,
            pltpu.SemaphoreType.DMA((6 * NT,)),
            pltpu.SemaphoreType.DMA((6 * NT,)),
        ],
        compiler_params=pltpu.CompilerParams(
            collective_id=tag, has_side_effects=True, vmem_limit_bytes=56 * 1024 * 1024
        ),
    )(*operands)


def group_of(axes):
    sizes = [lax.axis_size(a) for a in axes]
    count = math.prod(sizes)
    return count, sizes


def group_place(axes, sizes):
    place = 0
    for axis, size in zip(axes, sizes):
        place = place * size + lax.axis_index(axis)
    return place


def group_device(axes, sizes, peer):
    coords = {}
    rest = peer
    for axis, size in reversed(list(zip(axes, sizes))):
        coords[axis] = rest % size
        rest = rest // size
    return tuple(coords[a] if a in coords else lax.axis_index(a) for a in ("gx", "gy"))


def exchange(pieces, axes, gather, tag, summed=False):
    count, sizes = group_of(axes)
    piece_shape = pieces.shape if gather else pieces.shape[1:]

    def kernel(x_ref, o_ref, send_sem, recv_sem):
        me = group_place(axes, sizes)
        barrier = pltpu.get_barrier_semaphore()
        for step in range(1, count):
            peer = lax.rem(me + step, count)
            pl.semaphore_signal(
                barrier, 1, device_id=group_device(axes, sizes, peer),
                device_id_type=pl.DeviceIdType.MESH,
            )
        pl.semaphore_wait(barrier, count - 1)
        copies = []
        for step in range(1, count):
            peer = lax.rem(me + step, count)
            copy = pltpu.make_async_remote_copy(
                src_ref=x_ref if gather else x_ref.at[peer],
                dst_ref=o_ref.at[me],
                send_sem=send_sem.at[step],
                recv_sem=recv_sem.at[step],
                device_id=group_device(axes, sizes, peer),
                device_id_type=pl.DeviceIdType.MESH,
            )
            copy.start()
            copies.append(copy)
        own = x_ref[...] if gather else x_ref[me]
        o_ref[me] = own
        for copy in copies:
            copy.wait_send()
        for step in range(1, count):
            source = lax.rem(me + count - step, count)
            pltpu.make_async_remote_copy(
                src_ref=x_ref if gather else x_ref.at[source],
                dst_ref=o_ref.at[source],
                send_sem=send_sem.at[step],
                recv_sem=recv_sem.at[step],
                device_id=group_device(axes, sizes, source),
                device_id_type=pl.DeviceIdType.MESH,
            ).wait_recv()

    def summing_kernel(x_ref, s_ref, o_ref, send_sem, recv_sem):
        kernel(x_ref, o_ref, send_sem, recv_sem)
        total = o_ref[0]
        for source in range(1, count):
            total = total + o_ref[source]
        s_ref[...] = total

    gathered = jax.ShapeDtypeStruct((count,) + tuple(piece_shape), pieces.dtype)
    if summed:
        return pl.pallas_call(
            summing_kernel,
            out_shape=jax.ShapeDtypeStruct(tuple(piece_shape), pieces.dtype),
            in_specs=[pl.BlockSpec(memory_space=pltpu.VMEM)],
            out_specs=pl.BlockSpec(memory_space=pltpu.VMEM),
            scratch_shapes=[
                pltpu.VMEM(gathered.shape, pieces.dtype),
                pltpu.SemaphoreType.DMA((count,)),
                pltpu.SemaphoreType.DMA((count,)),
            ],
            compiler_params=pltpu.CompilerParams(collective_id=tag, has_side_effects=True),
        )(pieces)
    return pl.pallas_call(
        kernel,
        out_shape=gathered,
        in_specs=[pl.BlockSpec(memory_space=pltpu.VMEM)],
        out_specs=pl.BlockSpec(memory_space=pltpu.VMEM),
        scratch_shapes=[pltpu.SemaphoreType.DMA((count,)), pltpu.SemaphoreType.DMA((count,))],
        compiler_params=pltpu.CompilerParams(collective_id=tag, has_side_effects=True),
    )(pieces)


def focal_rows(pieces, weights, norm_scale, tag):
    count, sizes = group_of(("gy",))
    rows, width = pieces.shape[1:]

    def kernel(x_ref, t_ref, far_ref, o_ref, got, held, send_sem, recv_sem):
        me = lax.axis_index("gy")
        barrier = pltpu.get_barrier_semaphore()
        for step in range(1, count):
            pl.semaphore_signal(
                barrier, 1, device_id=(lax.axis_index("gx"), lax.rem(me + step, count)),
                device_id_type=pl.DeviceIdType.MESH,
            )
        pl.semaphore_wait(barrier, count - 1)

        def spread(phase, source_of):
            copies = []
            for step in range(1, count):
                peer = lax.rem(me + step, count)
                copy = pltpu.make_async_remote_copy(
                    src_ref=source_of(peer),
                    dst_ref=(got if phase == 0 else o_ref).at[me],
                    send_sem=send_sem.at[phase * count + step],
                    recv_sem=recv_sem.at[phase * count + step],
                    device_id=(lax.axis_index("gx"), peer),
                    device_id_type=pl.DeviceIdType.MESH,
                )
                copy.start()
                copies.append(copy)
            for copy in copies:
                copy.wait_send()
            for step in range(1, count):
                source = lax.rem(me + count - step, count)
                pltpu.make_async_remote_copy(
                    src_ref=source_of(source),
                    dst_ref=(got if phase == 0 else o_ref).at[source],
                    send_sem=send_sem.at[phase * count + step],
                    recv_sem=recv_sem.at[phase * count + step],
                    device_id=(lax.axis_index("gx"), source),
                    device_id_type=pl.DeviceIdType.MESH,
                ).wait_recv()

        got[me] = x_ref[me]
        spread(0, lambda peer: x_ref.at[peer])
        total = got[0]
        for source in range(1, count):
            total = total + got[source]
        far = norm_scale * total
        far_ref[...] = far
        odd = lax.broadcasted_iota(jnp.int32, far.shape, 0) % 2 == 1
        scaled = t_ref[...] * far
        weighted = jnp.where(odd, -scaled, scaled)
        held[...] = weighted
        o_ref[me] = weighted
        spread(1, lambda peer: held)

    return pl.pallas_call(
        kernel,
        out_shape=(
            jax.ShapeDtypeStruct((rows, width), jnp.float32),
            jax.ShapeDtypeStruct((count, rows, width), jnp.float32),
        ),
        in_specs=[pl.BlockSpec(memory_space=pltpu.VMEM)] * 2,
        out_specs=(pl.BlockSpec(memory_space=pltpu.VMEM),) * 2,
        scratch_shapes=[
            pltpu.VMEM((count, rows, width), jnp.float32),
            pltpu.VMEM((rows, width), jnp.float32),
            pltpu.SemaphoreType.DMA((2 * count,)),
            pltpu.SemaphoreType.DMA((2 * count,)),
        ],
        compiler_params=pltpu.CompilerParams(collective_id=tag, has_side_effects=True),
    )(pieces, weights)


def kernel_table(count_out, count_in, offset, length):
    focal_pos = (jnp.arange(count_out, dtype=jnp.float32) + 0.5) / count_out - 0.5
    cell_pos = (
        offset.astype(jnp.float32) + jnp.arange(length, dtype=jnp.float32) + 0.5
    ) / count_in - 0.5
    phase = math.pi * count_out * (focal_pos[:, None] - cell_pos[None, :]) ** 2
    return (jnp.cos(phase), jnp.sin(phase))


def contract(pattern, first_op, second_op):
    return jnp.einsum(pattern, first_op, second_op, precision=lax.Precision.HIGHEST)


def route_pillars(rows, slot_ids, devices, capacity):
    slots = devices * capacity
    placing = (slot_ids[:, None] == jnp.arange(slots, dtype=jnp.int32)[None, :]).astype(
        jnp.float32
    )
    packed = contract("ps,pk->sk", placing, rows)
    got = exchange(packed.reshape(devices, capacity, rows.shape[1]), ("gx", "gy"), False, 0)
    return placing, got.reshape(slots, rows.shape[1])


def shards(fields, eps_background, target, widths, intersection, pillar_tile, anchors):
    span_x = lax.axis_size("gx")
    span_y = lax.axis_size("gy")
    devices = span_x * span_y
    place_x = lax.axis_index("gx")
    place_y = lax.axis_index("gy")
    linear = place_x * span_y + place_y
    offsets = jnp.arange(16, dtype=jnp.int32)
    capacity = 2 * max(1, P_DEV // devices)
    target_tile = pillar_tile[:, 0]
    pillar_index = jnp.arange(target_tile.shape[0], dtype=jnp.int32)
    same_before = (target_tile[None, :] == target_tile[:, None]) & (
        pillar_index[None, :] < pillar_index[:, None]
    )
    order_in = jnp.sum(same_before.astype(jnp.int32), axis=1)
    slot_ids = target_tile * capacity + order_in
    rows = jnp.concatenate(
        [intersection * widths[:, None], anchors.astype(jnp.float32)], axis=1
    )
    placing, got = route_pillars(rows, slot_ids, devices, capacity)
    local_vals = got[:, :16]
    local_at = got[:, 16:18].astype(jnp.int32)
    cells_x = (local_at[:, 0:1] + (offsets // 4)[None, :]).reshape(-1)
    cells_y = (local_at[:, 1:2] + (offsets % 4)[None, :]).reshape(-1)
    lanes = jnp.arange(TILE, dtype=jnp.int32)
    pick_x = (cells_x[:, None] == lanes[None, :]).astype(jnp.float32)
    pick_y = (cells_y[:, None] == lanes[None, :]).astype(jnp.float32)
    filling = contract("sx,sy->xy", pick_x, pick_y * local_vals.reshape(-1)[:, None])
    z_index = jnp.arange(fields.shape[3], dtype=jnp.int32)
    layers = ((z_index >= ZM - ZP) & (z_index < ZM)).astype(jnp.float32)
    permittivity = eps_background + DELTA_EPS * filling[:, :, None] * layers[None, None, :]
    inv_eps = 1.0 / permittivity
    final_fields, e_changes, packed_mon = run_leaps(fields, inv_eps, None, None, 10)
    packed_mon = packed_mon[:, :, :, :TILE].swapaxes(2, 3)
    mon_re = jnp.zeros((2, TILE, TILE), jnp.float32)
    mon_im = jnp.zeros((2, TILE, TILE), jnp.float32)
    for moment in range(1, NT + 1):
        monitor = packed_mon[moment - 1]
        mon_re = mon_re + math.cos(ANGULAR_STEP * moment) * monitor
        mon_im = mon_im - math.sin(ANGULAR_STEP * moment) * monitor
    norm_scale = (TILE * span_x * TILE * span_y) ** (-0.5)
    x_re, x_im = kernel_table(U, TILE * span_x, place_x * TILE, TILE)
    y_re, y_im = kernel_table(V, TILE * span_y, place_y * TILE, TILE)
    part = jnp.stack(
        [
            contract("ux,cxy->ucy", x_re, mon_re) - contract("ux,cxy->ucy", x_im, mon_im),
            contract("ux,cxy->ucy", x_re, mon_im) + contract("ux,cxy->ucy", x_im, mon_re),
        ]
    )
    chunk_u = U // span_x
    part = part.reshape(2, span_x, chunk_u, 2, TILE).transpose(1, 2, 0, 3, 4)
    part = exchange(part.reshape(span_x, chunk_u, 4 * TILE), ("gx",), False, 1, summed=True)
    part = part.reshape(chunk_u, 2, 2, TILE)
    part_re, part_im = part[:, 0], part[:, 1]
    far = jnp.stack(
        [
            contract("ucy,vy->cuv", part_re, y_re) - contract("ucy,vy->cuv", part_im, y_im),
            contract("ucy,vy->cuv", part_re, y_im) + contract("ucy,vy->cuv", part_im, y_re),
        ],
        axis=2,
    )
    row_count = U // devices
    far = far.reshape(2, span_y, row_count, 2, V).transpose(1, 0, 2, 3, 4)
    mine_target = lax.dynamic_slice_in_dim(target, linear * row_count, row_count, 0)
    row_weights = jnp.broadcast_to(mine_target[None, :, None, :], (2, row_count, 2, V))
    far, weighted = focal_rows(
        far.reshape(span_y, 2 * row_count * 2, V),
        row_weights.reshape(2 * row_count * 2, V),
        norm_scale,
        2,
    )
    far = far.reshape(2, row_count, 2, V)
    focal_power = jnp.sum(far * far, axis=(0, 2))
    weighted = weighted.reshape(span_y, 2, row_count, 2, V).transpose(1, 0, 2, 3, 4)
    weighted = weighted.reshape(2, span_y * row_count, 2, V)
    w_re, w_im = weighted[:, :, 0], weighted[:, :, 1]
    half = jnp.stack(
        [
            contract("cuv,vy->cuy", w_re, y_re) - contract("cuv,vy->cuy", w_im, y_im),
            contract("cuv,vy->cuy", w_re, y_im) + contract("cuv,vy->cuy", w_im, y_re),
        ]
    )
    half = half.transpose(2, 0, 1, 3).reshape(chunk_u, 4 * TILE)
    half = exchange(half, ("gx",), True, 4)
    half = half.reshape(span_x * chunk_u, 2, 2, TILE).transpose(1, 2, 0, 3)
    half_re, half_im = half[0], half[1]
    back_re = 2.0 * norm_scale * (
        contract("ux,cuy->cxy", x_re, half_re) - contract("ux,cuy->cxy", x_im, half_im)
    )
    back_im = 2.0 * norm_scale * (
        contract("ux,cuy->cxy", x_re, half_im) + contract("ux,cuy->cxy", x_im, half_re)
    )
    drives = []
    for moment in range(1, NT + 1):
        source_step = NT + 1 - moment
        adj_drive = (
            math.cos(ANGULAR_STEP * source_step) * back_re
            + math.sin(ANGULAR_STEP * source_step) * back_im
        )
        drives.append(adj_drive)
    drive = jnp.stack(drives).swapaxes(2, 3)
    drive = jnp.pad(drive, ((0, 0), (0, 0), (0, 0), (0, fields.shape[3] - TILE)))
    grad_eps = run_leaps(None, inv_eps, e_changes, drive, 11)
    column_grad = jnp.sum(grad_eps[:, :, ZM - ZP : ZM], axis=2)
    spread = contract("sx,xy->sy", pick_x, column_grad)
    picked = jnp.sum(spread * pick_y, axis=1).reshape(devices * capacity, 16)
    returned = exchange(picked.reshape(devices, capacity, 16), ("gx", "gy"), False, 5)
    own_vals = contract("ps,sk->pk", placing, returned.reshape(devices * capacity, 16))
    grad_widths = DELTA_EPS * jnp.sum(intersection * own_vals, axis=1)
    return (final_fields, focal_power, grad_widths)


def solution(mesh):
    placed = (
        P(None, "gx", "gy", None),
        P("gx", "gy", None),
        P(),
        P(("gx", "gy")),
        P(("gx", "gy"), None),
        P(("gx", "gy"), None),
        P(("gx", "gy"), None),
    )
    return jax.shard_map(
        shards,
        mesh=mesh,
        in_specs=placed,
        out_specs=(P(None, "gx", "gy", None), P(("gx", "gy"), None), P(("gx", "gy"))),
        check_vma=False,
    )
```

```python
import math

import jax
import jax.numpy as jnp
from jax import lax
from jax.sharding import PartitionSpec as P
from jax.experimental import pallas as pl
from jax.experimental.pallas import tpu as pltpu

TILE = 32
P_DEV = 128
NT = 4
ZP = 4
U = 256
V = 256
ZM = 64


COURANT = 0.5
ANGULAR_STEP = 0.9
DELTA_EPS = 4.0


def passed_along(shard, axis, by):
    count = lax.axis_size(axis)
    pairs = [(i, i + by) for i in range(count) if 0 <= i + by < count]
    return lax.ppermute(shard, axis, pairs)


def plus_diff(field, rim_layer, axis):
    extended = jnp.concatenate([field, rim_layer], axis=axis)
    return lax.slice_in_dim(extended, 1, extended.shape[axis], axis=axis) - field


def minus_diff(field, rim_layer, axis):
    extended = jnp.concatenate([rim_layer, field], axis=axis)
    return field - lax.slice_in_dim(extended, 0, field.shape[axis], axis=axis)


def leap_step(fields_now, inv_eps, sources):
    elec_x, elec_y, elec_z, magn_x, magn_y, magn_z = fields_now
    z_blank = jnp.zeros_like(elec_x[:, :, :1])
    rim_east = passed_along(jnp.stack([elec_y[:1], elec_z[:1]]), "gx", -1)
    rim_north = passed_along(jnp.stack([elec_x[:, :1], elec_z[:, :1]]), "gy", -1)
    curl_x = plus_diff(elec_z, rim_north[1], 1) - plus_diff(elec_y, z_blank, 2)
    curl_y = plus_diff(elec_x, z_blank, 2) - plus_diff(elec_z, rim_east[1], 0)
    curl_z = plus_diff(elec_y, rim_east[0], 0) - plus_diff(elec_x, rim_north[0], 1)
    magn_x = magn_x - COURANT * curl_x
    magn_y = magn_y - COURANT * curl_y
    magn_z = magn_z - COURANT * curl_z
    rim_west = passed_along(jnp.stack([magn_y[-1:], magn_z[-1:]]), "gx", 1)
    rim_south = passed_along(jnp.stack([magn_x[:, -1:], magn_z[:, -1:]]), "gy", 1)
    curl_x = minus_diff(magn_z, rim_south[1], 1) - minus_diff(magn_y, z_blank, 2)
    curl_y = minus_diff(magn_x, z_blank, 2) - minus_diff(magn_z, rim_west[1], 0)
    curl_z = minus_diff(magn_y, rim_west[0], 0) - minus_diff(magn_x, rim_south[0], 1)
    elec_x = elec_x + COURANT * (curl_x - sources[0]) * inv_eps
    elec_y = elec_y + COURANT * (curl_y - sources[1]) * inv_eps
    elec_z = elec_z + COURANT * curl_z * inv_eps
    return (elec_x, elec_y, elec_z, magn_x, magn_y, magn_z)


def run_leaps(fields, inv_eps, history, drive, tag):
    span_x = lax.axis_size("gx")
    span_y = lax.axis_size("gy")
    size_x, size_y, size_z = inv_eps.shape
    half = size_x // 2
    adjoint = history is not None
    mesh_id = pl.DeviceIdType.MESH
    order_h = list(range(half - 1, size_x - 1)) + list(range(0, half - 1)) + [size_x - 1]
    order_e = list(range(half - 1, size_x - 1)) + list(range(1, half - 1)) + [size_x - 1, 0]
    slot_h = {x: i for i, x in enumerate(order_h)}
    slot_e = {x: i for i, x in enumerate(order_e)}

    def kernel(*refs):
        refs = list(refs)
        if adjoint:
            hist, eps_ref, drv, col_out = refs[:4]
            a_hist, h_state, acc = refs[4:7]
            rest = refs[7:]
        else:
            f_in, eps_ref, final, chg, mon = refs[:5]
            a_hist = refs[5]
            rest = refs[6:]
        east, north, west, south, xs_e, ys_e, xs_h, ys_h, ssem, rsem = rest
        px = lax.axis_index("gx")
        py = lax.axis_index("gy")
        barrier = pltpu.get_barrier_semaphore()
        for peer in (
            (lax.rem(px + 1, span_x), py),
            (lax.rem(px + span_x - 1, span_x), py),
            (px, lax.rem(py + 1, span_y)),
            (px, lax.rem(py + span_y - 1, span_y)),
        ):
            pl.semaphore_signal(barrier, 1, device_id=peer, device_id_type=mesh_id)
        pl.semaphore_wait(barrier, 4)
        has_east = px < span_x - 1
        has_west = px > 0
        has_north = py < span_y - 1
        has_south = py > 0
        west_dev = (lax.rem(px + span_x - 1, span_x), py)
        east_dev = (lax.rem(px + 1, span_x), py)
        south_dev = (px, lax.rem(py + span_y - 1, span_y))
        north_dev = (px, lax.rem(py + 1, span_y))
        zero_slab = jnp.zeros((size_y, size_z), jnp.float32)
        iy = lax.broadcasted_iota(jnp.int32, (size_y, size_z), 0)
        iz = lax.broadcasted_iota(jnp.int32, (size_y, size_z), 1)

        for flag, buf in ((has_east, east), (has_north, north), (has_west, west), (has_south, south)):
            @pl.when(jnp.logical_not(flag))
            def _(buf=buf):
                buf[...] = jnp.zeros(buf.shape, jnp.float32)

        def up_y(slab, row):
            return jnp.where(iy == size_y - 1, row, pltpu.roll(slab, size_y - 1, 0))

        def down_y(slab, row):
            return jnp.where(iy == 0, row, pltpu.roll(slab, 1, 0))

        def up_z(slab):
            return jnp.where(iz == size_z - 1, 0.0, pltpu.roll(slab, size_z - 1, 1))

        def down_z(slab):
            return jnp.where(iz == 0, 0.0, pltpu.roll(slab, 1, 1))

        def load_e(step, comp, x):
            if step == 0:
                return zero_slab if adjoint else f_in[comp, x]
            return a_hist[(step - 1) % 2, comp, x]

        def store_e(step, comp, x, value):
            if step == NT - 1 and not adjoint:
                final[comp, x] = value
            else:
                a_hist[step % 2, comp, x] = value

        def load_h(step, comp, x):
            if adjoint and step <= 1:
                return zero_slab
            if step == 0:
                return f_in[3 + comp, x]
            return h_state[comp, x] if adjoint else final[3 + comp, x]

        def store_h(comp, x, value):
            if adjoint:
                h_state[comp, x] = value
            else:
                final[3 + comp, x] = value

        sent = []

        def link(src, dst, sem, device, sends):
            copy = pltpu.make_async_remote_copy(
                src_ref=src, dst_ref=dst, send_sem=ssem.at[sem], recv_sem=rsem.at[sem],
                device_id=device, device_id_type=mesh_id,
            )
            pl.when(sends)(copy.start)
            sent.append((copy, sends))
            return copy

        def wait_for(src, dst, sem, device, gets):
            copy = pltpu.make_async_remote_copy(
                src_ref=src, dst_ref=dst, send_sem=ssem.at[sem], recv_sem=rsem.at[sem],
                device_id=device, device_id_type=mesh_id,
            )
            pl.when(gets)(copy.wait_recv)

        def send_e_rows(step, chunk):
            link(ys_e.at[step, chunk], north.at[step, chunk], 6 * step + chunk, south_dev, has_south)

        def send_e_slab(step):
            link(xs_e.at[step], east.at[step], 6 * step + 2, west_dev, has_west)

        def get_e_rows(step, chunk):
            wait_for(ys_e.at[step, chunk], north.at[step, chunk], 6 * step + chunk, north_dev, has_north)

        def get_e_slab(step):
            wait_for(xs_e.at[step], east.at[step], 6 * step + 2, east_dev, has_east)

        def send_h_rows(step, chunk):
            link(ys_h.at[step, chunk], south.at[step, chunk], 6 * step + 3 + chunk, north_dev, has_north)

        def send_h_slab(step):
            link(xs_h.at[step], west.at[step], 6 * step + 5, east_dev, has_east)

        def get_h_rows(step, chunk):
            wait_for(ys_h.at[step, chunk], south.at[step, chunk], 6 * step + 3 + chunk, south_dev, has_south)

        def get_h_slab(step):
            wait_for(xs_h.at[step], west.at[step], 6 * step + 5, west_dev, has_west)

        def e_row_ref(buf, step, comp, x):
            slot = slot_e[x]
            return buf[step, slot // half, comp, pl.ds(slot % half, 1), :]

        def h_row_ref(buf, step, comp, x):
            slot = slot_h[x]
            return buf[step, slot // half, comp, pl.ds(slot % half, 1), :]

        def stage_e_rows(step, x, ex, ez):
            slot = slot_e[x]
            ys_e[step, slot // half, 0, pl.ds(slot % half, 1), :] = ex[0:1, :]
            ys_e[step, slot // half, 1, pl.ds(slot % half, 1), :] = ez[0:1, :]

        if not adjoint:
            xs_e[0, 0] = f_in[1, 0]
            xs_e[0, 1] = f_in[2, 0]
            for x in order_e:
                stage_e_rows(0, x, f_in[0, x], f_in[2, x])
            send_e_rows(0, 0)
            send_e_rows(0, 1)
            send_e_slab(0)

        def magnetic(step, x):
            ex = load_e(step, 0, x)
            ey = load_e(step, 1, x)
            ez = load_e(step, 2, x)
            if x + 1 < size_x:
                ey_next = load_e(step, 1, x + 1)
                ez_next = load_e(step, 2, x + 1)
            else:
                ey_next = east[step, 0]
                ez_next = east[step, 1]
            nx_row = e_row_ref(north, step, 0, x)
            nz_row = e_row_ref(north, step, 1, x)
            curl_x = (up_y(ez, nz_row) - ez) - (up_z(ey) - ey)
            curl_y = (up_z(ex) - ex) - (ez_next - ez)
            curl_z = (ey_next - ey) - (up_y(ex, nx_row) - ex)
            hx = load_h(step, 0, x) - COURANT * curl_x
            hy = load_h(step, 1, x) - COURANT * curl_y
            hz = load_h(step, 2, x) - COURANT * curl_z
            store_h(0, x, hx)
            store_h(1, x, hy)
            store_h(2, x, hz)
            slot = slot_h[x]
            ys_h[step, slot // half, 0, pl.ds(slot % half, 1), :] = hx[size_y - 1 : size_y, :]
            ys_h[step, slot // half, 1, pl.ds(slot % half, 1), :] = hz[size_y - 1 : size_y, :]
            if x == size_x - 1:
                xs_h[step, 0] = hy
                xs_h[step, 1] = hz

        def electric(step, x, skip_magnetic):
            if skip_magnetic:
                curl_x = curl_y = curl_z = zero_slab
            else:
                hx = load_h(step + 1, 0, x)
                hy = load_h(step + 1, 1, x)
                hz = load_h(step + 1, 2, x)
                if x > 0:
                    hy_prev = load_h(step + 1, 1, x - 1)
                    hz_prev = load_h(step + 1, 2, x - 1)
                else:
                    hy_prev = west[step, 0]
                    hz_prev = west[step, 1]
                sx_row = h_row_ref(south, step, 0, x)
                sz_row = h_row_ref(south, step, 1, x)
                curl_x = (hz - down_y(hz, sz_row)) - (hy - down_z(hy))
                curl_y = (hx - down_z(hx)) - (hz - hz_prev)
                curl_z = (hy - hy_prev) - (hx - down_y(hx, sx_row))
            if adjoint:
                to_layer = (ZM - x) % size_z
                curl_x = curl_x - jnp.where(iz == ZM, pltpu.roll(drv[step, 0], to_layer, 1), 0.0)
                curl_y = curl_y - jnp.where(iz == ZM, pltpu.roll(drv[step, 1], to_layer, 1), 0.0)
            scale = eps_ref[x]
            e_old = [load_e(step, comp, x) for comp in range(3)]
            ex = e_old[0] + COURANT * curl_x * scale
            ey = e_old[1] + COURANT * curl_y * scale
            ez = e_old[2] + COURANT * curl_z * scale
            store_e(step, 0, x, ex)
            store_e(step, 1, x, ey)
            store_e(step, 2, x, ez)
            if adjoint:
                moment = NT - step
                product = (
                    ex * hist[moment - 1, 0, x]
                    + ey * hist[moment - 1, 1, x]
                    + ez * hist[moment - 1, 2, x]
                )
                before = zero_slab if step == 0 else acc[x]
                total = before - product * scale
                if step == NT - 1:
                    pair = total + pltpu.roll(total, size_z - 1, 1)
                    quad = pair + pltpu.roll(pair, size_z - 2, 1)
                    moved = pltpu.roll(quad, (x - (ZM - ZP)) % size_z, 1)
                    column[0] = jnp.where(iz == x, moved, column[0])
                else:
                    acc[x] = total
            else:
                for comp, value in enumerate((ex, ey, ez)):
                    chg[step, comp, x] = value - e_old[comp]
                from_layer = (x - ZM) % size_z
                for comp, value in enumerate((ex, ey)):
                    packed[comp] = jnp.where(iz == x, pltpu.roll(value, from_layer, 1), packed[comp])
            if step + 1 < NT:
                stage_e_rows(step + 1, x, ex, ez)
                if x == 0:
                    xs_e[step + 1, 0] = ey
                    xs_e[step + 1, 1] = ez

        packed = [zero_slab, zero_slab]
        column = [zero_slab]
        for step in range(NT):
            skip_magnetic = adjoint and step == 0
            if not skip_magnetic:
                get_e_rows(step, 0)
                for x in order_h[:half]:
                    magnetic(step, x)
                send_h_rows(step, 0)
                get_e_rows(step, 1)
                for x in order_h[half:-1]:
                    magnetic(step, x)
                get_e_slab(step)
                magnetic(step, order_h[-1])
                send_h_rows(step, 1)
                send_h_slab(step)
                get_h_rows(step, 0)
            for x in order_e[:half]:
                electric(step, x, skip_magnetic)
            if step + 1 < NT:
                send_e_rows(step + 1, 0)
            if not skip_magnetic:
                get_h_rows(step, 1)
            for x in order_e[half:-1]:
                electric(step, x, skip_magnetic)
            if not skip_magnetic:
                get_h_slab(step)
            electric(step, order_e[-1], skip_magnetic)
            if step + 1 < NT:
                send_e_rows(step + 1, 1)
                send_e_slab(step + 1)
            if not adjoint:
                mon[step, 0] = packed[0]
                mon[step, 1] = packed[1]

        for copy, sends in sent:
            pl.when(sends)(copy.wait_send)
        if adjoint:
            col_out[...] = column[0]

    rim_x = pltpu.VMEM((NT, 2, size_y, size_z), jnp.float32)
    rim_y = pltpu.VMEM((NT, 2, 2, half, size_z), jnp.float32)
    field_shape = (size_x, size_y, size_z)
    if adjoint:
        operands = [history, inv_eps, drive]
        out_shape = jax.ShapeDtypeStruct((size_y, size_z), jnp.float32)
        out_specs = pl.BlockSpec(memory_space=pltpu.VMEM)
        state = [
            pltpu.VMEM((2, 3) + field_shape, jnp.float32),
            pltpu.VMEM((3,) + field_shape, jnp.float32),
            pltpu.VMEM(field_shape, jnp.float32),
        ]
    else:
        operands = [fields, inv_eps]
        out_shape = (
            jax.ShapeDtypeStruct((6,) + field_shape, jnp.float32),
            jax.ShapeDtypeStruct((NT, 3) + field_shape, jnp.float32),
            jax.ShapeDtypeStruct((NT, 2, size_y, size_z), jnp.float32),
        )
        out_specs = (pl.BlockSpec(memory_space=pltpu.VMEM),) * 3
        state = [pltpu.VMEM((2, 3) + field_shape, jnp.float32)]
    return pl.pallas_call(
        kernel,
        out_shape=out_shape,
        in_specs=[pl.BlockSpec(memory_space=pltpu.VMEM)] * len(operands),
        out_specs=out_specs,
        scratch_shapes=state + [
            rim_x, rim_y, rim_x, rim_y, rim_x, rim_y, rim_x, rim_y,
            pltpu.SemaphoreType.DMA((6 * NT,)),
            pltpu.SemaphoreType.DMA((6 * NT,)),
        ],
        compiler_params=pltpu.CompilerParams(
            collective_id=tag, has_side_effects=True, vmem_limit_bytes=56 * 1024 * 1024
        ),
    )(*operands)


def group_of(axes):
    sizes = [lax.axis_size(a) for a in axes]
    count = math.prod(sizes)
    return count, sizes


def group_place(axes, sizes):
    place = 0
    for axis, size in zip(axes, sizes):
        place = place * size + lax.axis_index(axis)
    return place


def group_device(axes, sizes, peer):
    coords = {}
    rest = peer
    for axis, size in reversed(list(zip(axes, sizes))):
        coords[axis] = rest % size
        rest = rest // size
    return tuple(coords[a] if a in coords else lax.axis_index(a) for a in ("gx", "gy"))


def exchange(pieces, axes, gather, tag, summed=False):
    count, sizes = group_of(axes)
    piece_shape = pieces.shape if gather else pieces.shape[1:]

    def kernel(x_ref, o_ref, send_sem, recv_sem):
        me = group_place(axes, sizes)
        barrier = pltpu.get_barrier_semaphore()
        for step in range(1, count):
            peer = lax.rem(me + step, count)
            pl.semaphore_signal(
                barrier, 1, device_id=group_device(axes, sizes, peer),
                device_id_type=pl.DeviceIdType.MESH,
            )
        pl.semaphore_wait(barrier, count - 1)
        copies = []
        for step in range(1, count):
            peer = lax.rem(me + step, count)
            copy = pltpu.make_async_remote_copy(
                src_ref=x_ref if gather else x_ref.at[peer],
                dst_ref=o_ref.at[me],
                send_sem=send_sem.at[step],
                recv_sem=recv_sem.at[step],
                device_id=group_device(axes, sizes, peer),
                device_id_type=pl.DeviceIdType.MESH,
            )
            copy.start()
            copies.append(copy)
        own = x_ref[...] if gather else x_ref[me]
        o_ref[me] = own
        for copy in copies:
            copy.wait_send()
        for step in range(1, count):
            source = lax.rem(me + count - step, count)
            pltpu.make_async_remote_copy(
                src_ref=x_ref if gather else x_ref.at[source],
                dst_ref=o_ref.at[source],
                send_sem=send_sem.at[step],
                recv_sem=recv_sem.at[step],
                device_id=group_device(axes, sizes, source),
                device_id_type=pl.DeviceIdType.MESH,
            ).wait_recv()

    def summing_kernel(x_ref, s_ref, o_ref, send_sem, recv_sem):
        kernel(x_ref, o_ref, send_sem, recv_sem)
        total = o_ref[0]
        for source in range(1, count):
            total = total + o_ref[source]
        s_ref[...] = total

    gathered = jax.ShapeDtypeStruct((count,) + tuple(piece_shape), pieces.dtype)
    if summed:
        return pl.pallas_call(
            summing_kernel,
            out_shape=jax.ShapeDtypeStruct(tuple(piece_shape), pieces.dtype),
            in_specs=[pl.BlockSpec(memory_space=pltpu.VMEM)],
            out_specs=pl.BlockSpec(memory_space=pltpu.VMEM),
            scratch_shapes=[
                pltpu.VMEM(gathered.shape, pieces.dtype),
                pltpu.SemaphoreType.DMA((count,)),
                pltpu.SemaphoreType.DMA((count,)),
            ],
            compiler_params=pltpu.CompilerParams(collective_id=tag, has_side_effects=True),
        )(pieces)
    return pl.pallas_call(
        kernel,
        out_shape=gathered,
        in_specs=[pl.BlockSpec(memory_space=pltpu.VMEM)],
        out_specs=pl.BlockSpec(memory_space=pltpu.VMEM),
        scratch_shapes=[pltpu.SemaphoreType.DMA((count,)), pltpu.SemaphoreType.DMA((count,))],
        compiler_params=pltpu.CompilerParams(collective_id=tag, has_side_effects=True),
    )(pieces)


def focal_rows(pieces, weights, norm_scale, tag):
    count, sizes = group_of(("gy",))
    rows, width = pieces.shape[1:]

    def kernel(x_ref, t_ref, far_ref, o_ref, got, held, send_sem, recv_sem):
        me = lax.axis_index("gy")
        barrier = pltpu.get_barrier_semaphore()
        for step in range(1, count):
            pl.semaphore_signal(
                barrier, 1, device_id=(lax.axis_index("gx"), lax.rem(me + step, count)),
                device_id_type=pl.DeviceIdType.MESH,
            )
        pl.semaphore_wait(barrier, count - 1)

        def spread(phase, source_of):
            copies = []
            for step in range(1, count):
                peer = lax.rem(me + step, count)
                copy = pltpu.make_async_remote_copy(
                    src_ref=source_of(peer),
                    dst_ref=(got if phase == 0 else o_ref).at[me],
                    send_sem=send_sem.at[phase * count + step],
                    recv_sem=recv_sem.at[phase * count + step],
                    device_id=(lax.axis_index("gx"), peer),
                    device_id_type=pl.DeviceIdType.MESH,
                )
                copy.start()
                copies.append(copy)
            for copy in copies:
                copy.wait_send()
            for step in range(1, count):
                source = lax.rem(me + count - step, count)
                pltpu.make_async_remote_copy(
                    src_ref=source_of(source),
                    dst_ref=(got if phase == 0 else o_ref).at[source],
                    send_sem=send_sem.at[phase * count + step],
                    recv_sem=recv_sem.at[phase * count + step],
                    device_id=(lax.axis_index("gx"), source),
                    device_id_type=pl.DeviceIdType.MESH,
                ).wait_recv()

        got[me] = x_ref[me]
        spread(0, lambda peer: x_ref.at[peer])
        total = got[0]
        for source in range(1, count):
            total = total + got[source]
        far = norm_scale * total
        far_ref[...] = far
        odd = lax.broadcasted_iota(jnp.int32, far.shape, 0) % 2 == 1
        scaled = t_ref[...] * far
        weighted = jnp.where(odd, -scaled, scaled)
        held[...] = weighted
        o_ref[me] = weighted
        spread(1, lambda peer: held)

    return pl.pallas_call(
        kernel,
        out_shape=(
            jax.ShapeDtypeStruct((rows, width), jnp.float32),
            jax.ShapeDtypeStruct((count, rows, width), jnp.float32),
        ),
        in_specs=[pl.BlockSpec(memory_space=pltpu.VMEM)] * 2,
        out_specs=(pl.BlockSpec(memory_space=pltpu.VMEM),) * 2,
        scratch_shapes=[
            pltpu.VMEM((count, rows, width), jnp.float32),
            pltpu.VMEM((rows, width), jnp.float32),
            pltpu.SemaphoreType.DMA((2 * count,)),
            pltpu.SemaphoreType.DMA((2 * count,)),
        ],
        compiler_params=pltpu.CompilerParams(collective_id=tag, has_side_effects=True),
    )(pieces, weights)


def kernel_table(count_out, count_in, offset, length):
    focal_pos = (jnp.arange(count_out, dtype=jnp.float32) + 0.5) / count_out - 0.5
    cell_pos = (
        offset.astype(jnp.float32) + jnp.arange(length, dtype=jnp.float32) + 0.5
    ) / count_in - 0.5
    phase = math.pi * count_out * (focal_pos[:, None] - cell_pos[None, :]) ** 2
    return (jnp.cos(phase), jnp.sin(phase))


def contract(pattern, first_op, second_op):
    return jnp.einsum(pattern, first_op, second_op, precision=lax.Precision.HIGHEST)


def route_pillars(rows, slot_ids, devices, capacity):
    slots = devices * capacity
    placing = (slot_ids[:, None] == jnp.arange(slots, dtype=jnp.int32)[None, :]).astype(
        jnp.float32
    )
    packed = contract("ps,pk->sk", placing, rows)
    got = exchange(packed.reshape(devices, capacity, rows.shape[1]), ("gx", "gy"), False, 0)
    return placing, got.reshape(slots, rows.shape[1])


def shards(fields, eps_background, target, widths, intersection, pillar_tile, anchors):
    span_x = lax.axis_size("gx")
    span_y = lax.axis_size("gy")
    devices = span_x * span_y
    place_x = lax.axis_index("gx")
    place_y = lax.axis_index("gy")
    linear = place_x * span_y + place_y
    offsets = jnp.arange(16, dtype=jnp.int32)
    capacity = 2 * max(1, P_DEV // devices)
    target_tile = pillar_tile[:, 0]
    pillar_index = jnp.arange(target_tile.shape[0], dtype=jnp.int32)
    same_before = (target_tile[None, :] == target_tile[:, None]) & (
        pillar_index[None, :] < pillar_index[:, None]
    )
    order_in = jnp.sum(same_before.astype(jnp.int32), axis=1)
    slot_ids = target_tile * capacity + order_in
    rows = jnp.concatenate(
        [intersection * widths[:, None], anchors.astype(jnp.float32)], axis=1
    )
    placing, got = route_pillars(rows, slot_ids, devices, capacity)
    local_vals = got[:, :16]
    local_at = got[:, 16:18].astype(jnp.int32)
    cells_x = (local_at[:, 0:1] + (offsets // 4)[None, :]).reshape(-1)
    cells_y = (local_at[:, 1:2] + (offsets % 4)[None, :]).reshape(-1)
    lanes = jnp.arange(TILE, dtype=jnp.int32)
    pick_x = (cells_x[:, None] == lanes[None, :]).astype(jnp.float32)
    pick_y = (cells_y[:, None] == lanes[None, :]).astype(jnp.float32)
    filling = contract("sx,sy->xy", pick_x, pick_y * local_vals.reshape(-1)[:, None])
    z_index = jnp.arange(fields.shape[3], dtype=jnp.int32)
    layers = ((z_index >= ZM - ZP) & (z_index < ZM)).astype(jnp.float32)
    permittivity = eps_background + DELTA_EPS * filling[:, :, None] * layers[None, None, :]
    inv_eps = 1.0 / permittivity
    final_fields, e_changes, packed_mon = run_leaps(fields, inv_eps, None, None, 10)
    packed_mon = packed_mon[:, :, :, :TILE].swapaxes(2, 3)
    mon_re = jnp.zeros((2, TILE, TILE), jnp.float32)
    mon_im = jnp.zeros((2, TILE, TILE), jnp.float32)
    for moment in range(1, NT + 1):
        monitor = packed_mon[moment - 1]
        mon_re = mon_re + math.cos(ANGULAR_STEP * moment) * monitor
        mon_im = mon_im - math.sin(ANGULAR_STEP * moment) * monitor
    norm_scale = (TILE * span_x * TILE * span_y) ** (-0.5)
    x_re, x_im = kernel_table(U, TILE * span_x, place_x * TILE, TILE)
    y_re, y_im = kernel_table(V, TILE * span_y, place_y * TILE, TILE)
    part = jnp.stack(
        [
            contract("ux,cxy->ucy", x_re, mon_re) - contract("ux,cxy->ucy", x_im, mon_im),
            contract("ux,cxy->ucy", x_re, mon_im) + contract("ux,cxy->ucy", x_im, mon_re),
        ]
    )
    chunk_u = U // span_x
    part = part.reshape(2, span_x, chunk_u, 2, TILE).transpose(1, 2, 0, 3, 4)
    part = exchange(part.reshape(span_x, chunk_u, 4 * TILE), ("gx",), False, 1, summed=True)
    part = part.reshape(chunk_u, 2, 2, TILE)
    part_re, part_im = part[:, 0], part[:, 1]
    far = jnp.stack(
        [
            contract("ucy,vy->cuv", part_re, y_re) - contract("ucy,vy->cuv", part_im, y_im),
            contract("ucy,vy->cuv", part_re, y_im) + contract("ucy,vy->cuv", part_im, y_re),
        ],
        axis=2,
    )
    row_count = U // devices
    far = far.reshape(2, span_y, row_count, 2, V).transpose(1, 0, 2, 3, 4)
    mine_target = lax.dynamic_slice_in_dim(target, linear * row_count, row_count, 0)
    row_weights = jnp.broadcast_to(mine_target[None, :, None, :], (2, row_count, 2, V))
    far, weighted = focal_rows(
        far.reshape(span_y, 2 * row_count * 2, V),
        row_weights.reshape(2 * row_count * 2, V),
        norm_scale,
        2,
    )
    far = far.reshape(2, row_count, 2, V)
    focal_power = jnp.sum(far * far, axis=(0, 2))
    weighted = weighted.reshape(span_y, 2, row_count, 2, V).transpose(1, 0, 2, 3, 4)
    weighted = weighted.reshape(2, span_y * row_count, 2, V)
    w_re, w_im = weighted[:, :, 0], weighted[:, :, 1]
    half = jnp.stack(
        [
            contract("cuv,vy->cuy", w_re, y_re) - contract("cuv,vy->cuy", w_im, y_im),
            contract("cuv,vy->cuy", w_re, y_im) + contract("cuv,vy->cuy", w_im, y_re),
        ]
    )
    half = half.transpose(2, 0, 1, 3).reshape(chunk_u, 4 * TILE)
    half = exchange(half, ("gx",), True, 4)
    half = half.reshape(span_x * chunk_u, 2, 2, TILE).transpose(1, 2, 0, 3)
    half_re, half_im = half[0], half[1]
    back_re = 2.0 * norm_scale * (
        contract("ux,cuy->cxy", x_re, half_re) - contract("ux,cuy->cxy", x_im, half_im)
    )
    back_im = 2.0 * norm_scale * (
        contract("ux,cuy->cxy", x_re, half_im) + contract("ux,cuy->cxy", x_im, half_re)
    )
    drives = []
    for moment in range(1, NT + 1):
        source_step = NT + 1 - moment
        adj_drive = (
            math.cos(ANGULAR_STEP * source_step) * back_re
            + math.sin(ANGULAR_STEP * source_step) * back_im
        )
        drives.append(adj_drive)
    drive = jnp.stack(drives).swapaxes(2, 3)
    drive = jnp.pad(drive, ((0, 0), (0, 0), (0, 0), (0, fields.shape[3] - TILE)))
    column_grad_t = run_leaps(None, inv_eps, e_changes, drive, 11)[:, :TILE]
    spread = contract("sx,yx->sy", pick_x, column_grad_t)
    picked = jnp.sum(spread * pick_y, axis=1).reshape(devices * capacity, 16)
    returned = exchange(picked.reshape(devices, capacity, 16), ("gx", "gy"), False, 5)
    own_vals = contract("ps,sk->pk", placing, returned.reshape(devices * capacity, 16))
    grad_widths = DELTA_EPS * jnp.sum(intersection * own_vals, axis=1)
    return (final_fields, focal_power, grad_widths)


def solution(mesh):
    placed = (
        P(None, "gx", "gy", None),
        P("gx", "gy", None),
        P(),
        P(("gx", "gy")),
        P(("gx", "gy"), None),
        P(("gx", "gy"), None),
        P(("gx", "gy"), None),
    )
    return jax.shard_map(
        shards,
        mesh=mesh,
        in_specs=placed,
        out_specs=(P(None, "gx", "gy", None), P(("gx", "gy"), None), P(("gx", "gy"))),
        check_vma=False,
    )
```

```python
import math

import jax
import jax.numpy as jnp
from jax import lax
from jax.sharding import PartitionSpec as P
from jax.experimental import pallas as pl
from jax.experimental.pallas import tpu as pltpu

TILE = 32
P_DEV = 128
NT = 4
ZP = 4
U = 256
V = 256
ZM = 64


COURANT = 0.5
ANGULAR_STEP = 0.9
DELTA_EPS = 4.0


def passed_along(shard, axis, by):
    count = lax.axis_size(axis)
    pairs = [(i, i + by) for i in range(count) if 0 <= i + by < count]
    return lax.ppermute(shard, axis, pairs)


def plus_diff(field, rim_layer, axis):
    extended = jnp.concatenate([field, rim_layer], axis=axis)
    return lax.slice_in_dim(extended, 1, extended.shape[axis], axis=axis) - field


def minus_diff(field, rim_layer, axis):
    extended = jnp.concatenate([rim_layer, field], axis=axis)
    return field - lax.slice_in_dim(extended, 0, field.shape[axis], axis=axis)


def leap_step(fields_now, inv_eps, sources):
    elec_x, elec_y, elec_z, magn_x, magn_y, magn_z = fields_now
    z_blank = jnp.zeros_like(elec_x[:, :, :1])
    rim_east = passed_along(jnp.stack([elec_y[:1], elec_z[:1]]), "gx", -1)
    rim_north = passed_along(jnp.stack([elec_x[:, :1], elec_z[:, :1]]), "gy", -1)
    curl_x = plus_diff(elec_z, rim_north[1], 1) - plus_diff(elec_y, z_blank, 2)
    curl_y = plus_diff(elec_x, z_blank, 2) - plus_diff(elec_z, rim_east[1], 0)
    curl_z = plus_diff(elec_y, rim_east[0], 0) - plus_diff(elec_x, rim_north[0], 1)
    magn_x = magn_x - COURANT * curl_x
    magn_y = magn_y - COURANT * curl_y
    magn_z = magn_z - COURANT * curl_z
    rim_west = passed_along(jnp.stack([magn_y[-1:], magn_z[-1:]]), "gx", 1)
    rim_south = passed_along(jnp.stack([magn_x[:, -1:], magn_z[:, -1:]]), "gy", 1)
    curl_x = minus_diff(magn_z, rim_south[1], 1) - minus_diff(magn_y, z_blank, 2)
    curl_y = minus_diff(magn_x, z_blank, 2) - minus_diff(magn_z, rim_west[1], 0)
    curl_z = minus_diff(magn_y, rim_west[0], 0) - minus_diff(magn_x, rim_south[0], 1)
    elec_x = elec_x + COURANT * (curl_x - sources[0]) * inv_eps
    elec_y = elec_y + COURANT * (curl_y - sources[1]) * inv_eps
    elec_z = elec_z + COURANT * curl_z * inv_eps
    return (elec_x, elec_y, elec_z, magn_x, magn_y, magn_z)


def run_leaps(fields, inv_eps, history, drive, tag):
    span_x = lax.axis_size("gx")
    span_y = lax.axis_size("gy")
    size_x, size_y, size_z = inv_eps.shape
    half = size_x // 2
    adjoint = history is not None
    mesh_id = pl.DeviceIdType.MESH
    order_h = list(range(half - 1, size_x - 1)) + list(range(0, half - 1)) + [size_x - 1]
    order_e = list(range(half - 1, size_x - 1)) + list(range(1, half - 1)) + [size_x - 1, 0]
    slot_h = {x: i for i, x in enumerate(order_h)}
    slot_e = {x: i for i, x in enumerate(order_e)}

    def kernel(*refs):
        refs = list(refs)
        if adjoint:
            hist, eps_ref, drv, acc = refs[:4]
            a_hist, h_state = refs[4:6]
            rest = refs[6:]
        else:
            f_in, eps_ref, final, chg, mon = refs[:5]
            a_hist = refs[5]
            rest = refs[6:]
        east, north, west, south, xs_e, ys_e, xs_h, ys_h, ssem, rsem = rest
        px = lax.axis_index("gx")
        py = lax.axis_index("gy")
        barrier = pltpu.get_barrier_semaphore()
        for peer in (
            (lax.rem(px + 1, span_x), py),
            (lax.rem(px + span_x - 1, span_x), py),
            (px, lax.rem(py + 1, span_y)),
            (px, lax.rem(py + span_y - 1, span_y)),
        ):
            pl.semaphore_signal(barrier, 1, device_id=peer, device_id_type=mesh_id)
        pl.semaphore_wait(barrier, 4)
        has_east = px < span_x - 1
        has_west = px > 0
        has_north = py < span_y - 1
        has_south = py > 0
        west_dev = (lax.rem(px + span_x - 1, span_x), py)
        east_dev = (lax.rem(px + 1, span_x), py)
        south_dev = (px, lax.rem(py + span_y - 1, span_y))
        north_dev = (px, lax.rem(py + 1, span_y))
        zero_slab = jnp.zeros((size_y, size_z), jnp.float32)
        iy = lax.broadcasted_iota(jnp.int32, (size_y, size_z), 0)
        iz = lax.broadcasted_iota(jnp.int32, (size_y, size_z), 1)

        for flag, buf in ((has_east, east), (has_north, north), (has_west, west), (has_south, south)):
            @pl.when(jnp.logical_not(flag))
            def _(buf=buf):
                buf[...] = jnp.zeros(buf.shape, jnp.float32)

        def up_y(slab, row):
            return jnp.where(iy == size_y - 1, row, pltpu.roll(slab, size_y - 1, 0))

        def down_y(slab, row):
            return jnp.where(iy == 0, row, pltpu.roll(slab, 1, 0))

        def up_z(slab):
            return jnp.where(iz == size_z - 1, 0.0, pltpu.roll(slab, size_z - 1, 1))

        def down_z(slab):
            return jnp.where(iz == 0, 0.0, pltpu.roll(slab, 1, 1))

        def load_e(step, comp, x):
            if step == 0:
                return zero_slab if adjoint else f_in[comp, x]
            return a_hist[(step - 1) % 2, comp, x]

        def store_e(step, comp, x, value):
            if step == NT - 1 and not adjoint:
                final[comp, x] = value
            else:
                a_hist[step % 2, comp, x] = value

        def load_h(step, comp, x):
            if adjoint and step <= 1:
                return zero_slab
            if step == 0:
                return f_in[3 + comp, x]
            return h_state[comp, x] if adjoint else final[3 + comp, x]

        def store_h(comp, x, value):
            if adjoint:
                h_state[comp, x] = value
            else:
                final[3 + comp, x] = value

        sent = []

        def link(src, dst, sem, device, sends):
            copy = pltpu.make_async_remote_copy(
                src_ref=src, dst_ref=dst, send_sem=ssem.at[sem], recv_sem=rsem.at[sem],
                device_id=device, device_id_type=mesh_id,
            )
            pl.when(sends)(copy.start)
            sent.append((copy, sends))
            return copy

        def wait_for(src, dst, sem, device, gets):
            copy = pltpu.make_async_remote_copy(
                src_ref=src, dst_ref=dst, send_sem=ssem.at[sem], recv_sem=rsem.at[sem],
                device_id=device, device_id_type=mesh_id,
            )
            pl.when(gets)(copy.wait_recv)

        def send_e_rows(step, chunk):
            link(ys_e.at[step, chunk], north.at[step, chunk], 6 * step + chunk, south_dev, has_south)

        def send_e_slab(step):
            link(xs_e.at[step], east.at[step], 6 * step + 2, west_dev, has_west)

        def get_e_rows(step, chunk):
            wait_for(ys_e.at[step, chunk], north.at[step, chunk], 6 * step + chunk, north_dev, has_north)

        def get_e_slab(step):
            wait_for(xs_e.at[step], east.at[step], 6 * step + 2, east_dev, has_east)

        def send_h_rows(step, chunk):
            link(ys_h.at[step, chunk], south.at[step, chunk], 6 * step + 3 + chunk, north_dev, has_north)

        def send_h_slab(step):
            link(xs_h.at[step], west.at[step], 6 * step + 5, east_dev, has_east)

        def get_h_rows(step, chunk):
            wait_for(ys_h.at[step, chunk], south.at[step, chunk], 6 * step + 3 + chunk, south_dev, has_south)

        def get_h_slab(step):
            wait_for(xs_h.at[step], west.at[step], 6 * step + 5, west_dev, has_west)

        def e_row_ref(buf, step, comp, x):
            slot = slot_e[x]
            return buf[step, slot // half, comp, pl.ds(slot % half, 1), :]

        def h_row_ref(buf, step, comp, x):
            slot = slot_h[x]
            return buf[step, slot // half, comp, pl.ds(slot % half, 1), :]

        def stage_e_rows(step, x, ex, ez):
            slot = slot_e[x]
            ys_e[step, slot // half, 0, pl.ds(slot % half, 1), :] = ex[0:1, :]
            ys_e[step, slot // half, 1, pl.ds(slot % half, 1), :] = ez[0:1, :]

        if not adjoint:
            xs_e[0, 0] = f_in[1, 0]
            xs_e[0, 1] = f_in[2, 0]
            for x in order_e:
                stage_e_rows(0, x, f_in[0, x], f_in[2, x])
            send_e_rows(0, 0)
            send_e_rows(0, 1)
            send_e_slab(0)

        def magnetic(step, x):
            ex = load_e(step, 0, x)
            ey = load_e(step, 1, x)
            ez = load_e(step, 2, x)
            if x + 1 < size_x:
                ey_next = load_e(step, 1, x + 1)
                ez_next = load_e(step, 2, x + 1)
            else:
                ey_next = east[step, 0]
                ez_next = east[step, 1]
            nx_row = e_row_ref(north, step, 0, x)
            nz_row = e_row_ref(north, step, 1, x)
            curl_x = (up_y(ez, nz_row) - ez) - (up_z(ey) - ey)
            curl_y = (up_z(ex) - ex) - (ez_next - ez)
            curl_z = (ey_next - ey) - (up_y(ex, nx_row) - ex)
            hx = load_h(step, 0, x) - COURANT * curl_x
            hy = load_h(step, 1, x) - COURANT * curl_y
            hz = load_h(step, 2, x) - COURANT * curl_z
            store_h(0, x, hx)
            store_h(1, x, hy)
            store_h(2, x, hz)
            slot = slot_h[x]
            ys_h[step, slot // half, 0, pl.ds(slot % half, 1), :] = hx[size_y - 1 : size_y, :]
            ys_h[step, slot // half, 1, pl.ds(slot % half, 1), :] = hz[size_y - 1 : size_y, :]
            if x == size_x - 1:
                xs_h[step, 0] = hy
                xs_h[step, 1] = hz

        def electric(step, x, skip_magnetic):
            if skip_magnetic:
                curl_x = curl_y = curl_z = zero_slab
            else:
                hx = load_h(step + 1, 0, x)
                hy = load_h(step + 1, 1, x)
                hz = load_h(step + 1, 2, x)
                if x > 0:
                    hy_prev = load_h(step + 1, 1, x - 1)
                    hz_prev = load_h(step + 1, 2, x - 1)
                else:
                    hy_prev = west[step, 0]
                    hz_prev = west[step, 1]
                sx_row = h_row_ref(south, step, 0, x)
                sz_row = h_row_ref(south, step, 1, x)
                curl_x = (hz - down_y(hz, sz_row)) - (hy - down_z(hy))
                curl_y = (hx - down_z(hx)) - (hz - hz_prev)
                curl_z = (hy - hy_prev) - (hx - down_y(hx, sx_row))
            if adjoint:
                to_layer = (ZM - x) % size_z
                curl_x = curl_x - jnp.where(iz == ZM, pltpu.roll(drv[step, 0], to_layer, 1), 0.0)
                curl_y = curl_y - jnp.where(iz == ZM, pltpu.roll(drv[step, 1], to_layer, 1), 0.0)
            scale = eps_ref[x]
            e_old = [load_e(step, comp, x) for comp in range(3)]
            ex = e_old[0] + COURANT * curl_x * scale
            ey = e_old[1] + COURANT * curl_y * scale
            ez = e_old[2] + COURANT * curl_z * scale
            store_e(step, 0, x, ex)
            store_e(step, 1, x, ey)
            store_e(step, 2, x, ez)
            if adjoint:
                moment = NT - step
                product = (
                    ex * hist[moment - 1, 0, x]
                    + ey * hist[moment - 1, 1, x]
                    + ez * hist[moment - 1, 2, x]
                )
                before = zero_slab if step == 0 else acc[x]
                acc[x] = before - product * scale
            else:
                for comp, value in enumerate((ex, ey, ez)):
                    chg[step, comp, x] = value - e_old[comp]
                from_layer = (x - ZM) % size_z
                for comp, value in enumerate((ex, ey)):
                    packed[comp] = jnp.where(iz == x, pltpu.roll(value, from_layer, 1), packed[comp])
            if step + 1 < NT:
                stage_e_rows(step + 1, x, ex, ez)
                if x == 0:
                    xs_e[step + 1, 0] = ey
                    xs_e[step + 1, 1] = ez

        packed = [zero_slab, zero_slab]
        for step in range(NT):
            skip_magnetic = adjoint and step == 0
            if not skip_magnetic:
                get_e_rows(step, 0)
                for x in order_h[:half]:
                    magnetic(step, x)
                send_h_rows(step, 0)
                get_e_rows(step, 1)
                for x in order_h[half:-1]:
                    magnetic(step, x)
                get_e_slab(step)
                magnetic(step, order_h[-1])
                send_h_rows(step, 1)
                send_h_slab(step)
                get_h_rows(step, 0)
            for x in order_e[:half]:
                electric(step, x, skip_magnetic)
            if step + 1 < NT:
                send_e_rows(step + 1, 0)
            if not skip_magnetic:
                get_h_rows(step, 1)
            for x in order_e[half:-1]:
                electric(step, x, skip_magnetic)
            if not skip_magnetic:
                get_h_slab(step)
            electric(step, order_e[-1], skip_magnetic)
            if step + 1 < NT:
                send_e_rows(step + 1, 1)
                send_e_slab(step + 1)
            if not adjoint:
                mon[step, 0] = packed[0]
                mon[step, 1] = packed[1]

        for copy, sends in sent:
            pl.when(sends)(copy.wait_send)

    rim_x = pltpu.VMEM((NT, 2, size_y, size_z), jnp.float32)
    rim_y = pltpu.VMEM((NT, 2, 2, half, size_z), jnp.float32)
    field_shape = (size_x, size_y, size_z)
    if adjoint:
        operands = [history, inv_eps, drive]
        out_shape = jax.ShapeDtypeStruct(field_shape, jnp.float32)
        out_specs = pl.BlockSpec(memory_space=pltpu.VMEM)
        state = [
            pltpu.VMEM((2, 3) + field_shape, jnp.float32),
            pltpu.VMEM((3,) + field_shape, jnp.float32),
        ]
    else:
        operands = [fields, inv_eps]
        out_shape = (
            jax.ShapeDtypeStruct((6,) + field_shape, jnp.float32),
            jax.ShapeDtypeStruct((NT, 3) + field_shape, jnp.float32),
            jax.ShapeDtypeStruct((NT, 2, size_y, size_z), jnp.float32),
        )
        out_specs = (pl.BlockSpec(memory_space=pltpu.VMEM),) * 3
        state = [pltpu.VMEM((2, 3) + field_shape, jnp.float32)]
    return pl.pallas_call(
        kernel,
        out_shape=out_shape,
        in_specs=[pl.BlockSpec(memory_space=pltpu.VMEM)] * len(operands),
        out_specs=out_specs,
        scratch_shapes=state + [
            rim_x, rim_y, rim_x, rim_y, rim_x, rim_y, rim_x, rim_y,
            pltpu.SemaphoreType.DMA((6 * NT,)),
            pltpu.SemaphoreType.DMA((6 * NT,)),
        ],
        compiler_params=pltpu.CompilerParams(
            collective_id=tag, has_side_effects=True, vmem_limit_bytes=56 * 1024 * 1024
        ),
    )(*operands)


def group_of(axes):
    sizes = [lax.axis_size(a) for a in axes]
    count = math.prod(sizes)
    return count, sizes


def group_place(axes, sizes):
    place = 0
    for axis, size in zip(axes, sizes):
        place = place * size + lax.axis_index(axis)
    return place


def group_device(axes, sizes, peer):
    coords = {}
    rest = peer
    for axis, size in reversed(list(zip(axes, sizes))):
        coords[axis] = rest % size
        rest = rest // size
    return tuple(coords[a] if a in coords else lax.axis_index(a) for a in ("gx", "gy"))


def exchange(pieces, axes, gather, tag, summed=False):
    count, sizes = group_of(axes)
    piece_shape = pieces.shape if gather else pieces.shape[1:]

    def kernel(x_ref, o_ref, send_sem, recv_sem):
        me = group_place(axes, sizes)
        barrier = pltpu.get_barrier_semaphore()
        for step in range(1, count):
            peer = lax.rem(me + step, count)
            pl.semaphore_signal(
                barrier, 1, device_id=group_device(axes, sizes, peer),
                device_id_type=pl.DeviceIdType.MESH,
            )
        pl.semaphore_wait(barrier, count - 1)
        copies = []
        for step in range(1, count):
            peer = lax.rem(me + step, count)
            copy = pltpu.make_async_remote_copy(
                src_ref=x_ref if gather else x_ref.at[peer],
                dst_ref=o_ref.at[me],
                send_sem=send_sem.at[step],
                recv_sem=recv_sem.at[step],
                device_id=group_device(axes, sizes, peer),
                device_id_type=pl.DeviceIdType.MESH,
            )
            copy.start()
            copies.append(copy)
        own = x_ref[...] if gather else x_ref[me]
        o_ref[me] = own
        for copy in copies:
            copy.wait_send()
        for step in range(1, count):
            source = lax.rem(me + count - step, count)
            pltpu.make_async_remote_copy(
                src_ref=x_ref if gather else x_ref.at[source],
                dst_ref=o_ref.at[source],
                send_sem=send_sem.at[step],
                recv_sem=recv_sem.at[step],
                device_id=group_device(axes, sizes, source),
                device_id_type=pl.DeviceIdType.MESH,
            ).wait_recv()

    def summing_kernel(x_ref, s_ref, o_ref, send_sem, recv_sem):
        kernel(x_ref, o_ref, send_sem, recv_sem)
        total = o_ref[0]
        for source in range(1, count):
            total = total + o_ref[source]
        s_ref[...] = total

    gathered = jax.ShapeDtypeStruct((count,) + tuple(piece_shape), pieces.dtype)
    if summed:
        return pl.pallas_call(
            summing_kernel,
            out_shape=jax.ShapeDtypeStruct(tuple(piece_shape), pieces.dtype),
            in_specs=[pl.BlockSpec(memory_space=pltpu.VMEM)],
            out_specs=pl.BlockSpec(memory_space=pltpu.VMEM),
            scratch_shapes=[
                pltpu.VMEM(gathered.shape, pieces.dtype),
                pltpu.SemaphoreType.DMA((count,)),
                pltpu.SemaphoreType.DMA((count,)),
            ],
            compiler_params=pltpu.CompilerParams(collective_id=tag, has_side_effects=True),
        )(pieces)
    return pl.pallas_call(
        kernel,
        out_shape=gathered,
        in_specs=[pl.BlockSpec(memory_space=pltpu.VMEM)],
        out_specs=pl.BlockSpec(memory_space=pltpu.VMEM),
        scratch_shapes=[pltpu.SemaphoreType.DMA((count,)), pltpu.SemaphoreType.DMA((count,))],
        compiler_params=pltpu.CompilerParams(collective_id=tag, has_side_effects=True),
    )(pieces)


def focal_rows(pieces, weights, norm_scale, tag):
    count, sizes = group_of(("gy",))
    rows, width = pieces.shape[1:]

    def kernel(x_ref, t_ref, far_ref, o_ref, got, held, send_sem, recv_sem):
        me = lax.axis_index("gy")
        barrier = pltpu.get_barrier_semaphore()
        for step in range(1, count):
            pl.semaphore_signal(
                barrier, 1, device_id=(lax.axis_index("gx"), lax.rem(me + step, count)),
                device_id_type=pl.DeviceIdType.MESH,
            )
        pl.semaphore_wait(barrier, count - 1)

        def spread(phase, source_of):
            copies = []
            for step in range(1, count):
                peer = lax.rem(me + step, count)
                copy = pltpu.make_async_remote_copy(
                    src_ref=source_of(peer),
                    dst_ref=(got if phase == 0 else o_ref).at[me],
                    send_sem=send_sem.at[phase * count + step],
                    recv_sem=recv_sem.at[phase * count + step],
                    device_id=(lax.axis_index("gx"), peer),
                    device_id_type=pl.DeviceIdType.MESH,
                )
                copy.start()
                copies.append(copy)
            for copy in copies:
                copy.wait_send()
            for step in range(1, count):
                source = lax.rem(me + count - step, count)
                pltpu.make_async_remote_copy(
                    src_ref=source_of(source),
                    dst_ref=(got if phase == 0 else o_ref).at[source],
                    send_sem=send_sem.at[phase * count + step],
                    recv_sem=recv_sem.at[phase * count + step],
                    device_id=(lax.axis_index("gx"), source),
                    device_id_type=pl.DeviceIdType.MESH,
                ).wait_recv()

        got[me] = x_ref[me]
        spread(0, lambda peer: x_ref.at[peer])
        total = got[0]
        for source in range(1, count):
            total = total + got[source]
        far = norm_scale * total
        far_ref[...] = far
        odd = lax.broadcasted_iota(jnp.int32, far.shape, 0) % 2 == 1
        scaled = t_ref[...] * far
        weighted = jnp.where(odd, -scaled, scaled)
        held[...] = weighted
        o_ref[me] = weighted
        spread(1, lambda peer: held)

    return pl.pallas_call(
        kernel,
        out_shape=(
            jax.ShapeDtypeStruct((rows, width), jnp.float32),
            jax.ShapeDtypeStruct((count, rows, width), jnp.float32),
        ),
        in_specs=[pl.BlockSpec(memory_space=pltpu.VMEM)] * 2,
        out_specs=(pl.BlockSpec(memory_space=pltpu.VMEM),) * 2,
        scratch_shapes=[
            pltpu.VMEM((count, rows, width), jnp.float32),
            pltpu.VMEM((rows, width), jnp.float32),
            pltpu.SemaphoreType.DMA((2 * count,)),
            pltpu.SemaphoreType.DMA((2 * count,)),
        ],
        compiler_params=pltpu.CompilerParams(collective_id=tag, has_side_effects=True),
    )(pieces, weights)


def kernel_table(count_out, count_in, offset, length):
    focal_pos = (jnp.arange(count_out, dtype=jnp.float32) + 0.5) / count_out - 0.5
    cell_pos = (
        offset.astype(jnp.float32) + jnp.arange(length, dtype=jnp.float32) + 0.5
    ) / count_in - 0.5
    phase = math.pi * count_out * (focal_pos[:, None] - cell_pos[None, :]) ** 2
    return (jnp.cos(phase), jnp.sin(phase))


def contract(pattern, first_op, second_op):
    return jnp.einsum(pattern, first_op, second_op, precision=lax.Precision.HIGHEST)


def route_pillars(rows, slot_ids, devices, capacity):
    slots = devices * capacity
    placing = (slot_ids[:, None] == jnp.arange(slots, dtype=jnp.int32)[None, :]).astype(
        jnp.float32
    )
    packed = contract("ps,pk->sk", placing, rows)
    got = exchange(packed.reshape(devices, capacity, rows.shape[1]), ("gx", "gy"), False, 0)
    return placing, got.reshape(slots, rows.shape[1])


def shards(fields, eps_background, target, widths, intersection, pillar_tile, anchors):
    span_x = lax.axis_size("gx")
    span_y = lax.axis_size("gy")
    devices = span_x * span_y
    place_x = lax.axis_index("gx")
    place_y = lax.axis_index("gy")
    linear = place_x * span_y + place_y
    offsets = jnp.arange(16, dtype=jnp.int32)
    capacity = 2 * max(1, P_DEV // devices)
    target_tile = pillar_tile[:, 0]
    pillar_index = jnp.arange(target_tile.shape[0], dtype=jnp.int32)
    same_before = (target_tile[None, :] == target_tile[:, None]) & (
        pillar_index[None, :] < pillar_index[:, None]
    )
    order_in = jnp.sum(same_before.astype(jnp.int32), axis=1)
    slot_ids = target_tile * capacity + order_in
    rows = jnp.concatenate(
        [intersection * widths[:, None], anchors.astype(jnp.float32)], axis=1
    )
    placing, got = route_pillars(rows, slot_ids, devices, capacity)
    local_vals = got[:, :16]
    local_at = got[:, 16:18].astype(jnp.int32)
    cells_x = (local_at[:, 0:1] + (offsets // 4)[None, :]).reshape(-1)
    cells_y = (local_at[:, 1:2] + (offsets % 4)[None, :]).reshape(-1)
    lanes = jnp.arange(TILE, dtype=jnp.int32)
    pick_x = (cells_x[:, None] == lanes[None, :]).astype(jnp.float32)
    pick_y = (cells_y[:, None] == lanes[None, :]).astype(jnp.float32)
    filling = contract("sx,sy->xy", pick_x, pick_y * local_vals.reshape(-1)[:, None])
    z_index = jnp.arange(fields.shape[3], dtype=jnp.int32)
    layers = ((z_index >= ZM - ZP) & (z_index < ZM)).astype(jnp.float32)
    permittivity = eps_background + DELTA_EPS * filling[:, :, None] * layers[None, None, :]
    inv_eps = 1.0 / permittivity
    final_fields, e_changes, packed_mon = run_leaps(fields, inv_eps, None, None, 10)
    packed_mon = packed_mon[:, :, :, :TILE].swapaxes(2, 3)
    mon_re = jnp.zeros((2, TILE, TILE), jnp.float32)
    mon_im = jnp.zeros((2, TILE, TILE), jnp.float32)
    for moment in range(1, NT + 1):
        monitor = packed_mon[moment - 1]
        mon_re = mon_re + math.cos(ANGULAR_STEP * moment) * monitor
        mon_im = mon_im - math.sin(ANGULAR_STEP * moment) * monitor
    norm_scale = (TILE * span_x * TILE * span_y) ** (-0.5)
    x_re, x_im = kernel_table(U, TILE * span_x, place_x * TILE, TILE)
    y_re, y_im = kernel_table(V, TILE * span_y, place_y * TILE, TILE)
    part = jnp.stack(
        [
            contract("ux,cxy->ucy", x_re, mon_re) - contract("ux,cxy->ucy", x_im, mon_im),
            contract("ux,cxy->ucy", x_re, mon_im) + contract("ux,cxy->ucy", x_im, mon_re),
        ]
    )
    chunk_u = U // span_x
    part = part.reshape(2, span_x, chunk_u, 2, TILE).transpose(1, 2, 0, 3, 4)
    part = exchange(part.reshape(span_x, chunk_u, 4 * TILE), ("gx",), False, 1, summed=True)
    part = part.reshape(chunk_u, 2, 2, TILE)
    part_re, part_im = part[:, 0], part[:, 1]
    far = jnp.stack(
        [
            contract("ucy,vy->cuv", part_re, y_re) - contract("ucy,vy->cuv", part_im, y_im),
            contract("ucy,vy->cuv", part_re, y_im) + contract("ucy,vy->cuv", part_im, y_re),
        ],
        axis=2,
    )
    row_count = U // devices
    far = far.reshape(2, span_y, row_count, 2, V).transpose(1, 0, 2, 3, 4)
    mine_target = lax.dynamic_slice_in_dim(target, linear * row_count, row_count, 0)
    row_weights = jnp.broadcast_to(mine_target[None, :, None, :], (2, row_count, 2, V))
    far, weighted = focal_rows(
        far.reshape(span_y, 2 * row_count * 2, V),
        row_weights.reshape(2 * row_count * 2, V),
        norm_scale,
        2,
    )
    far = far.reshape(2, row_count, 2, V)
    focal_power = jnp.sum(far * far, axis=(0, 2))
    weighted = weighted.reshape(span_y, 2, row_count, 2, V).transpose(1, 0, 2, 3, 4)
    weighted = weighted.reshape(2, span_y * row_count, 2, V)
    w_re, w_im = weighted[:, :, 0], weighted[:, :, 1]
    half = jnp.stack(
        [
            contract("cuv,vy->cuy", w_re, y_re) - contract("cuv,vy->cuy", w_im, y_im),
            contract("cuv,vy->cuy", w_re, y_im) + contract("cuv,vy->cuy", w_im, y_re),
        ]
    )
    half = half.transpose(2, 0, 1, 3).reshape(chunk_u, 4 * TILE)
    half = exchange(half, ("gx",), True, 4)
    half = half.reshape(span_x * chunk_u, 2, 2, TILE).transpose(1, 2, 0, 3)
    half_re, half_im = half[0], half[1]
    back_re = 2.0 * norm_scale * (
        contract("ux,cuy->cyx", x_re, half_re) - contract("ux,cuy->cyx", x_im, half_im)
    )
    back_im = 2.0 * norm_scale * (
        contract("ux,cuy->cyx", x_re, half_im) + contract("ux,cuy->cyx", x_im, half_re)
    )
    drives = []
    for moment in range(1, NT + 1):
        source_step = NT + 1 - moment
        adj_drive = (
            math.cos(ANGULAR_STEP * source_step) * back_re
            + math.sin(ANGULAR_STEP * source_step) * back_im
        )
        drives.append(adj_drive)
    drive = jnp.stack(drives)
    drive = jnp.pad(drive, ((0, 0), (0, 0), (0, 0), (0, fields.shape[3] - TILE)))
    grad_eps = run_leaps(None, inv_eps, e_changes, drive, 11)
    column_grad = jnp.sum(grad_eps[:, :, ZM - ZP : ZM], axis=2)
    spread = contract("sx,xy->sy", pick_x, column_grad)
    picked = jnp.sum(spread * pick_y, axis=1).reshape(devices * capacity, 16)
    returned = exchange(picked.reshape(devices, capacity, 16), ("gx", "gy"), False, 5)
    own_vals = contract("ps,sk->pk", placing, returned.reshape(devices * capacity, 16))
    grad_widths = DELTA_EPS * jnp.sum(intersection * own_vals, axis=1)
    return (final_fields, focal_power, grad_widths)


def solution(mesh):
    placed = (
        P(None, "gx", "gy", None),
        P("gx", "gy", None),
        P(),
        P(("gx", "gy")),
        P(("gx", "gy"), None),
        P(("gx", "gy"), None),
        P(("gx", "gy"), None),
    )
    return jax.shard_map(
        shards,
        mesh=mesh,
        in_specs=placed,
        out_specs=(P(None, "gx", "gy", None), P(("gx", "gy"), None), P(("gx", "gy"))),
        check_vma=False,
    )
```
